32 devices in a mesh: dp: 16 (over z, x, core), seq: 2 (over y).
Axes of the slice: x: 2, y: 2, z: 4, core: 2. Of those that a mesh axis runs over, the one named last changes fastest.
Arguments:
- captions: bfloat16 [16, 1024, 768], P('dp', 'seq'), may hold values from -6 to 6
- patches: bfloat16 [16, 196, 768], P('dp', 'seq'), may hold values from -32 to 32, as said below
- prefix: bfloat16 [16, 32, 768], P('dp', 'seq'), may hold values from -6 to 6
- prefix_count: int32 [16], P('dp'), may hold values from 0 to 32, as said below
- caption_len: int32 [16], P('dp'), may hold values from 513 to 1024, as said below
- cotangent: bfloat16 [16, 1024, 768], P('dp', 'seq'), may hold values from -6 to 6
- w_patch: bfloat16 [768, 768], P('dp'), may hold values from -0.21875 to 0.21875
- w_conv: bfloat16 [2, 6912, 768], P(None, 'dp'), may hold values from -0.078125 to 0.078125
- w_self_qkv: bfloat16 [768, 2304], P('dp'), may hold values from -0.21875 to 0.21875
- w_self_out: bfloat16 [768, 768], P('dp'), may hold values from -3.5 to 3.5
- w_cross_q: bfloat16 [768, 768], P('dp'), may hold values from -0.21875 to 0.21875
- w_cross_kv: bfloat16 [768, 1536], P('dp'), may hold values from -0.21875 to 0.21875
- w_cross_out: bfloat16 [768, 768], P('dp'), may hold values from -1.75 to 1.75
- w_up: bfloat16 [768, 3072], P('dp'), may hold values from -0.21875 to 0.21875
- w_down: bfloat16 [3072, 768], P('dp'), may hold values from -0.109375 to 0.109375
- norm_params: bfloat16 [12, 768], P(None, 'dp'), may hold values from 0.25 to 1.75
Outputs:
- block_output: bfloat16 [16, 1024, 768], P('dp', 'seq')
- caption_grad: bfloat16 [16, 1024, 768], P('dp', 'seq')
- prefix_grad: bfloat16 [16, 32, 768], P('dp', 'seq')
- grad_w_patch: float32 [768, 768], P('dp')
- grad_w_conv: float32 [2, 6912, 768], P(None, 'dp')
- grad_w_self_qkv: float32 [768, 2304], P('dp')
- grad_w_self_out: float32 [768, 768], P('dp')
- grad_w_cross_q: float32 [768, 768], P('dp')
- grad_w_cross_kv: float32 [768, 1536], P('dp')
- grad_w_cross_out: float32 [768, 768], P('dp')
- grad_w_up: float32 [768, 3072], P('dp')
- grad_w_down: float32 [3072, 768], P('dp')
- grad_norm_params: float32 [12, 768], P(None, 'dp')
The draws below stay inside these ranges and needn't reach their ends.
Inputs may be any that keep to these rules, and one draw needn't show every extreme that they name: `prefix_count`: each example has between 0 and 32 live prefix slots; some example has all 32 and some none. `caption_len`: every caption reaches past the first 512 slots; some caption fills all 1024 slots. `patches`: pixel values; each example has its own overall scale.
All inputs are finite; a program needn't handle non-finite values.
Results may differ from the reference program's by a relative error of at most 0.035.
Values may be sent and summed in bfloat16 or wider, within the bound.
A program may use at most 384 MiB of HBM per device.

```python
import jax
import jax.numpy as jnp
from jax import lax

D = 768
FF = 3072
HEADS = 12
PIX = 768
SIDE = 14
GRID = 196
PRE = 32
CAP_DEV = 512
CAP = 1024
EXAMPLES = 16


def draw_patches(key, part):
    noise_key = jax.random.fold_in(key, 11)
    shift_key = jax.random.fold_in(key, 12)
    fraction = jnp.arange(EXAMPLES, dtype=jnp.float32) / max(EXAMPLES - 1, 1)
    example_scale = 1.0 + 2.0 * fraction
    noise = jax.random.normal(noise_key, (EXAMPLES, GRID, PIX))
    channel_shift = jax.random.normal(shift_key, (PIX,)) * 0.5
    values = example_scale[:, None, None] * (noise + channel_shift[None, None, :])
    return jnp.clip(values, -32.0, 32.0).astype(jnp.float32).astype(jnp.bfloat16)


def draw_prefix_count(key, part):
    counts = jax.random.randint(jax.random.fold_in(key, 21), (EXAMPLES,), 0, PRE + 1)
    return counts.at[0].set(PRE).at[1].set(0).astype(jnp.int32)


def draw_caption_len(key, part):
    lengths = jax.random.randint(jax.random.fold_in(key, 31), (EXAMPLES,), CAP - CAP_DEV + 1, CAP + 1)
    return lengths.at[0].set(CAP).astype(jnp.int32)


def level_of(own_key, extent, split, least, high):
    factor_of = 1.0
    for position, parts in split:
        draws = jax.random.uniform(jax.random.fold_in(jax.random.fold_in(own_key, 6), position), (parts,), jnp.float32, least / len(split), high / len(split))
        factor_of = factor_of * jnp.repeat(jnp.exp(draws), extent[position] // parts).reshape((-1,) + (1,) * (len(extent) - 1 - position))
    return factor_of


def scatter_about(rng, dims, width, reach, pieces=(), kind=jnp.bfloat16):
    factor_of = level_of(rng, dims, pieces, -0.22, 0.18) if pieces else 1.0
    values = jax.random.normal(rng, dims, jnp.float32) * width * factor_of
    return jnp.minimum(jnp.maximum(values, -reach), reach).astype(kind)


def setup_inputs(seed: int = 0) -> dict:
    arg_keys = jax.random.split(jax.random.key(seed), 17)
    return {
        "captions": scatter_about(arg_keys[0], (EXAMPLES, CAP, D), 1.0, 6.0, ((0, 16), (1, 2))),
        "patches": draw_patches(jax.random.fold_in(arg_keys[16], 71), 0),
        "prefix": scatter_about(arg_keys[2], (EXAMPLES, PRE, D), 1.0, 6.0, ((0, 16), (1, 2))),
        "prefix_count": draw_prefix_count(jax.random.fold_in(arg_keys[16], 71), 0),
        "caption_len": draw_caption_len(jax.random.fold_in(arg_keys[16], 71), 0),
        "cotangent": scatter_about(arg_keys[5], (EXAMPLES, CAP, D), 1.0, 6.0, ((0, 16), (1, 2))),
        "w_patch": scatter_about(arg_keys[6], (PIX, D), PIX ** -0.5, 0.21875, ((0, 16),)),
        "w_conv": scatter_about(arg_keys[7], (2, 9 * D, D), (9 * D) ** -0.5, 0.078125, ((1, 16),)),
        "w_self_qkv": scatter_about(arg_keys[8], (D, 3 * D), D ** -0.5, 0.21875, ((0, 16),)),
        "w_self_out": scatter_about(arg_keys[9], (D, D), (max(4 * D // CAP, 1)) ** -0.5, 3.5, ((0, 16),)),
        "w_cross_q": scatter_about(arg_keys[10], (D, D), D ** -0.5, 0.21875, ((0, 16),)),
        "w_cross_kv": scatter_about(arg_keys[11], (D, 2 * D), D ** -0.5, 0.21875, ((0, 16),)),
        "w_cross_out": scatter_about(arg_keys[12], (D, D), (max(4 * D // (PRE + GRID), 1)) ** -0.5, 1.75, ((0, 16),)),
        "w_up": scatter_about(arg_keys[13], (D, FF), D ** -0.5, 0.21875, ((0, 16),)),
        "w_down": scatter_about(arg_keys[14], (FF, D), FF ** -0.5, 0.109375, ((0, 16),)),
        "norm_params": jnp.clip(1.0 + 0.15 * jax.random.normal(arg_keys[15], (12, D), jnp.float32), 0.25, 1.75).astype(jnp.bfloat16),
    }


highest = lax.Precision.HIGHEST

@jax.custom_vjp
def low(v):
    return lax.optimization_barrier(v.astype(jnp.bfloat16)).astype(jnp.float32)

@jax.custom_vjp
def low_back(v):
    return v

def low_keep(v):
    return (low(v), None)

def low_pass(kept, grad):
    return (grad,)

def back_keep(v):
    return (v, None)

def back_low(kept, grad):
    return (low(grad),)
low.defvjp(low_keep, low_pass)
low_back.defvjp(back_keep, back_low)

def rounded(value_in):
    return low_back(low(value_in))

def product(left, right):
    return jnp.dot(left, right, precision=highest, preferred_element_type=jnp.float32)

def layer_norm(activ, gain_vec, bias_vec):
    row_mean = lax.optimization_barrier(jnp.mean(activ, -1, keepdims=True))
    centred = activ - row_mean
    spread = lax.optimization_barrier(jnp.mean(centred * centred, -1, keepdims=True))
    return centred * lax.rsqrt(spread + 1e-06) * gain_vec + bias_vec

def batch_norm(values, gain_vec, bias_vec):
    col_mean = lax.optimization_barrier(jnp.mean(values, 0))
    centred = values - col_mean
    col_var = lax.optimization_barrier(jnp.mean(centred * centred, 0))
    return centred * lax.rsqrt(col_var + 1e-05) * gain_vec + bias_vec

def conv_grid(grid_in, weight):
    padded = jnp.pad(grid_in, ((0, 0), (1, 1), (1, 1), (0, 0)))
    total = jnp.zeros((EXAMPLES * GRID, D), jnp.float32)
    for row_tap in range(3):
        for col_tap in range(3):
            tap = 3 * row_tap + col_tap
            window = padded[:, row_tap:row_tap + SIDE, col_tap:col_tap + SIDE].reshape(-1, D)
            total = total + product(window, weight[tap * D:(tap + 1) * D])
    return total

def attention(queries, key_rows, value_rows, allow_fn):
    row_count = queries.shape[0]
    head_size = D // HEADS
    block_rows = min(512, row_count)
    block_count = row_count // block_rows
    score_scale = head_size ** (-0.5)
    query_blocks = queries.reshape(block_count, block_rows, HEADS, head_size)
    head_keys = key_rows.reshape(-1, HEADS, head_size)
    head_values = value_rows.reshape(-1, HEADS, head_size)

    def one_block(block_pair):
        query_part, first_row = block_pair
        scores = jnp.einsum('qhd,khd->hqk', query_part, head_keys, precision=highest)
        scores = low_back(scores * score_scale)
        scores = jnp.where(allow_fn(first_row, block_rows)[None], scores, -1000000000.0)
        row_max = lax.optimization_barrier(jnp.max(scores, -1, keepdims=True))
        exponent = jnp.exp(scores - row_max)
        softmax = low(exponent / lax.optimization_barrier(jnp.sum(exponent, -1, keepdims=True)))
        return jnp.einsum('hqk,khd->qhd', softmax, head_values, precision=highest)
    starts = jnp.arange(block_count, dtype=jnp.int32) * block_rows
    outputs = lax.map(jax.checkpoint(one_block), (query_blocks, starts))
    return outputs.reshape(row_count, D)

def reference(captions, patches, prefix, prefix_count, caption_len, cotangent, w_patch, w_conv, w_self_qkv, w_self_out, w_cross_q, w_cross_kv, w_cross_out, w_up, w_down, norm_params):
    pixels = patches.astype(jnp.float32).reshape(-1, PIX)

    def forward(cap_in, prefix_in, wp, wconv, wqkv, wso, wcq, wckv, wco, wup, wdn, norms):
        stem_out = low_back(product(pixels, wp))
        first_out = jax.nn.gelu(batch_norm(stem_out, norms[0], norms[1]))
        conv_two = low_back(conv_grid(low(first_out).reshape(EXAMPLES, SIDE, SIDE, D), wconv[0]))
        second_out = first_out + jax.nn.gelu(batch_norm(conv_two, norms[2], norms[3]))
        conv_three = low_back(conv_grid(low(second_out).reshape(EXAMPLES, SIDE, SIDE, D), wconv[1]))
        third_out = second_out + jax.nn.gelu(batch_norm(conv_three, norms[4], norms[5]))
        patch_emb = low(third_out).reshape(EXAMPLES, GRID, D)
        memory = jnp.concatenate([prefix_in, patch_emb], 1)
        mem_kv = rounded(product(memory.reshape(-1, D), wckv)).reshape(EXAMPLES, PRE + GRID, 2 * D)

        def one_example(example):
            cap_rows, kv_rows, count_one, length_one = example
            key_pos = jnp.arange(CAP, dtype=jnp.int32)

            def self_allow(first_row, block_rows):
                query_pos = first_row + jnp.arange(block_rows, dtype=jnp.int32)
                return (key_pos[None] <= query_pos[:, None]) & (key_pos[None] < length_one)
            slot_ids = jnp.arange(PRE + GRID, dtype=jnp.int32)
            mem_allowed = (slot_ids >= PRE) | (slot_ids < count_one)

            def cross_allow(first_row, block_rows):
                return jnp.broadcast_to(mem_allowed[None], (block_rows, PRE + GRID))
            low_one = low(layer_norm(cap_rows, norms[6], norms[7]))
            qkv = rounded(product(low_one, wqkv))
            self_att = rounded(attention(qkv[:, :D], qkv[:, D:2 * D], qkv[:, 2 * D:], self_allow))
            after_self = cap_rows + low_back(product(self_att, wso))
            low_two = low(layer_norm(after_self, norms[8], norms[9]))
            cross_q = rounded(product(low_two, wcq))
            cross_att = rounded(attention(cross_q, kv_rows[:, :D], kv_rows[:, D:], cross_allow))
            after_cross = after_self + low_back(product(cross_att, wco))
            low_three = low(layer_norm(after_cross, norms[10], norms[11]))
            up_proj = low_back(product(low_three, wup))
            hidden = low(jax.nn.gelu(up_proj))
            return after_cross + low_back(product(hidden, wdn))
        return lax.map(jax.checkpoint(one_example), (cap_in, mem_kv, prefix_count, caption_len))
    primals = tuple((item.astype(jnp.float32) for item in (captions, prefix, w_patch, w_conv, w_self_qkv, w_self_out, w_cross_q, w_cross_kv, w_cross_out, w_up, w_down, norm_params)))
    result, pullback = jax.vjp(forward, *primals)
    grads = pullback(cotangent.astype(jnp.float32))
    return (result.astype(jnp.bfloat16), grads[0].astype(jnp.bfloat16), grads[1].astype(jnp.bfloat16), grads[2], grads[3], grads[4], grads[5], grads[6], grads[7], grads[8], grads[9], grads[10], grads[11])
```

```python
import functools

import jax
import jax.numpy as jnp
import numpy as np
from jax import lax
from jax.experimental import pallas as pl
from jax.experimental.pallas import tpu as pltpu
from jax.sharding import PartitionSpec as P

HEADS = 12
SIDE = 14
MESH = pl.DeviceIdType.MESH
LOW = jnp.bfloat16

STEPS = ((4, 3, 2, 0), (4, 0, 3, 2), (4, 2, 0, 3))
PORTIONS = 3
GROUP = 8


def my_bits():
    a = lax.axis_index("dp")
    return [
        lax.axis_index("seq"),
        lax.rem(a, 2),
        lax.rem(a // 2, 2),
        lax.rem(a // 4, 2),
        lax.rem(a // 8, 2),
    ]


def flipped(bits, which):
    return [1 - b if i == which else b for i, b in enumerate(bits)]


def place(bits):
    return (bits[1] + 2 * bits[2] + 4 * bits[3] + 8 * bits[4], bits[0])


def slot_of(bits, p):
    order = STEPS[p]
    return (
        bits[order[0]] + 2 * bits[order[1]] + 4 * bits[order[2]] + 8 * bits[order[3]] + 16 * bits[1]
    )


def device_of_slot(p):
    owners = np.zeros(32, np.int64)
    for e in range(32):
        bits = [(e >> i) & 1 for i in range(5)]
        owners[int(slot_of(bits, p))] = e
    return owners


def slots_to_devices(array):
    parts = []
    for p in range(PORTIONS):
        rest = array.shape[2:]
        names = [1, STEPS[p][3], STEPS[p][2], STEPS[p][1], STEPS[p][0]]
        cube = array[p].reshape((2,) * 5 + rest)
        perm = [names.index(bit) for bit in (4, 3, 2, 1, 0)]
        cube = cube.transpose(perm + [5 + i for i in range(len(rest))])
        parts.append(cube.reshape((32,) + rest))
    return jnp.stack(parts, 1)


def devices_to_slots(array):
    parts = []
    for p in range(PORTIONS):
        rest = array.shape[2:]
        names = [4, 3, 2, 1, 0]
        cube = array[:, p].reshape((2,) * 5 + rest)
        want = [1, STEPS[p][3], STEPS[p][2], STEPS[p][1], STEPS[p][0]]
        perm = [names.index(bit) for bit in want]
        cube = cube.transpose(perm + [5 + i for i in range(len(rest))])
        parts.append(cube.reshape((32,) + rest))
    return jnp.stack(parts, 0)


def greet(places):
    barrier = pltpu.get_barrier_semaphore()
    for where in places:
        pl.semaphore_signal(barrier, inc=1, device_id=where, device_id_type=MESH)
    pl.semaphore_wait(barrier, len(places))


def arrived(ref, sem):
    pltpu.make_async_remote_copy(
        src_ref=ref,
        dst_ref=ref,
        send_sem=sem,
        recv_sem=sem,
        device_id=(lax.axis_index("dp"), 1 - lax.axis_index("seq")),
        device_id_type=MESH,
    ).wait_recv()


def gather_body(x_ref, o_ref, send_sem, recv_sem, own_sem):
    bits = my_bits()
    greet([place(flipped(bits, b)) for b in range(5)])
    started = []

    def send(p, src, start, size, to_bit, k):
        copy = pltpu.make_async_remote_copy(
            src_ref=src,
            dst_ref=o_ref.at[p, pl.ds(start, size)],
            send_sem=send_sem.at[p, k],
            recv_sem=recv_sem.at[p, k],
            device_id=place(flipped(bits, to_bit)),
            device_id_type=MESH,
        )
        copy.start()
        started.append(copy)

    def await_run(p, start, size, k):
        run = o_ref.at[p, pl.ds(start, size)]
        arrived(run, recv_sem.at[p, k])

    slots = [slot_of(bits, p) for p in range(PORTIONS)]
    owns = []
    for p in range(PORTIONS):
        own = pltpu.make_async_copy(
            x_ref.at[pl.ds(p, 1)], o_ref.at[p, pl.ds(slots[p], 1)], own_sem.at[p]
        )
        own.start()
        owns.append(own)
    for p in range(PORTIONS):
        send(p, x_ref.at[pl.ds(p, 1)], slots[p], 1, STEPS[p][0], 0)
    for p in range(PORTIONS):
        send(p, x_ref.at[pl.ds(p, 1)], slots[p], 1, 1, 4)
    for own in owns:
        own.wait()
    fresh = [None] * PORTIONS
    for k in range(4):
        size = 2**k
        for p in range(PORTIONS):
            mine = (slots[p] // size) * size
            bit = bits[STEPS[p][k]]
            theirs = mine + size * (1 - 2 * bit)
            await_run(p, theirs, size, k)
            fresh[p] = theirs
            if k < 3:
                both = (slots[p] // (2 * size)) * (2 * size)
                send(p, o_ref.at[p, pl.ds(both, 2 * size)], both, 2 * size, STEPS[p][k + 1], k + 1)
        for p in range(PORTIONS):
            send(p, o_ref.at[p, pl.ds(fresh[p], size)], fresh[p], size, 1, 5 + k)
    for p in range(PORTIONS):
        other = 16 * (1 - 2 * bits[1])
        await_run(p, slots[p] + other, 1, 4)
        for k in range(4):
            size = 2**k
            mine = (slots[p] // size) * size
            theirs = mine + size * (1 - 2 * bits[STEPS[p][k]])
            await_run(p, theirs + other, size, 5 + k)
    for copy in started:
        copy.wait_send()


def gather_all(x, cid):
    return pl.pallas_call(
        gather_body,
        name="gather_all",
        out_shape=jax.ShapeDtypeStruct((PORTIONS, 32) + x.shape[1:], x.dtype),
        in_specs=[pl.BlockSpec(memory_space=pltpu.HBM)],
        out_specs=pl.BlockSpec(memory_space=pltpu.HBM),
        scratch_shapes=[
            pltpu.SemaphoreType.DMA((PORTIONS, 9)),
            pltpu.SemaphoreType.DMA((PORTIONS, 9)),
            pltpu.SemaphoreType.DMA((PORTIONS,)),
        ],
        compiler_params=pltpu.CompilerParams(collective_id=cid, has_side_effects=True),
    )(x)


def reduce_body(x_ref, o_ref, r0, r1, r2, r3, r4, send_sem, recv_sem):
    bits = my_bits()
    greet([place(flipped(bits, b)) for b in range(5)])
    started = []
    slots = [slot_of(bits, p) for p in range(PORTIONS)]
    bufs = (r0, r1, r2, r3, r4)

    def send(p, src, dst, bit, k):
        copy = pltpu.make_async_remote_copy(
            src_ref=src,
            dst_ref=dst,
            send_sem=send_sem.at[p, k],
            recv_sem=recv_sem.at[p, k],
            device_id=place(flipped(bits, bit)),
            device_id_type=MESH,
        )
        copy.start()
        started.append(copy)

    for p in range(PORTIONS):
        away = 16 * (1 - bits[1])
        send(p, x_ref.at[p, pl.ds(away, 16)], r0.at[p], 1, 0)
    for k in range(5):
        size = 16 >> k
        for p in range(PORTIONS):
            got = bufs[k].at[p]
            arrived(got, recv_sem.at[p, k])
            if k == 0:
                base, held = 16 * bits[1], x_ref
            else:
                bit = bits[STEPS[p][4 - k]]
                base, held = size * bit, bufs[k - 1]
            if k == 4:
                o_ref[p] = held[p, base].astype(jnp.float32) + bufs[k][p, 0].astype(jnp.float32)
                continue
            for j in range(size):
                total = held[p, base + j].astype(jnp.float32) + bufs[k][p, j].astype(jnp.float32)
                bufs[k][p, j] = total.astype(bufs[k].dtype)
            half = size // 2
            nbit = bits[STEPS[p][3 - k]]
            send(
                p,
                bufs[k].at[p, pl.ds(half * (1 - nbit), half)],
                bufs[k + 1].at[p],
                STEPS[p][3 - k],
                k + 1,
            )
    for copy in started:
        copy.wait_send()


def reduce_all(x, cid):
    rest = x.shape[2:]
    return pl.pallas_call(
        reduce_body,
        name="reduce_all",
        out_shape=jax.ShapeDtypeStruct((PORTIONS,) + rest, jnp.float32),
        in_specs=[pl.BlockSpec(memory_space=pltpu.VMEM)],
        out_specs=pl.BlockSpec(memory_space=pltpu.VMEM),
        scratch_shapes=[pltpu.VMEM((PORTIONS, 16 >> k) + rest, x.dtype) for k in range(5)]
        + [pltpu.SemaphoreType.DMA((PORTIONS, 5)), pltpu.SemaphoreType.DMA((PORTIONS, 5))],
        compiler_params=pltpu.CompilerParams(
            collective_id=cid, has_side_effects=True, vmem_limit_bytes=40 << 20
        ),
    )(x)


def swap_body(x_ref, o_ref, send_sem, recv_sem, own_sem):
    a, s = lax.axis_index("dp"), lax.axis_index("seq")
    count = x_ref.shape[0]
    greet([(lax.rem(a + j, count), s) for j in range(1, count)])
    own = pltpu.make_async_copy(x_ref.at[a], o_ref.at[a], own_sem)
    own.start()
    copies = []
    for j in range(1, count):
        to = lax.rem(a + j, count)
        copy = pltpu.make_async_remote_copy(
            src_ref=x_ref.at[to],
            dst_ref=o_ref.at[a],
            send_sem=send_sem.at[j],
            recv_sem=recv_sem.at[j],
            device_id=(to, s),
            device_id_type=MESH,
        )
        copy.start()
        copies.append(copy)
    for j in range(1, count):
        got = o_ref.at[lax.rem(a - j + count, count)]
        arrived(got, recv_sem.at[j])
    for copy in copies:
        copy.wait_send()
    own.wait()


def swap_dp(x, cid):
    count = x.shape[0]
    return pl.pallas_call(
        swap_body,
        name="swap_dp",
        out_shape=jax.ShapeDtypeStruct(x.shape, x.dtype),
        in_specs=[pl.BlockSpec(memory_space=pltpu.HBM)],
        out_specs=pl.BlockSpec(memory_space=pltpu.HBM),
        scratch_shapes=[
            pltpu.SemaphoreType.DMA((count,)),
            pltpu.SemaphoreType.DMA((count,)),
            pltpu.SemaphoreType.DMA,
        ],
        compiler_params=pltpu.CompilerParams(collective_id=cid, has_side_effects=True),
    )(x)


def swap_both_body(x_ref, o_ref, send_sem, recv_sem, pass_sem, got_sem, own_sem):
    a, s = lax.axis_index("dp"), lax.axis_index("seq")
    count = x_ref.shape[0]
    greet([(lax.rem(a + j, count), s) for j in range(1, count)] + [(a, 1 - s)])
    own = pltpu.make_async_copy(x_ref.at[a], o_ref.at[s, a], own_sem)
    own.start()
    copies = []

    def pass_on(src, slot, j):
        copy = pltpu.make_async_remote_copy(
            src_ref=src,
            dst_ref=o_ref.at[s, slot],
            send_sem=pass_sem.at[j],
            recv_sem=got_sem.at[j],
            device_id=(a, 1 - s),
            device_id_type=MESH,
        )
        copy.start()
        copies.append(copy)

    pass_on(x_ref.at[a], a, 0)
    for j in range(1, count):
        to = lax.rem(a + j, count)
        copy = pltpu.make_async_remote_copy(
            src_ref=x_ref.at[to],
            dst_ref=o_ref.at[s, a],
            send_sem=send_sem.at[j],
            recv_sem=recv_sem.at[j],
            device_id=(to, s),
            device_id_type=MESH,
        )
        copy.start()
        copies.append(copy)
    for j in range(1, count):
        source = lax.rem(a - j + count, count)
        got = o_ref.at[s, source]
        arrived(got, recv_sem.at[j])
        pass_on(got, source, j)
    for j in range(count):
        got = o_ref.at[1 - s, lax.rem(a - j + count, count)]
        arrived(got, got_sem.at[j])
    for copy in copies:
        copy.wait_send()
    own.wait()


def swap_both(x, cid):
    count = x.shape[0]
    return pl.pallas_call(
        swap_both_body,
        name="swap_both",
        out_shape=jax.ShapeDtypeStruct((2,) + x.shape, x.dtype),
        in_specs=[pl.BlockSpec(memory_space=pltpu.HBM)],
        out_specs=pl.BlockSpec(memory_space=pltpu.HBM),
        scratch_shapes=[pltpu.SemaphoreType.DMA((count,))] * 4 + [pltpu.SemaphoreType.DMA],
        compiler_params=pltpu.CompilerParams(collective_id=cid, has_side_effects=True),
    )(x)


def exchange_body(x_ref, o_ref, send_sem, recv_sem, own_sem):
    e = 2 * lax.axis_index("dp") + lax.axis_index("seq")
    count = x_ref.shape[0]

    def where(number):
        return (number // 2, lax.rem(number, 2))

    greet([where(lax.rem(e + j, count)) for j in range(1, count)])
    own = pltpu.make_async_copy(x_ref.at[e], o_ref.at[e], own_sem)
    own.start()
    copies = []
    for j in range(1, count):
        to = lax.rem(e + j, count)
        copy = pltpu.make_async_remote_copy(
            src_ref=x_ref.at[to],
            dst_ref=o_ref.at[e],
            send_sem=send_sem.at[j],
            recv_sem=recv_sem.at[j],
            device_id=where(to),
            device_id_type=MESH,
        )
        copy.start()
        copies.append(copy)
    for j in range(1, count):
        got = o_ref.at[lax.rem(e - j + count, count)]
        arrived(got, recv_sem.at[j])
    for copy in copies:
        copy.wait_send()
    own.wait()


def exchange_all(x, cid):
    count = x.shape[0]
    return pl.pallas_call(
        exchange_body,
        name="exchange_all",
        out_shape=jax.ShapeDtypeStruct(x.shape, x.dtype),
        in_specs=[pl.BlockSpec(memory_space=pltpu.HBM)],
        out_specs=pl.BlockSpec(memory_space=pltpu.HBM),
        scratch_shapes=[
            pltpu.SemaphoreType.DMA((count,)),
            pltpu.SemaphoreType.DMA((count,)),
            pltpu.SemaphoreType.DMA,
        ],
        compiler_params=pltpu.CompilerParams(collective_id=cid, has_side_effects=True),
    )(x)


def pair_body(x_ref, o_ref, send_sem, recv_sem):
    a, s = lax.axis_index("dp"), lax.axis_index("seq")
    greet([(a, 1 - s)])
    copy = pltpu.make_async_remote_copy(
        src_ref=x_ref,
        dst_ref=o_ref,
        send_sem=send_sem,
        recv_sem=recv_sem,
        device_id=(a, 1 - s),
        device_id_type=MESH,
    )
    copy.start()
    copy.wait()


def pair_swap(x, cid):
    return pl.pallas_call(
        pair_body,
        name="pair_swap",
        out_shape=jax.ShapeDtypeStruct(x.shape, x.dtype),
        in_specs=[pl.BlockSpec(memory_space=pltpu.HBM)],
        out_specs=pl.BlockSpec(memory_space=pltpu.HBM),
        scratch_shapes=[pltpu.SemaphoreType.DMA, pltpu.SemaphoreType.DMA],
        compiler_params=pltpu.CompilerParams(collective_id=cid, has_side_effects=True),
    )(x)


GELU_C = 0.7978845608028654
GELU_A = 0.044715


def gelu_of(x):
    return 0.5 * x * (1.0 + jnp.tanh(GELU_C * (x + GELU_A * (x * x * x))))


def gelu_slope(x):
    t = jnp.tanh(GELU_C * (x + GELU_A * (x * x * x)))
    return 0.5 * (1.0 + t) + 0.5 * x * (1.0 - t * t) * (GELU_C * (1.0 + 3.0 * GELU_A * (x * x)))


CHUNK = 640


def tap_masks(cells, examples):
    rows = examples * SIDE * SIDE
    at = np.arange(rows)
    i, j = (at // SIDE) % SIDE, at % SIDE
    out = np.zeros((16, cells), np.float32)
    for r in range(3):
        for c in range(3):
            ok = (i + r - 1 >= 0) & (i + r - 1 < SIDE) & (j + c - 1 >= 0) & (j + c - 1 < SIDE)
            out[3 * r + c, :rows] = ok
    out[9, :rows] = 1.0
    return out


def tap_shift(tap):
    return SIDE * (tap // 3 - 1) + tap % 3 - 1


def norm_act(values, valid, gain, bias, number):
    centre = jnp.sum(values, 1, keepdims=True) / number
    away = jnp.where(valid > 0, values - centre, 0.0)
    rstd = lax.rsqrt(jnp.sum(away * away, 1, keepdims=True) / number + 1e-05)
    normed = away * rstd
    return normed, rstd, gelu_of(normed * gain + bias)


def put_low(x_ref, y):
    for p in range(PORTIONS):
        x_ref[p] = y[GROUP * p : GROUP * (p + 1)].astype(x_ref.dtype)


def first_body(number, p_ref, w_ref, gb_ref, m_ref, n_ref, rstd_ref, y_ref, x_ref, v_ref):
    cells = p_ref.shape[0]
    for start in range(0, cells, CHUNK):
        v_ref[:, start : start + CHUNK] = lax.dot_general(
            w_ref[...],
            p_ref[start : start + CHUNK, :],
            (((1,), (1,)), ((), ())),
            preferred_element_type=jnp.float32,
        )
    normed, rstd, act = norm_act(v_ref[...], m_ref[9:10, :], gb_ref[:, 0:1], gb_ref[:, 1:2], number)
    n_ref[...] = normed
    rstd_ref[...] = jnp.broadcast_to(rstd, rstd_ref.shape)
    y_ref[...] = act
    put_low(x_ref, act)


def conv_body(number, layer, x_in, w_ref, gb_ref, m_ref, y_in, n_ref, rstd_ref, y_ref, x_ref, z_ref):
    cells = x_in.shape[1]
    rows = y_in.shape[0]
    for start in range(0, cells, CHUNK):
        z_ref[:, start : start + CHUNK] = jnp.dot(
            w_ref[...], x_in[:, start : start + CHUNK], preferred_element_type=jnp.float32
        )
    total = jnp.zeros((rows, cells), jnp.float32)
    for tap in range(9):
        moved = z_ref[rows * tap : rows * (tap + 1), :]
        shift = (-tap_shift(tap)) % cells
        if shift:
            moved = pltpu.roll(moved, shift, 1)
        total = total + jnp.where(m_ref[tap : tap + 1, :] > 0, moved, 0.0)
    normed, rstd, act = norm_act(
        total,
        m_ref[9:10, :],
        gb_ref[:, 2 * layer : 2 * layer + 1],
        gb_ref[:, 2 * layer + 1 : 2 * layer + 2],
        number,
    )
    n_ref[...] = normed
    rstd_ref[...] = jnp.broadcast_to(rstd, rstd_ref.shape)
    y = y_in[...] + act
    y_ref[...] = y
    put_low(x_ref, y)


def norm_slope(number, dy, normed, rstd, gain, bias):
    e = dy * gelu_slope(normed * gain + bias)
    d_gain = jnp.sum(e * normed, 1, keepdims=True)
    d_bias = jnp.sum(e, 1, keepdims=True)
    dn = e * gain
    mean_dn = d_bias * gain / number
    mean_dnn = d_gain * gain / number
    return rstd * (dn - mean_dn - normed * mean_dnn), d_gain, d_bias


def conv_back_body(
    number, layer, dy_ref, n_ref, rstd_ref, gb_ref, m_ref, x_in, wt_ref, dx_ref, g_ref, s_ref, d_ref
):
    cells = x_in.shape[1]
    rows = dy_ref.shape[0]
    dv, d_gain, d_bias = norm_slope(
        number,
        dy_ref[...],
        n_ref[...],
        rstd_ref[:, 0:1],
        gb_ref[:, 2 * layer : 2 * layer + 1],
        gb_ref[:, 2 * layer + 1 : 2 * layer + 2],
    )
    lanes = lax.broadcasted_iota(jnp.int32, s_ref.shape, 1)
    s_ref[...] = jnp.where(lanes == 0, d_gain, d_bias)
    for tap in range(9):
        shift = tap_shift(tap) % cells
        moved = pltpu.roll(dv, shift, 1) if shift else dv
        moved = jnp.where(m_ref[8 - tap : 9 - tap, :] > 0, moved, 0.0)
        d_ref[rows * tap : rows * (tap + 1), :] = moved.astype(d_ref.dtype)
    for start in range(0, cells, CHUNK):
        dx_ref[:, start : start + CHUNK] = jnp.dot(
            wt_ref[...], d_ref[:, start : start + CHUNK], preferred_element_type=jnp.float32
        ).astype(dx_ref.dtype)
    for start in range(0, x_in.shape[0], 256):
        g_ref[:, start : start + 256] = lax.dot_general(
            d_ref[...],
            x_in[start : start + 256, :],
            (((1,), (1,)), ((), ())),
            preferred_element_type=jnp.float32,
        ).astype(g_ref.dtype)


def first_back_body(number, dy_ref, n_ref, rstd_ref, gb_ref, p_ref, g_ref, s_ref):
    dv, d_gain, d_bias = norm_slope(
        number, dy_ref[...], n_ref[...], rstd_ref[:, 0:1], gb_ref[:, 0:1], gb_ref[:, 1:2]
    )
    lanes = lax.broadcasted_iota(jnp.int32, s_ref.shape, 1)
    s_ref[...] = jnp.where(lanes == 0, d_gain, d_bias)
    g_ref[...] = jnp.dot(
        dv.astype(p_ref.dtype), p_ref[...], preferred_element_type=jnp.float32
    ).astype(g_ref.dtype)


BIG = pltpu.CompilerParams(vmem_limit_bytes=48 << 20)


def first_block(pixels, w, gb, masks, number):
    rows, cells = w.shape[0], pixels.shape[0]
    return pl.pallas_call(
        functools.partial(first_body, number),
        name="stem_first",
        out_shape=(
            jax.ShapeDtypeStruct((rows, cells), jnp.float32),
            jax.ShapeDtypeStruct((rows, 128), jnp.float32),
            jax.ShapeDtypeStruct((rows, cells), jnp.float32),
            jax.ShapeDtypeStruct((PORTIONS, GROUP, cells), LOW),
        ),
        scratch_shapes=[pltpu.VMEM((rows, cells), jnp.float32)],
        compiler_params=BIG,
    )(pixels, w, gb, masks)


def conv_block(layer, x_all, w, gb, masks, y, number):
    rows, cells = y.shape
    return pl.pallas_call(
        functools.partial(conv_body, number, layer),
        name="stem_conv",
        out_shape=(
            jax.ShapeDtypeStruct((rows, cells), jnp.float32),
            jax.ShapeDtypeStruct((rows, 128), jnp.float32),
            jax.ShapeDtypeStruct((rows, cells), jnp.float32),
            jax.ShapeDtypeStruct((PORTIONS, GROUP, cells), LOW),
        ),
        scratch_shapes=[pltpu.VMEM((9 * rows, cells), jnp.float32)],
        compiler_params=BIG,
    )(x_all, w, gb, masks, y)


def conv_block_back(layer, dy, normed, rstd, gb, masks, x_all, w_t, number):
    rows, cells = dy.shape
    features = x_all.shape[0]
    return pl.pallas_call(
        functools.partial(conv_back_body, number, layer),
        name="stem_conv_back",
        out_shape=(
            jax.ShapeDtypeStruct((features, cells), LOW),
            jax.ShapeDtypeStruct((9 * rows, features), LOW),
            jax.ShapeDtypeStruct((rows, 128), jnp.float32),
        ),
        scratch_shapes=[pltpu.VMEM((9 * rows, cells), LOW)],
        compiler_params=BIG,
    )(dy, normed, rstd, gb, masks, x_all, w_t)


def first_block_back(dy, normed, rstd, gb, pixels, number):
    rows, cells = dy.shape
    return pl.pallas_call(
        functools.partial(first_back_body, number),
        name="stem_first_back",
        out_shape=(
            jax.ShapeDtypeStruct((rows, pixels.shape[1]), LOW),
            jax.ShapeDtypeStruct((rows, 128), jnp.float32),
        ),
        compiler_params=BIG,
    )(dy, normed, rstd, gb, pixels)


def padded_2(cells, sides, width):
    for axis, dim in sides:
        count = lax.axis_size(axis)
        ends = count - 1
        head = lax.slice_in_dim(cells, 0, width, axis=dim)
        tail = lax.slice_in_dim(cells, cells.shape[dim] - width, cells.shape[dim], axis=dim)
        cells = jnp.concatenate(
            [
                lax.ppermute(tail, axis, [(i, (i + 1) % count) for i in range(ends)]),
                cells,
                lax.ppermute(head, axis, [((i + 1) % count, i) for i in range(ends)]),
            ],
            axis=dim,
        )
    return cells


def passed_along(array, axis, by):
    length = lax.axis_size(axis)
    pairs = [(i, i + by) for i in range(length) if 0 <= i + by < length]
    return lax.ppermute(array, axis, pairs)


def layer_norm(activ, gain_vec, bias_vec):
    row_mean = jnp.mean(activ, -1, keepdims=True)
    centred = activ - row_mean
    spread = jnp.mean(centred * centred, -1, keepdims=True)
    return centred * lax.rsqrt(spread + 1e-06) * gain_vec + bias_vec


def heads_of(matrix):
    return matrix.reshape(matrix.shape[0], HEADS, -1)


def dot_float(left, right):
    return jnp.dot(left, right, preferred_element_type=jnp.float32)


def norm_batch(values, gain_vec, bias_vec, number):
    sums = lax.psum((jnp.sum(values, 0), jnp.sum(values * values, 0)), ("dp", "seq"))
    col_mean = sums[0] / number
    col_var = sums[1] / number - col_mean * col_mean
    inv_std = lax.rsqrt(col_var + 1e-05)
    normed = (values - col_mean) * inv_std
    return (normed, inv_std, normed * gain_vec + bias_vec)


def batch_back(d_pre, normed, inv_std, gain_vec, number):
    grad_gain = jnp.sum(d_pre * normed, 0)
    grad_bias = jnp.sum(d_pre, 0)
    d_normed = d_pre * gain_vec
    sums = lax.psum((jnp.sum(d_normed, 0), jnp.sum(d_normed * normed, 0)), ("dp", "seq"))
    d_values = inv_std * (d_normed - sums[0] / number - normed * (sums[1] / number))
    return (d_values, grad_gain, grad_bias)


def conv_fwd(flat_low, weight):
    features = flat_low.shape[1]
    grid_rows = flat_low.shape[0] // SIDE
    grid = flat_low.reshape(grid_rows, SIDE, features)
    padded = padded_2(grid, (("seq", 0),), 1)
    padded = jnp.pad(padded, ((0, 0), (1, 1), (0, 0)))
    total = jnp.zeros((grid_rows * SIDE, features), jnp.float32)
    for row_tap in range(3):
        for col_tap in range(3):
            tap = 3 * row_tap + col_tap
            window = padded[row_tap : row_tap + grid_rows, col_tap : col_tap + SIDE].reshape(
                -1, features
            )
            total = total + dot_float(window, weight[tap * features : (tap + 1) * features])
    return (total, padded)


def send_rim(rim_rows, offset):
    return passed_along(rim_rows.astype(jnp.bfloat16), "seq", offset).astype(rim_rows.dtype)


def conv_back(padded, d_out_low, weight):
    features = d_out_low.shape[1]
    grid_rows = padded.shape[0] - 2
    d_padded = jnp.zeros((grid_rows + 2, SIDE + 2, features), jnp.float32)
    tap_grads = []
    for row_tap in range(3):
        for col_tap in range(3):
            tap = 3 * row_tap + col_tap
            tap_weight = weight[tap * features : (tap + 1) * features]
            window = padded[row_tap : row_tap + grid_rows, col_tap : col_tap + SIDE].reshape(
                -1, features
            )
            tap_grads.append(dot_float(window.T, d_out_low))
            spread = dot_float(d_out_low, tap_weight.T).reshape(grid_rows, SIDE, features)
            d_padded = d_padded + jnp.pad(
                spread, ((row_tap, 2 - row_tap), (col_tap, 2 - col_tap), (0, 0))
            )
    inner = d_padded[1 : grid_rows + 1, 1 : SIDE + 1]
    from_below = send_rim(d_padded[0, 1 : SIDE + 1], -1)
    from_above = send_rim(d_padded[grid_rows + 1, 1 : SIDE + 1], 1)
    inner = inner.at[grid_rows - 1].add(from_below).at[0].add(from_above)
    return (jnp.concatenate(tap_grads, 0), inner.reshape(-1, features))


def attend_block(queries, key_rows, value_rows, allowed, score_scale):
    scores = (
        jnp.einsum("qhd,khd->hqk", queries, key_rows, preferred_element_type=jnp.float32)
        * score_scale
    )
    scores = jnp.where(allowed[None], scores, -1000000000.0)
    row_max = jnp.max(scores, -1, keepdims=True)
    exponent = jnp.exp(scores - row_max)
    row_total = jnp.sum(exponent, -1, keepdims=True)
    softmax = (exponent / row_total).astype(jnp.bfloat16)
    outputs = jnp.einsum("hqk,khd->qhd", softmax, value_rows, preferred_element_type=jnp.float32)
    return (outputs, row_max + jnp.log(row_total))


def attend_back(queries, key_rows, value_rows, allowed, score_scale, grad_out, log_total):
    scores = (
        jnp.einsum("qhd,khd->hqk", queries, key_rows, preferred_element_type=jnp.float32)
        * score_scale
    )
    scores = jnp.where(allowed[None], scores, -1000000000.0)
    softmax = jnp.exp(scores - log_total)
    d_softmax = jnp.einsum("qhd,khd->hqk", grad_out, value_rows, preferred_element_type=jnp.float32)
    row_delta = jnp.sum(softmax * d_softmax, -1, keepdims=True)
    d_scores = (softmax * (d_softmax - row_delta)).astype(jnp.bfloat16)
    d_query = (
        jnp.einsum("hqk,khd->qhd", d_scores, key_rows, preferred_element_type=jnp.float32)
        * score_scale
    )
    d_keys = (
        jnp.einsum("hqk,qhd->khd", d_scores, queries, preferred_element_type=jnp.float32)
        * score_scale
    )
    d_values = jnp.einsum(
        "hqk,qhd->khd", softmax.astype(jnp.bfloat16), grad_out, preferred_element_type=jnp.float32
    )
    return (d_query, d_keys, d_values)


def run_attention(queries, key_rows, value_rows, allow_fn, score_scale):
    row_count = queries.shape[0]
    block_rows = min(512, row_count)
    block_count = row_count // block_rows
    query_blocks = queries.reshape(block_count, block_rows, queries.shape[1], queries.shape[2])
    starts = jnp.arange(block_count, dtype=jnp.int32) * block_rows

    def one_block(block_pair):
        return attend_block(
            block_pair[0], key_rows, value_rows, allow_fn(block_pair[1], block_rows), score_scale
        )

    outputs, log_total = lax.map(one_block, (query_blocks, starts))
    return (outputs.reshape(queries.shape), log_total)


def run_back(queries, key_rows, value_rows, allow_fn, score_scale, grad_out, log_total):
    row_count = queries.shape[0]
    block_rows = min(512, row_count)
    block_count = row_count // block_rows
    query_blocks = queries.reshape(block_count, block_rows, queries.shape[1], queries.shape[2])
    grad_blocks = grad_out.reshape(query_blocks.shape)
    starts = jnp.arange(block_count, dtype=jnp.int32) * block_rows

    def one_block(running, block_items):
        query_part, grad_part, total_part, first_row = block_items
        d_query, d_keys, d_values = attend_back(
            query_part,
            key_rows,
            value_rows,
            allow_fn(first_row, block_rows),
            score_scale,
            grad_part,
            total_part,
        )
        return ((running[0] + d_keys, running[1] + d_values), d_query)

    zero_grads = jnp.zeros(key_rows.shape, jnp.float32)
    sums_kv, d_query = lax.scan(
        one_block, (zero_grads, zero_grads), (query_blocks, grad_blocks, log_total, starts)
    )
    return (d_query.reshape(queries.shape), sums_kv[0], sums_kv[1])


def general_device(
    captions,
    patches,
    prefix,
    prefix_count,
    caption_len,
    cotangent,
    w_patch,
    w_conv,
    w_self_qkv,
    w_self_out,
    w_cross_q,
    w_cross_kv,
    w_cross_out,
    w_up,
    w_down,
    norm_params,
):
    gathered = (
        lax.all_gather(w_patch, "dp", axis=0, tiled=True),
        lax.all_gather(w_conv, "dp", axis=1, tiled=True),
        lax.all_gather(w_self_qkv, "dp", axis=0, tiled=True),
        lax.all_gather(w_self_out, "dp", axis=0, tiled=True),
        lax.all_gather(w_cross_q, "dp", axis=0, tiled=True),
        lax.all_gather(w_cross_kv, "dp", axis=0, tiled=True),
        lax.all_gather(w_cross_out, "dp", axis=0, tiled=True),
        lax.all_gather(w_up, "dp", axis=0, tiled=True),
        lax.all_gather(w_down, "dp", axis=0, tiled=True),
        lax.all_gather(norm_params, "dp", axis=1, tiled=True),
    )
    (
        full_patch,
        full_conv,
        full_qkv,
        full_sout,
        full_cq,
        full_ckv,
        full_cout,
        full_up,
        full_down,
        full_norms,
    ) = gathered
    norms = full_norms.astype(jnp.float32)
    features = full_sout.shape[0]
    score_scale = (features // HEADS) ** (-0.5)
    seq_count = lax.axis_size("seq")
    seq_index = lax.axis_index("seq")
    pixels = patches[0]
    stem_out = dot_float(pixels, full_patch)
    number = stem_out.shape[0] * lax.axis_size("dp") * seq_count
    normed_one, inv_one, pre_one = norm_batch(stem_out, norms[0], norms[1], number)
    first_out = jax.nn.gelu(pre_one)
    first_low = first_out.astype(jnp.bfloat16)
    conv_two, padded_two = conv_fwd(first_low, full_conv[0])
    normed_two, inv_two, pre_two = norm_batch(conv_two, norms[2], norms[3], number)
    second_out = first_out + jax.nn.gelu(pre_two)
    second_low = second_out.astype(jnp.bfloat16)
    conv_three, padded_three = conv_fwd(second_low, full_conv[1])
    normed_three, inv_three, pre_three = norm_batch(conv_three, norms[4], norms[5], number)
    third_out = second_out + jax.nn.gelu(pre_three)
    patch_low = third_out.astype(jnp.bfloat16)
    prefix_low = prefix[0]
    kv_prefix = dot_float(prefix_low, full_ckv).astype(jnp.bfloat16)
    kv_patch = dot_float(patch_low, full_ckv).astype(jnp.bfloat16)
    all_prefix, all_patch = (
        lax.all_gather(kv_prefix, "seq", axis=0, tiled=True),
        lax.all_gather(kv_patch, "seq", axis=0, tiled=True),
    )
    memory_kv = jnp.concatenate([all_prefix, all_patch], 0)
    mem_rows = memory_kv.shape[0]
    prefix_total = all_prefix.shape[0]
    mem_keys = heads_of(memory_kv[:, :features])
    mem_values = heads_of(memory_kv[:, features:])
    slot_ids = jnp.arange(mem_rows, dtype=jnp.int32)
    mem_allowed = (slot_ids >= prefix_total) | (slot_ids < prefix_count[0])

    def cross_allow(first_row, block_rows):
        return jnp.broadcast_to(mem_allowed[None], (block_rows, mem_rows))

    inputs = captions[0].astype(jnp.float32)
    row_count = inputs.shape[0]
    low_one = layer_norm(inputs, norms[6], norms[7]).astype(jnp.bfloat16)
    qkv = dot_float(low_one, full_qkv).astype(jnp.bfloat16)
    queries = heads_of(qkv[:, :features])
    own_keys = heads_of(qkv[:, features : 2 * features])
    own_values = heads_of(qkv[:, 2 * features :])
    key_parts = [own_keys]
    value_parts = [own_values]
    position_parts = [seq_index * row_count + jnp.arange(row_count, dtype=jnp.int32)]
    offset = 1
    got_keys, got_values = passed_along((own_keys, own_values), "seq", offset)
    key_parts.insert(0, got_keys)
    value_parts.insert(0, got_values)
    position_parts.insert(
        0, (seq_index - offset) * row_count + jnp.arange(row_count, dtype=jnp.int32)
    )
    all_keys = jnp.concatenate(key_parts, 0)
    all_values = jnp.concatenate(value_parts, 0)
    key_pos = jnp.concatenate(position_parts, 0)
    length_one = caption_len[0]

    def self_allow(first_row, block_rows):
        query_pos = seq_index * row_count + first_row + jnp.arange(block_rows, dtype=jnp.int32)
        return (
            (key_pos[None] <= query_pos[:, None])
            & (key_pos[None] >= 0)
            & (key_pos[None] < length_one)
        )

    self_out, self_total = run_attention(queries, all_keys, all_values, self_allow, score_scale)
    self_low = self_out.reshape(row_count, features).astype(jnp.bfloat16)
    after_self = inputs + dot_float(self_low, full_sout)
    low_two = layer_norm(after_self, norms[8], norms[9]).astype(jnp.bfloat16)
    cross_flat = dot_float(low_two, full_cq).astype(jnp.bfloat16)
    cross_q = heads_of(cross_flat)
    cross_out, cross_total = run_attention(cross_q, mem_keys, mem_values, cross_allow, score_scale)
    cross_low = cross_out.reshape(row_count, features).astype(jnp.bfloat16)
    after_cross = after_self + dot_float(cross_low, full_cout)
    low_three = layer_norm(after_cross, norms[10], norms[11]).astype(jnp.bfloat16)
    up_proj = dot_float(low_three, full_up)
    hidden_low = jax.nn.gelu(up_proj).astype(jnp.bfloat16)
    result = after_cross + dot_float(hidden_low, full_down)
    back_weights = (
        lax.all_gather(w_patch, "dp", axis=0, tiled=True),
        lax.all_gather(w_conv, "dp", axis=1, tiled=True),
        lax.all_gather(w_self_qkv, "dp", axis=0, tiled=True),
        lax.all_gather(w_self_out, "dp", axis=0, tiled=True),
        lax.all_gather(w_cross_q, "dp", axis=0, tiled=True),
        lax.all_gather(w_cross_kv, "dp", axis=0, tiled=True),
        lax.all_gather(w_cross_out, "dp", axis=0, tiled=True),
        lax.all_gather(w_up, "dp", axis=0, tiled=True),
        lax.all_gather(w_down, "dp", axis=0, tiled=True),
        lax.all_gather(norm_params, "dp", axis=1, tiled=True),
    )
    (
        back_patch,
        back_conv,
        back_qkv,
        back_sout,
        back_cq,
        back_ckv,
        back_cout,
        back_up,
        back_down,
        back_norms,
    ) = back_weights
    bnorms = back_norms.astype(jnp.float32)
    out_grad = cotangent[0].astype(jnp.float32)
    grad_low = cotangent[0]
    grad_down = dot_float(hidden_low.T, grad_low)
    d_hidden = dot_float(grad_low, back_down.T)
    unused_gelu, gelu_back = jax.vjp(jax.nn.gelu, up_proj)
    d_upper = gelu_back(d_hidden)[0].astype(jnp.bfloat16)
    grad_up = dot_float(low_three.T, d_upper)
    unused_three, norm_back_three = jax.vjp(layer_norm, after_cross, bnorms[10], bnorms[11])
    d_three, grad_gain_three, grad_bias_three = norm_back_three(dot_float(d_upper, back_up.T))
    d_after_cross = out_grad + d_three
    cross_grad_low = d_after_cross.astype(jnp.bfloat16)
    grad_cout = dot_float(cross_low.T, cross_grad_low)
    d_cross = heads_of(dot_float(cross_grad_low, back_cout.T).astype(jnp.bfloat16))
    d_cross_q, d_mem_keys, d_mem_values = run_back(
        cross_q, mem_keys, mem_values, cross_allow, score_scale, d_cross, cross_total
    )
    d_cross_low = d_cross_q.reshape(row_count, features).astype(jnp.bfloat16)
    grad_cq = dot_float(low_two.T, d_cross_low)
    unused_two, norm_back_two = jax.vjp(layer_norm, after_self, bnorms[8], bnorms[9])
    d_two, grad_gain_two, grad_bias_two = norm_back_two(dot_float(d_cross_low, back_cq.T))
    d_after_self = d_after_cross + d_two
    d_memory = jnp.concatenate(
        [d_mem_keys.reshape(mem_rows, features), d_mem_values.reshape(mem_rows, features)], 1
    )
    mine_prefix, mine_patch = (
        lax.psum_scatter(
            d_memory[:prefix_total].astype(jnp.bfloat16), "seq", scatter_dimension=0, tiled=True
        ).astype(jnp.float32),
        lax.psum_scatter(
            d_memory[prefix_total:].astype(jnp.bfloat16), "seq", scatter_dimension=0, tiled=True
        ).astype(jnp.float32),
    )
    mine_prefix_low = mine_prefix.astype(jnp.bfloat16)
    mine_patch_low = mine_patch.astype(jnp.bfloat16)
    grad_ckv = dot_float(prefix_low.T, mine_prefix_low) + dot_float(patch_low.T, mine_patch_low)
    prefix_back = dot_float(mine_prefix_low, back_ckv.T)
    d_third = dot_float(mine_patch_low, back_ckv.T)
    unused_act_three, act_back_three = jax.vjp(jax.nn.gelu, pre_three)
    d_conv_three, grad_gain_bn3, grad_bias_bn3 = batch_back(
        act_back_three(d_third)[0], normed_three, inv_three, bnorms[4], number
    )
    grad_conv_one, d_second_in = conv_back(
        padded_three, d_conv_three.astype(jnp.bfloat16), back_conv[1]
    )
    d_second = d_third + d_second_in
    unused_act_two, act_back_two = jax.vjp(jax.nn.gelu, pre_two)
    d_conv_two, grad_gain_bn2, grad_bias_bn2 = batch_back(
        act_back_two(d_second)[0], normed_two, inv_two, bnorms[2], number
    )
    grad_conv_zero, d_first_in = conv_back(
        padded_two, d_conv_two.astype(jnp.bfloat16), back_conv[0]
    )
    d_first = d_second + d_first_in
    unused_act_one, act_back_one = jax.vjp(jax.nn.gelu, pre_one)
    d_stem, grad_gain_bn1, grad_bias_bn1 = batch_back(
        act_back_one(d_first)[0], normed_one, inv_one, bnorms[0], number
    )
    grad_patch = dot_float(pixels.T, d_stem.astype(jnp.bfloat16))
    grad_conv = jnp.stack([grad_conv_zero, grad_conv_one])
    self_grad_low = d_after_self.astype(jnp.bfloat16)
    grad_sout = dot_float(self_low.T, self_grad_low)
    d_self = heads_of(dot_float(self_grad_low, back_sout.T).astype(jnp.bfloat16))
    d_query, d_all_keys, d_all_values = run_back(
        queries, all_keys, all_values, self_allow, score_scale, d_self, self_total
    )
    own_start = (seq_count - 1) * row_count
    own_dkeys = d_all_keys[own_start:]
    own_dvalues = d_all_values[own_start:]
    offset = 1
    piece_start = (seq_count - 1 - offset) * row_count
    back_keys = passed_along(
        d_all_keys[piece_start : piece_start + row_count].astype(jnp.bfloat16), "seq", -offset
    ).astype(jnp.float32)
    back_values = passed_along(
        d_all_values[piece_start : piece_start + row_count].astype(jnp.bfloat16), "seq", -offset
    ).astype(jnp.float32)
    own_dkeys = own_dkeys + back_keys
    own_dvalues = own_dvalues + back_values
    d_qkv = jnp.concatenate(
        [
            d_query.reshape(row_count, features),
            own_dkeys.reshape(row_count, features),
            own_dvalues.reshape(row_count, features),
        ],
        1,
    ).astype(jnp.bfloat16)
    grad_qkv = dot_float(low_one.T, d_qkv)
    unused_one, norm_back_one = jax.vjp(layer_norm, inputs, bnorms[6], bnorms[7])
    d_one, grad_gain_one, grad_bias_one = norm_back_one(dot_float(d_qkv, back_qkv.T))
    d_inputs = d_after_self + d_one
    grad_norms = jnp.stack(
        [
            grad_gain_bn1,
            grad_bias_bn1,
            grad_gain_bn2,
            grad_bias_bn2,
            grad_gain_bn3,
            grad_bias_bn3,
            grad_gain_one,
            grad_bias_one,
            grad_gain_two,
            grad_bias_two,
            grad_gain_three,
            grad_bias_three,
        ]
    )
    shard_sums = (
        lax.psum_scatter(grad_patch, "dp", scatter_dimension=0, tiled=True),
        lax.psum_scatter(grad_conv, "dp", scatter_dimension=1, tiled=True),
        lax.psum_scatter(grad_qkv, "dp", scatter_dimension=0, tiled=True),
        lax.psum_scatter(grad_sout, "dp", scatter_dimension=0, tiled=True),
        lax.psum_scatter(grad_cq, "dp", scatter_dimension=0, tiled=True),
        lax.psum_scatter(grad_ckv, "dp", scatter_dimension=0, tiled=True),
        lax.psum_scatter(grad_cout, "dp", scatter_dimension=0, tiled=True),
        lax.psum_scatter(grad_up, "dp", scatter_dimension=0, tiled=True),
        lax.psum_scatter(grad_down, "dp", scatter_dimension=0, tiled=True),
        lax.psum_scatter(grad_norms, "dp", scatter_dimension=1, tiled=True),
    )
    totals = (
        lax.psum(shard_sums[0].astype(jnp.bfloat16), "seq").astype(jnp.float32),
        lax.psum(shard_sums[1].astype(jnp.bfloat16), "seq").astype(jnp.float32),
        lax.psum(shard_sums[2].astype(jnp.bfloat16), "seq").astype(jnp.float32),
        lax.psum(shard_sums[3].astype(jnp.bfloat16), "seq").astype(jnp.float32),
        lax.psum(shard_sums[4].astype(jnp.bfloat16), "seq").astype(jnp.float32),
        lax.psum(shard_sums[5].astype(jnp.bfloat16), "seq").astype(jnp.float32),
        lax.psum(shard_sums[6].astype(jnp.bfloat16), "seq").astype(jnp.float32),
        lax.psum(shard_sums[7].astype(jnp.bfloat16), "seq").astype(jnp.float32),
        lax.psum(shard_sums[8].astype(jnp.bfloat16), "seq").astype(jnp.float32),
        lax.psum(shard_sums[9].astype(jnp.bfloat16), "seq").astype(jnp.float32),
    )
    return (
        result[None].astype(jnp.bfloat16),
        d_inputs[None].astype(jnp.bfloat16),
        prefix_back[None].astype(jnp.bfloat16),
        totals[0],
        totals[1],
        totals[2],
        totals[3],
        totals[4],
        totals[5],
        totals[6],
        totals[7],
        totals[8],
        totals[9],
    )


def low_dot(left, right):
    return dot_float(left, right).astype(LOW)


def dot_t(left, right):
    return lax.dot_general(left, right, (((1,), (1,)), ((), ())), preferred_element_type=jnp.float32)


def t_dot(left, right):
    return lax.dot_general(left, right, (((0,), (0,)), ((), ())), preferred_element_type=jnp.float32)


def stem_weights(w_patch, w_conv, norm_params, s):
    depth, conv_rows, patch_rows = w_conv.shape[0], w_conv.shape[1], w_patch.shape[0]
    features = w_patch.shape[1]
    flat = jnp.concatenate([w_conv.reshape(-1, features), w_patch], 0).T
    blocks = slots_to_devices(flat.reshape(PORTIONS, 32, GROUP, flat.shape[1]))
    blocks = blocks.reshape(16, 2, PORTIONS * GROUP, flat.shape[1])
    blocks = lax.dynamic_index_in_dim(blocks, s, 1, keepdims=False)
    rows = PORTIONS * GROUP
    extra = jnp.pad(norm_params, ((0, rows - norm_params.shape[0]), (0, 0)))
    blocks = jnp.concatenate([blocks, jnp.broadcast_to(extra, (16,) + extra.shape)], 2)
    got = swap_dp(blocks, 0)
    convs = []
    for layer in range(depth):
        part = got[:, :, layer * conv_rows : (layer + 1) * conv_rows]
        part = part.transpose(1, 0, 2).reshape(rows, 9, features).transpose(1, 0, 2)
        convs.append(part.reshape(9 * rows, features))
    at = depth * conv_rows
    patch = got[:, :, at : at + patch_rows].transpose(1, 0, 2).reshape(rows, -1)
    at = at + patch_rows
    norms = got[:, : norm_params.shape[0], at:].transpose(1, 0, 2).reshape(norm_params.shape[0], -1)
    return convs, patch, norms


def own_columns(norms):
    bits = my_bits()
    cut = norms.reshape(norms.shape[0], PORTIONS, 32, GROUP)
    parts = [
        lax.dynamic_index_in_dim(cut[:, p], slot_of(bits, p), 1, keepdims=False)
        for p in range(PORTIONS)
    ]
    mine = jnp.concatenate(parts, 1).T
    return jnp.pad(mine, ((0, 0), (0, 128 - mine.shape[1])))


def fast_device(
    captions,
    patches,
    prefix,
    prefix_count,
    caption_len,
    cotangent,
    w_patch,
    w_conv,
    w_self_qkv,
    w_self_out,
    w_cross_q,
    w_cross_kv,
    w_cross_out,
    w_up,
    w_down,
    norm_params,
):
    a_index, s_index = lax.axis_index("dp"), lax.axis_index("seq")
    examples, halves = 16, 2
    features = w_self_out.shape[1]
    score_scale = (features // HEADS) ** (-0.5)

    def chunks(w):
        return [w[:, i * features : (i + 1) * features] for i in range(w.shape[1] // features)]

    qkv_w = lax.all_gather(jnp.stack(chunks(w_self_qkv)), "dp", axis=1, tiled=True)
    rest_w = lax.all_gather(
        jnp.stack([w_self_out, w_cross_q] + chunks(w_cross_kv) + [w_cross_out] + chunks(w_up)),
        "dp",
        axis=1,
        tiled=True,
    )
    down_w = lax.all_gather(w_down, "dp", axis=0, tiled=True)
    sout_w, cq_w, ck_w, cv_w, cout_w = (rest_w[i] for i in range(5))
    up_ws = [rest_w[5 + i] for i in range(4)]
    down_ws = [down_w[i * features : (i + 1) * features] for i in range(4)]

    convs, patch_w, norms_low = stem_weights(w_patch, w_conv, norm_params, s_index)
    norms = norms_low.astype(jnp.float32)
    own_gb = own_columns(norms[:6])
    own_cells = patches.shape[1]
    number = own_cells * examples * halves
    cells = -(-number // CHUNK) * CHUNK
    masks = jnp.asarray(tap_masks(cells, examples))
    pixels_split = patches[0].reshape(own_cells, PORTIONS, -1).transpose(1, 0, 2)
    pixels = slots_to_devices(gather_all(pixels_split, 1))
    pixels = pixels.transpose(0, 2, 1, 3).reshape(number, -1)
    pixels = jnp.pad(pixels, ((0, cells - number), (0, 0)))
    n1, r1, y1, x1 = first_block(pixels, patch_w, own_gb, masks, number)
    x1_all = gather_all(x1, 2).reshape(features, cells)
    n2, r2, y2, x2 = conv_block(1, x1_all, convs[0], own_gb, masks, y1, number)
    x2_all = gather_all(x2, 3).reshape(features, cells)
    n3, r3, y3, x3 = conv_block(2, x2_all, convs[1], own_gb, masks, y2, number)
    rows_own = PORTIONS * GROUP
    grid = halves * own_cells
    out_blocks = x3.reshape(rows_own, cells)[:, :number].reshape(rows_own, examples, grid)
    out_blocks = jnp.broadcast_to(
        out_blocks.transpose(1, 0, 2)[:, None], (examples, halves, rows_own, grid)
    )
    in_blocks = exchange_all(out_blocks.reshape(32, rows_own, grid), 4)
    patch_all = devices_to_slots(in_blocks.reshape(32, PORTIONS, GROUP, grid))
    patch_all = patch_all.reshape(features, grid).T

    prefix_own = prefix[0]
    prefix_half = prefix_own.shape[0]
    prefix_other = lax.ppermute(prefix_own, "seq", [(0, 1), (1, 0)])
    first_half = s_index == 0
    prefix_all = jnp.concatenate(
        [
            jnp.where(first_half, prefix_own, prefix_other),
            jnp.where(first_half, prefix_other, prefix_own),
        ],
        0,
    )
    memory = jnp.concatenate([prefix_all, patch_all], 0)
    mem_rows = memory.shape[0]
    prefix_total = prefix_all.shape[0]
    mem_keys = heads_of(low_dot(memory, ck_w))
    mem_values = heads_of(low_dot(memory, cv_w))
    slot_ids = jnp.arange(mem_rows, dtype=jnp.int32)
    mem_allowed = (slot_ids >= prefix_total) | (slot_ids < prefix_count[0])

    def cross_allow(first_row, block_rows):
        return jnp.broadcast_to(mem_allowed[None], (block_rows, mem_rows))

    inputs = captions[0].astype(jnp.float32)
    row_count = inputs.shape[0]
    low_one = layer_norm(inputs, norms[6], norms[7]).astype(LOW)
    queries, own_keys, own_values = (heads_of(low_dot(low_one, qkv_w[i])) for i in range(3))
    got_keys, got_values = passed_along((own_keys, own_values), "seq", 1)
    all_keys = jnp.concatenate([got_keys, own_keys], 0)
    all_values = jnp.concatenate([got_values, own_values], 0)
    ids = jnp.arange(row_count, dtype=jnp.int32)
    key_pos = jnp.concatenate([(s_index - 1) * row_count + ids, s_index * row_count + ids], 0)
    length_one = caption_len[0]

    def self_allow(first_row, block_rows):
        query_pos = s_index * row_count + first_row + jnp.arange(block_rows, dtype=jnp.int32)
        return (
            (key_pos[None] <= query_pos[:, None])
            & (key_pos[None] >= 0)
            & (key_pos[None] < length_one)
        )

    self_out, self_total = run_attention(queries, all_keys, all_values, self_allow, score_scale)
    self_low = self_out.reshape(row_count, features).astype(LOW)
    after_self = inputs + dot_float(self_low, sout_w)
    low_two = layer_norm(after_self, norms[8], norms[9]).astype(LOW)
    cross_q = heads_of(low_dot(low_two, cq_w))
    cross_out, cross_total = run_attention(cross_q, mem_keys, mem_values, cross_allow, score_scale)
    cross_low = cross_out.reshape(row_count, features).astype(LOW)
    after_cross = after_self + dot_float(cross_low, cout_w)
    low_three = layer_norm(after_cross, norms[10], norms[11]).astype(LOW)
    ups = [dot_float(low_three, w) for w in up_ws]
    hiddens = [jax.nn.gelu(u).astype(LOW) for u in ups]
    result = after_cross
    for h, w in zip(hiddens, down_ws):
        result = result + dot_float(h, w)

    out_grad = cotangent[0].astype(jnp.float32)
    grad_low = cotangent[0]
    grads_down = low_dot(jnp.concatenate(hiddens, 1).T, grad_low)
    d_uppers = []
    for u, w in zip(ups, down_ws):
        d_uppers.append((dot_t(grad_low, w) * gelu_slope(u)).astype(LOW))
    grads_up = [t_dot(low_three, d).astype(LOW) for d in d_uppers]
    d_normed = dot_t(d_uppers[0], up_ws[0])
    for d, w in zip(d_uppers[1:], up_ws[1:]):
        d_normed = d_normed + dot_t(d, w)
    unused_three, norm_back_three = jax.vjp(layer_norm, after_cross, norms[10], norms[11])
    d_three, grad_gain_three, grad_bias_three = norm_back_three(d_normed)
    down_parts = grads_down.reshape(examples, 4, -1, features).transpose(1, 0, 2, 3)
    down_parts = down_parts.reshape(4, features, features)
    late_sums = [
        lax.psum_scatter(
            jnp.concatenate([down_parts, jnp.stack(grads_up)], 0),
            "dp",
            scatter_dimension=1,
            tiled=True,
        )
    ]
    d_after_cross = out_grad + d_three
    cross_grad_low = d_after_cross.astype(LOW)
    grad_cout = t_dot(cross_low, cross_grad_low).astype(LOW)
    d_cross = heads_of(dot_t(cross_grad_low, cout_w).astype(LOW))
    d_cross_q, d_mem_keys, d_mem_values = run_back(
        cross_q, mem_keys, mem_values, cross_allow, score_scale, d_cross, cross_total
    )
    d_cross_low = d_cross_q.reshape(row_count, features).astype(LOW)
    grad_cq = t_dot(low_two, d_cross_low).astype(LOW)
    unused_two, norm_back_two = jax.vjp(layer_norm, after_self, norms[8], norms[9])
    d_two, grad_gain_two, grad_bias_two = norm_back_two(dot_t(d_cross_low, cq_w))
    d_after_self = d_after_cross + d_two
    d_memory = jnp.concatenate(
        [d_mem_keys.reshape(mem_rows, features), d_mem_values.reshape(mem_rows, features)], 1
    )

    def half_of(array, which):
        return jnp.concatenate(
            [
                lax.dynamic_slice_in_dim(array, which * prefix_half, prefix_half, 0),
                lax.dynamic_slice_in_dim(array, prefix_total + which * own_cells, own_cells, 0),
            ],
            0,
        )

    theirs = pair_swap(half_of(d_memory, 1 - s_index).astype(LOW), 5)
    mine_low = (half_of(d_memory, s_index) + theirs.astype(jnp.float32)).astype(LOW)
    memory_own = half_of(memory, s_index)
    grad_ck = t_dot(memory_own, mine_low[:, :features]).astype(LOW)
    grad_cv = t_dot(memory_own, mine_low[:, features:]).astype(LOW)
    d_mem_rows = dot_t(mine_low[:, :features], ck_w) + dot_t(mine_low[:, features:], cv_w)
    prefix_back = d_mem_rows[:prefix_half]
    d_third = d_mem_rows[prefix_half:].astype(LOW)

    self_grad_low = d_after_self.astype(LOW)
    grad_sout = t_dot(self_low, self_grad_low).astype(LOW)
    d_self = heads_of(dot_t(self_grad_low, sout_w).astype(LOW))
    d_query, d_all_keys, d_all_values = run_back(
        queries, all_keys, all_values, self_allow, score_scale, d_self, self_total
    )
    back_keys, back_values = passed_along(
        (d_all_keys[:row_count].astype(LOW), d_all_values[:row_count].astype(LOW)), "seq", -1
    )
    own_dkeys = d_all_keys[row_count:] + back_keys.astype(jnp.float32)
    own_dvalues = d_all_values[row_count:] + back_values.astype(jnp.float32)
    d_qkv = [g.reshape(row_count, features).astype(LOW) for g in (d_query, own_dkeys, own_dvalues)]
    grads_qkv = [t_dot(low_one, g).astype(LOW) for g in d_qkv]
    unused_one, norm_back_one = jax.vjp(layer_norm, inputs, norms[6], norms[7])
    d_normed_one = dot_t(d_qkv[0], qkv_w[0]) + dot_t(d_qkv[1], qkv_w[1]) + dot_t(d_qkv[2], qkv_w[2])
    d_one, grad_gain_one, grad_bias_one = norm_back_one(d_normed_one)
    d_inputs = d_after_self + d_one
    late_sums.append(
        lax.psum_scatter(
            jnp.stack([grad_cout, grad_cq, grad_ck, grad_cv, grad_sout] + grads_qkv),
            "dp",
            scatter_dimension=1,
            tiled=True,
        )
    )

    d_blocks = slots_to_devices(d_third.T.reshape(PORTIONS, 32, GROUP, own_cells))
    d_blocks = exchange_all(d_blocks.reshape(32, rows_own, own_cells), 6)
    d_y3 = d_blocks.transpose(1, 0, 2).reshape(rows_own, number).astype(jnp.float32)
    d_y3 = jnp.pad(d_y3, ((0, 0), (0, cells - number)))

    def back_through(layer, d_y, n, r, x_all, w, cid):
        dx, grad_w, sums = conv_block_back(layer, d_y, n, r, own_gb, masks, x_all, w.T, number)
        total = reduce_all(dx.reshape(PORTIONS, 32, GROUP, cells), cid)
        grad_w = grad_w.reshape(9, rows_own, features).transpose(1, 0, 2)
        grad_w = grad_w.reshape(rows_own, examples, -1).transpose(1, 0, 2)
        return d_y + total.reshape(rows_own, cells), grad_w, sums

    d_y2, grad_conv_one, sums3 = back_through(2, d_y3, n3, r3, x2_all, convs[1], 7)
    d_y1, grad_conv_zero, sums2 = back_through(1, d_y2, n2, r2, x1_all, convs[0], 8)
    grad_patch, sums1 = first_block_back(d_y1, n1, r1, own_gb, pixels, number)
    grad_patch = grad_patch.reshape(rows_own, examples, -1).transpose(1, 0, 2)
    patch_rows = grad_patch.shape[2]
    bn_grads = jnp.concatenate([sums1[:, :2], sums2[:, :2], sums3[:, :2]], 1).astype(LOW)
    ln_grads = jnp.stack(
        [
            grad_gain_one,
            grad_bias_one,
            grad_gain_two,
            grad_bias_two,
            grad_gain_three,
            grad_bias_three,
        ]
    ).astype(LOW)
    ln_count = ln_grads.shape[0]
    ln_blocks = ln_grads.reshape(ln_count, examples, -1).transpose(1, 0, 2)
    ln_blocks = jnp.pad(ln_blocks, ((0, 0), (0, rows_own - ln_count), (0, 0)))
    send_blocks = jnp.concatenate(
        [
            grad_conv_zero,
            grad_conv_one,
            grad_patch,
            jnp.broadcast_to(bn_grads, (examples,) + bn_grads.shape),
            ln_blocks,
        ],
        2,
    )
    got = swap_both(send_blocks, 9).transpose(1, 0, 2, 3).reshape(32, rows_own, -1)
    conv_rows = w_conv.shape[1]
    width = 2 * conv_rows + patch_rows
    mixed = devices_to_slots(got[:, :, : width + 6].reshape(32, PORTIONS, GROUP, width + 6))
    mixed = mixed.reshape(features, width + 6)
    stem_grads = mixed[:, :width].T.astype(jnp.float32)
    bn_part = lax.dynamic_slice_in_dim(mixed[:, width:], a_index * patch_rows, patch_rows, 0)
    ln_part = jnp.sum(got[:, :ln_count, width + 6 :].astype(jnp.float32), 0)
    norm_grads = jnp.concatenate([bn_part.T.astype(jnp.float32), ln_part], 0)

    sums = jnp.concatenate(late_sums, 0)
    sums = sums.astype(jnp.float32) + pair_swap(sums, 10).astype(jnp.float32)
    down_sum = sums[:4].reshape(w_down.shape)
    up_sum = jnp.concatenate([sums[4 + i] for i in range(4)], 1)
    return (
        result[None].astype(LOW),
        d_inputs[None].astype(LOW),
        prefix_back[None].astype(LOW),
        stem_grads[2 * conv_rows :],
        stem_grads[: 2 * conv_rows].reshape(w_conv.shape),
        jnp.concatenate([sums[13], sums[14], sums[15]], 1),
        sums[12],
        sums[9],
        jnp.concatenate([sums[10], sums[11]], 1),
        sums[8],
        up_sum,
        down_sum,
        norm_grads,
    )


def suits(mesh):
    return mesh.shape["dp"] == 16 and mesh.shape["seq"] == 2


def solution(mesh):
    return jax.shard_map(
        fast_device if suits(mesh) else general_device,
        mesh=mesh,
        in_specs=(
            P("dp", "seq", None),
            P("dp", "seq", None),
            P("dp", "seq", None),
            P("dp"),
            P("dp"),
            P("dp", "seq", None),
            P("dp", None),
            P(None, "dp", None),
            P("dp", None),
            P("dp", None),
            P("dp", None),
            P("dp", None),
            P("dp", None),
            P("dp", None),
            P("dp", None),
            P(None, "dp"),
        ),
        out_specs=(
            P("dp", "seq", None),
            P("dp", "seq", None),
            P("dp", "seq", None),
            P("dp", None),
            P(None, "dp", None),
            P("dp", None),
            P("dp", None),
            P("dp", None),
            P("dp", None),
            P("dp", None),
            P("dp", None),
            P("dp", None),
            P(None, "dp"),
        ),
        check_vma=False,
    )
```

```python
import functools

import jax
import jax.numpy as jnp
import numpy as np
from jax import lax
from jax.experimental import pallas as pl
from jax.experimental.pallas import tpu as pltpu
from jax.sharding import PartitionSpec as P

HEADS = 12
SIDE = 14
MESH = pl.DeviceIdType.MESH
LOW = jnp.bfloat16

STEPS = ((4, 3, 2, 0), (4, 0, 3, 2), (4, 2, 0, 3))
PORTIONS = 3
GROUP = 8


def my_bits():
    a = lax.axis_index("dp")
    return [
        lax.axis_index("seq"),
        lax.rem(a, 2),
        lax.rem(a // 2, 2),
        lax.rem(a // 4, 2),
        lax.rem(a // 8, 2),
    ]


def flipped(bits, which):
    return [1 - b if i == which else b for i, b in enumerate(bits)]


def place(bits):
    return (bits[1] + 2 * bits[2] + 4 * bits[3] + 8 * bits[4], bits[0])


def slot_of(bits, p):
    order = STEPS[p]
    return (
        bits[order[0]] + 2 * bits[order[1]] + 4 * bits[order[2]] + 8 * bits[order[3]] + 16 * bits[1]
    )


def device_of_slot(p):
    owners = np.zeros(32, np.int64)
    for e in range(32):
        bits = [(e >> i) & 1 for i in range(5)]
        owners[int(slot_of(bits, p))] = e
    return owners


def slots_to_devices(array):
    parts = []
    for p in range(PORTIONS):
        rest = array.shape[2:]
        names = [1, STEPS[p][3], STEPS[p][2], STEPS[p][1], STEPS[p][0]]
        cube = array[p].reshape((2,) * 5 + rest)
        perm = [names.index(bit) for bit in (4, 3, 2, 1, 0)]
        cube = cube.transpose(perm + [5 + i for i in range(len(rest))])
        parts.append(cube.reshape((32,) + rest))
    return jnp.stack(parts, 1)


def devices_to_slots(array):
    parts = []
    for p in range(PORTIONS):
        rest = array.shape[2:]
        names = [4, 3, 2, 1, 0]
        cube = array[:, p].reshape((2,) * 5 + rest)
        want = [1, STEPS[p][3], STEPS[p][2], STEPS[p][1], STEPS[p][0]]
        perm = [names.index(bit) for bit in want]
        cube = cube.transpose(perm + [5 + i for i in range(len(rest))])
        parts.append(cube.reshape((32,) + rest))
    return jnp.stack(parts, 0)


def greet(places):
    barrier = pltpu.get_barrier_semaphore()
    for where in places:
        pl.semaphore_signal(barrier, inc=1, device_id=where, device_id_type=MESH)
    pl.semaphore_wait(barrier, len(places))


def arrived(ref, sem):
    pltpu.make_async_remote_copy(
        src_ref=ref,
        dst_ref=ref,
        send_sem=sem,
        recv_sem=sem,
        device_id=(lax.axis_index("dp"), 1 - lax.axis_index("seq")),
        device_id_type=MESH,
    ).wait_recv()


def gather_body(x_ref, o_ref, send_sem, recv_sem, own_sem):
    bits = my_bits()
    greet([place(flipped(bits, b)) for b in range(5)])
    started = []

    def send(p, src, start, size, to_bit, k):
        copy = pltpu.make_async_remote_copy(
            src_ref=src,
            dst_ref=o_ref.at[p, pl.ds(start, size)],
            send_sem=send_sem.at[p, k],
            recv_sem=recv_sem.at[p, k],
            device_id=place(flipped(bits, to_bit)),
            device_id_type=MESH,
        )
        copy.start()
        started.append(copy)

    def await_run(p, start, size, k):
        run = o_ref.at[p, pl.ds(start, size)]
        arrived(run, recv_sem.at[p, k])

    slots = [slot_of(bits, p) for p in range(PORTIONS)]
    owns = []
    for p in range(PORTIONS):
        own = pltpu.make_async_copy(
            x_ref.at[pl.ds(p, 1)], o_ref.at[p, pl.ds(slots[p], 1)], own_sem.at[p]
        )
        own.start()
        owns.append(own)
    for p in range(PORTIONS):
        send(p, x_ref.at[pl.ds(p, 1)], slots[p], 1, STEPS[p][0], 0)
    for p in range(PORTIONS):
        send(p, x_ref.at[pl.ds(p, 1)], slots[p], 1, 1, 4)
    for own in owns:
        own.wait()
    fresh = [None] * PORTIONS
    for k in range(4):
        size = 2**k
        for p in range(PORTIONS):
            mine = (slots[p] // size) * size
            bit = bits[STEPS[p][k]]
            theirs = mine + size * (1 - 2 * bit)
            await_run(p, theirs, size, k)
            fresh[p] = theirs
            if k < 3:
                both = (slots[p] // (2 * size)) * (2 * size)
                send(p, o_ref.at[p, pl.ds(both, 2 * size)], both, 2 * size, STEPS[p][k + 1], k + 1)
        for p in range(PORTIONS):
            send(p, o_ref.at[p, pl.ds(fresh[p], size)], fresh[p], size, 1, 5 + k)
    for p in range(PORTIONS):
        other = 16 * (1 - 2 * bits[1])
        await_run(p, slots[p] + other, 1, 4)
        for k in range(4):
            size = 2**k
            mine = (slots[p] // size) * size
            theirs = mine + size * (1 - 2 * bits[STEPS[p][k]])
            await_run(p, theirs + other, size, 5 + k)
    for copy in started:
        copy.wait_send()


def gather_all(x, cid):
    return pl.pallas_call(
        gather_body,
        name="gather_all",
        out_shape=jax.ShapeDtypeStruct((PORTIONS, 32) + x.shape[1:], x.dtype),
        in_specs=[pl.BlockSpec(memory_space=pltpu.HBM)],
        out_specs=pl.BlockSpec(memory_space=pltpu.HBM),
        scratch_shapes=[
            pltpu.SemaphoreType.DMA((PORTIONS, 9)),
            pltpu.SemaphoreType.DMA((PORTIONS, 9)),
            pltpu.SemaphoreType.DMA((PORTIONS,)),
        ],
        compiler_params=pltpu.CompilerParams(collective_id=cid, has_side_effects=True),
    )(x)


def reduce_body(x_ref, o_ref, r0, r1, r2, r3, r4, send_sem, recv_sem):
    bits = my_bits()
    greet([place(flipped(bits, b)) for b in range(5)])
    started = []
    slots = [slot_of(bits, p) for p in range(PORTIONS)]
    bufs = (r0, r1, r2, r3, r4)

    def send(p, src, dst, bit, k):
        copy = pltpu.make_async_remote_copy(
            src_ref=src,
            dst_ref=dst,
            send_sem=send_sem.at[p, k],
            recv_sem=recv_sem.at[p, k],
            device_id=place(flipped(bits, bit)),
            device_id_type=MESH,
        )
        copy.start()
        started.append(copy)

    for p in range(PORTIONS):
        away = 16 * (1 - bits[1])
        send(p, x_ref.at[p, pl.ds(away, 16)], r0.at[p], 1, 0)
    for k in range(5):
        size = 16 >> k
        for p in range(PORTIONS):
            got = bufs[k].at[p]
            arrived(got, recv_sem.at[p, k])
            if k == 0:
                base, held = 16 * bits[1], x_ref
            else:
                bit = bits[STEPS[p][4 - k]]
                base, held = size * bit, bufs[k - 1]
            if k == 4:
                o_ref[p] = held[p, base].astype(jnp.float32) + bufs[k][p, 0].astype(jnp.float32)
                continue
            for j in range(size):
                total = held[p, base + j].astype(jnp.float32) + bufs[k][p, j].astype(jnp.float32)
                bufs[k][p, j] = total.astype(bufs[k].dtype)
            half = size // 2
            nbit = bits[STEPS[p][3 - k]]
            send(
                p,
                bufs[k].at[p, pl.ds(half * (1 - nbit), half)],
                bufs[k + 1].at[p],
                STEPS[p][3 - k],
                k + 1,
            )
    for copy in started:
        copy.wait_send()


def reduce_all(x, cid):
    rest = x.shape[2:]
    return pl.pallas_call(
        reduce_body,
        name="reduce_all",
        out_shape=jax.ShapeDtypeStruct((PORTIONS,) + rest, jnp.float32),
        in_specs=[pl.BlockSpec(memory_space=pltpu.VMEM)],
        out_specs=pl.BlockSpec(memory_space=pltpu.VMEM),
        scratch_shapes=[pltpu.VMEM((PORTIONS, 16 >> k) + rest, x.dtype) for k in range(5)]
        + [pltpu.SemaphoreType.DMA((PORTIONS, 5)), pltpu.SemaphoreType.DMA((PORTIONS, 5))],
        compiler_params=pltpu.CompilerParams(
            collective_id=cid, has_side_effects=True, vmem_limit_bytes=40 << 20
        ),
    )(x)


def swap_body(x_ref, o_ref, send_sem, recv_sem, own_sem):
    a, s = lax.axis_index("dp"), lax.axis_index("seq")
    count = x_ref.shape[0]
    greet([(lax.rem(a + j, count), s) for j in range(1, count)])
    own = pltpu.make_async_copy(x_ref.at[a], o_ref.at[a], own_sem)
    own.start()
    copies = []
    for j in range(1, count):
        to = lax.rem(a + j, count)
        copy = pltpu.make_async_remote_copy(
            src_ref=x_ref.at[to],
            dst_ref=o_ref.at[a],
            send_sem=send_sem.at[j],
            recv_sem=recv_sem.at[j],
            device_id=(to, s),
            device_id_type=MESH,
        )
        copy.start()
        copies.append(copy)
    for j in range(1, count):
        got = o_ref.at[lax.rem(a - j + count, count)]
        arrived(got, recv_sem.at[j])
    for copy in copies:
        copy.wait_send()
    own.wait()


def swap_dp(x, cid):
    count = x.shape[0]
    return pl.pallas_call(
        swap_body,
        name="swap_dp",
        out_shape=jax.ShapeDtypeStruct(x.shape, x.dtype),
        in_specs=[pl.BlockSpec(memory_space=pltpu.HBM)],
        out_specs=pl.BlockSpec(memory_space=pltpu.HBM),
        scratch_shapes=[
            pltpu.SemaphoreType.DMA((count,)),
            pltpu.SemaphoreType.DMA((count,)),
            pltpu.SemaphoreType.DMA,
        ],
        compiler_params=pltpu.CompilerParams(collective_id=cid, has_side_effects=True),
    )(x)


def swap_both_body(
    x_ref, half_ref, o_ref, both_ref, send_sem, recv_sem, pass_sem, got_sem, own_sem, half_sem
):
    a, s = lax.axis_index("dp"), lax.axis_index("seq")
    count = x_ref.shape[0]
    greet([(lax.rem(a + j, count), s) for j in range(1, count)] + [(a, 1 - s)])
    own = pltpu.make_async_copy(x_ref.at[a], o_ref.at[s, a], own_sem)
    own.start()
    own_half = pltpu.make_async_copy(half_ref, both_ref.at[s], half_sem.at[0])
    own_half.start()
    copies = []

    def pass_on(src, slot, j):
        copy = pltpu.make_async_remote_copy(
            src_ref=src,
            dst_ref=o_ref.at[s, slot],
            send_sem=pass_sem.at[j],
            recv_sem=got_sem.at[j],
            device_id=(a, 1 - s),
            device_id_type=MESH,
        )
        copy.start()
        copies.append(copy)

    pass_on(x_ref.at[a], a, 0)
    for j in range(1, count):
        to = lax.rem(a + j, count)
        copy = pltpu.make_async_remote_copy(
            src_ref=x_ref.at[to],
            dst_ref=o_ref.at[s, a],
            send_sem=send_sem.at[j],
            recv_sem=recv_sem.at[j],
            device_id=(to, s),
            device_id_type=MESH,
        )
        copy.start()
        copies.append(copy)
    half = pltpu.make_async_remote_copy(
        src_ref=half_ref,
        dst_ref=both_ref.at[s],
        send_sem=half_sem.at[1],
        recv_sem=half_sem.at[2],
        device_id=(a, 1 - s),
        device_id_type=MESH,
    )
    half.start()
    copies.append(half)
    for j in range(1, count):
        source = lax.rem(a - j + count, count)
        got = o_ref.at[s, source]
        arrived(got, recv_sem.at[j])
        pass_on(got, source, j)
    for j in range(count):
        got = o_ref.at[1 - s, lax.rem(a - j + count, count)]
        arrived(got, got_sem.at[j])
    arrived(both_ref.at[1 - s], half_sem.at[2])
    for copy in copies:
        copy.wait_send()
    own.wait()
    own_half.wait()


def swap_both(x, half, cid):
    count = x.shape[0]
    return pl.pallas_call(
        swap_both_body,
        name="swap_both",
        out_shape=(
            jax.ShapeDtypeStruct((2,) + x.shape, x.dtype),
            jax.ShapeDtypeStruct((2,) + half.shape, half.dtype),
        ),
        in_specs=[pl.BlockSpec(memory_space=pltpu.HBM)] * 2,
        out_specs=(pl.BlockSpec(memory_space=pltpu.HBM),) * 2,
        scratch_shapes=[pltpu.SemaphoreType.DMA((count,))] * 4
        + [pltpu.SemaphoreType.DMA, pltpu.SemaphoreType.DMA((3,))],
        compiler_params=pltpu.CompilerParams(collective_id=cid, has_side_effects=True),
    )(x, half)


def exchange_body(x_ref, o_ref, send_sem, recv_sem, own_sem):
    e = 2 * lax.axis_index("dp") + lax.axis_index("seq")
    count = x_ref.shape[0]

    def where(number):
        return (number // 2, lax.rem(number, 2))

    greet([where(lax.rem(e + j, count)) for j in range(1, count)])
    own = pltpu.make_async_copy(x_ref.at[e], o_ref.at[e], own_sem)
    own.start()
    copies = []
    for j in range(1, count):
        to = lax.rem(e + j, count)
        copy = pltpu.make_async_remote_copy(
            src_ref=x_ref.at[to],
            dst_ref=o_ref.at[e],
            send_sem=send_sem.at[j],
            recv_sem=recv_sem.at[j],
            device_id=where(to),
            device_id_type=MESH,
        )
        copy.start()
        copies.append(copy)
    for j in range(1, count):
        got = o_ref.at[lax.rem(e - j + count, count)]
        arrived(got, recv_sem.at[j])
    for copy in copies:
        copy.wait_send()
    own.wait()


def exchange_all(x, cid):
    count = x.shape[0]
    return pl.pallas_call(
        exchange_body,
        name="exchange_all",
        out_shape=jax.ShapeDtypeStruct(x.shape, x.dtype),
        in_specs=[pl.BlockSpec(memory_space=pltpu.HBM)],
        out_specs=pl.BlockSpec(memory_space=pltpu.HBM),
        scratch_shapes=[
            pltpu.SemaphoreType.DMA((count,)),
            pltpu.SemaphoreType.DMA((count,)),
            pltpu.SemaphoreType.DMA,
        ],
        compiler_params=pltpu.CompilerParams(collective_id=cid, has_side_effects=True),
    )(x)


def pair_body(x_ref, o_ref, send_sem, recv_sem):
    a, s = lax.axis_index("dp"), lax.axis_index("seq")
    greet([(a, 1 - s)])
    copy = pltpu.make_async_remote_copy(
        src_ref=x_ref,
        dst_ref=o_ref,
        send_sem=send_sem,
        recv_sem=recv_sem,
        device_id=(a, 1 - s),
        device_id_type=MESH,
    )
    copy.start()
    copy.wait()


def pair_swap(x, cid):
    return pl.pallas_call(
        pair_body,
        name="pair_swap",
        out_shape=jax.ShapeDtypeStruct(x.shape, x.dtype),
        in_specs=[pl.BlockSpec(memory_space=pltpu.HBM)],
        out_specs=pl.BlockSpec(memory_space=pltpu.HBM),
        scratch_shapes=[pltpu.SemaphoreType.DMA, pltpu.SemaphoreType.DMA],
        compiler_params=pltpu.CompilerParams(collective_id=cid, has_side_effects=True),
    )(x)


GELU_C = 0.7978845608028654
GELU_A = 0.044715


def gelu_of(x):
    return 0.5 * x * (1.0 + jnp.tanh(GELU_C * (x + GELU_A * (x * x * x))))


def gelu_slope(x):
    t = jnp.tanh(GELU_C * (x + GELU_A * (x * x * x)))
    return 0.5 * (1.0 + t) + 0.5 * x * (1.0 - t * t) * (GELU_C * (1.0 + 3.0 * GELU_A * (x * x)))


CHUNK = 640


def tap_masks(cells, examples):
    rows = examples * SIDE * SIDE
    at = np.arange(rows)
    i, j = (at // SIDE) % SIDE, at % SIDE
    out = np.zeros((16, cells), np.float32)
    for r in range(3):
        for c in range(3):
            ok = (i + r - 1 >= 0) & (i + r - 1 < SIDE) & (j + c - 1 >= 0) & (j + c - 1 < SIDE)
            out[3 * r + c, :rows] = ok
    out[9, :rows] = 1.0
    return out


def tap_shift(tap):
    return SIDE * (tap // 3 - 1) + tap % 3 - 1


def norm_act(values, valid, gain, bias, number):
    centre = jnp.sum(values, 1, keepdims=True) / number
    away = jnp.where(valid > 0, values - centre, 0.0)
    rstd = lax.rsqrt(jnp.sum(away * away, 1, keepdims=True) / number + 1e-05)
    normed = away * rstd
    return normed, rstd, gelu_of(normed * gain + bias)


def put_low(x_ref, y):
    for p in range(PORTIONS):
        x_ref[p] = y[GROUP * p : GROUP * (p + 1)].astype(x_ref.dtype)


def first_body(number, v_ref, gb_ref, m_ref, n_ref, rstd_ref, y_ref, x_ref):
    normed, rstd, act = norm_act(v_ref[...], m_ref[9:10, :], gb_ref[:, 0:1], gb_ref[:, 1:2], number)
    n_ref[...] = normed
    rstd_ref[...] = jnp.broadcast_to(rstd, rstd_ref.shape)
    y_ref[...] = act
    put_low(x_ref, act)


def conv_body(number, layer, x_in, w_ref, gb_ref, m_ref, y_in, n_ref, rstd_ref, y_ref, x_ref, z_ref):
    cells = x_in.shape[1]
    rows = y_in.shape[0]
    for start in range(0, cells, CHUNK):
        z_ref[:, start : start + CHUNK] = jnp.dot(
            w_ref[...], x_in[:, start : start + CHUNK], preferred_element_type=jnp.float32
        )
    total = jnp.zeros((rows, cells), jnp.float32)
    for tap in range(9):
        moved = z_ref[rows * tap : rows * (tap + 1), :]
        shift = (-tap_shift(tap)) % cells
        if shift:
            moved = pltpu.roll(moved, shift, 1)
        total = total + jnp.where(m_ref[tap : tap + 1, :] > 0, moved, 0.0)
    normed, rstd, act = norm_act(
        total,
        m_ref[9:10, :],
        gb_ref[:, 2 * layer : 2 * layer + 1],
        gb_ref[:, 2 * layer + 1 : 2 * layer + 2],
        number,
    )
    n_ref[...] = normed
    rstd_ref[...] = jnp.broadcast_to(rstd, rstd_ref.shape)
    y = y_in[...] + act
    y_ref[...] = y
    put_low(x_ref, y)


def norm_slope(number, dy, normed, rstd, gain, bias):
    e = dy * gelu_slope(normed * gain + bias)
    d_gain = jnp.sum(e * normed, 1, keepdims=True)
    d_bias = jnp.sum(e, 1, keepdims=True)
    dn = e * gain
    mean_dn = d_bias * gain / number
    mean_dnn = d_gain * gain / number
    return rstd * (dn - mean_dn - normed * mean_dnn), d_gain, d_bias


def conv_back_body(
    number, layer, dy_ref, n_ref, rstd_ref, gb_ref, m_ref, x_in, wt_ref, dx_ref, g_ref, s_ref, d_ref
):
    cells = x_in.shape[1]
    rows = dy_ref.shape[0]
    dv, d_gain, d_bias = norm_slope(
        number,
        dy_ref[...],
        n_ref[...],
        rstd_ref[:, 0:1],
        gb_ref[:, 2 * layer : 2 * layer + 1],
        gb_ref[:, 2 * layer + 1 : 2 * layer + 2],
    )
    lanes = lax.broadcasted_iota(jnp.int32, s_ref.shape, 1)
    s_ref[...] = jnp.where(lanes == 0, d_gain, d_bias)
    for tap in range(9):
        shift = tap_shift(tap) % cells
        moved = pltpu.roll(dv, shift, 1) if shift else dv
        moved = jnp.where(m_ref[8 - tap : 9 - tap, :] > 0, moved, 0.0)
        d_ref[rows * tap : rows * (tap + 1), :] = moved.astype(d_ref.dtype)
    for start in range(0, cells, CHUNK):
        dx_ref[:, start : start + CHUNK] = jnp.dot(
            wt_ref[...], d_ref[:, start : start + CHUNK], preferred_element_type=jnp.float32
        ).astype(dx_ref.dtype)
    for start in range(0, x_in.shape[0], 256):
        g_ref[:, start : start + 256] = lax.dot_general(
            d_ref[...],
            x_in[start : start + 256, :],
            (((1,), (1,)), ((), ())),
            preferred_element_type=jnp.float32,
        ).astype(g_ref.dtype)


def first_back_body(number, dy_ref, n_ref, rstd_ref, gb_ref, p_ref, g_ref, s_ref):
    dv, d_gain, d_bias = norm_slope(
        number, dy_ref[...], n_ref[...], rstd_ref[:, 0:1], gb_ref[:, 0:1], gb_ref[:, 1:2]
    )
    lanes = lax.broadcasted_iota(jnp.int32, s_ref.shape, 1)
    s_ref[...] = jnp.where(lanes == 0, d_gain, d_bias)
    g_ref[...] = jnp.dot(
        dv[:, : p_ref.shape[0]].astype(p_ref.dtype), p_ref[...], preferred_element_type=jnp.float32
    ).astype(g_ref.dtype)


BIG = pltpu.CompilerParams(vmem_limit_bytes=48 << 20)


def first_block(values, gb, masks, number):
    rows, cells = values.shape
    return pl.pallas_call(
        functools.partial(first_body, number),
        name="stem_first",
        out_shape=(
            jax.ShapeDtypeStruct((rows, cells), jnp.float32),
            jax.ShapeDtypeStruct((rows, 128), jnp.float32),
            jax.ShapeDtypeStruct((rows, cells), jnp.float32),
            jax.ShapeDtypeStruct((PORTIONS, GROUP, cells), LOW),
        ),
        compiler_params=BIG,
    )(values, gb, masks)


def conv_block(layer, x_all, w, gb, masks, y, number):
    rows, cells = y.shape
    return pl.pallas_call(
        functools.partial(conv_body, number, layer),
        name="stem_conv",
        out_shape=(
            jax.ShapeDtypeStruct((rows, cells), jnp.float32),
            jax.ShapeDtypeStruct((rows, 128), jnp.float32),
            jax.ShapeDtypeStruct((rows, cells), jnp.float32),
            jax.ShapeDtypeStruct((PORTIONS, GROUP, cells), LOW),
        ),
        scratch_shapes=[pltpu.VMEM((9 * rows, cells), jnp.float32)],
        compiler_params=BIG,
    )(x_all, w, gb, masks, y)


def conv_block_back(layer, dy, normed, rstd, gb, masks, x_all, w_t, number):
    rows, cells = dy.shape
    features = x_all.shape[0]
    return pl.pallas_call(
        functools.partial(conv_back_body, number, layer),
        name="stem_conv_back",
        out_shape=(
            jax.ShapeDtypeStruct((features, cells), LOW),
            jax.ShapeDtypeStruct((9 * rows, features), LOW),
            jax.ShapeDtypeStruct((rows, 128), jnp.float32),
        ),
        scratch_shapes=[pltpu.VMEM((9 * rows, cells), LOW)],
        compiler_params=BIG,
    )(dy, normed, rstd, gb, masks, x_all, w_t)


def first_block_back(dy, normed, rstd, gb, pixels, number):
    rows, cells = dy.shape
    return pl.pallas_call(
        functools.partial(first_back_body, number),
        name="stem_first_back",
        out_shape=(
            jax.ShapeDtypeStruct((rows, pixels.shape[1]), LOW),
            jax.ShapeDtypeStruct((rows, 128), jnp.float32),
        ),
        compiler_params=BIG,
    )(dy, normed, rstd, gb, pixels)


def padded_2(cells, sides, width):
    for axis, dim in sides:
        count = lax.axis_size(axis)
        ends = count - 1
        head = lax.slice_in_dim(cells, 0, width, axis=dim)
        tail = lax.slice_in_dim(cells, cells.shape[dim] - width, cells.shape[dim], axis=dim)
        cells = jnp.concatenate(
            [
                lax.ppermute(tail, axis, [(i, (i + 1) % count) for i in range(ends)]),
                cells,
                lax.ppermute(head, axis, [((i + 1) % count, i) for i in range(ends)]),
            ],
            axis=dim,
        )
    return cells


def passed_along(array, axis, by):
    length = lax.axis_size(axis)
    pairs = [(i, i + by) for i in range(length) if 0 <= i + by < length]
    return lax.ppermute(array, axis, pairs)


def layer_norm(activ, gain_vec, bias_vec):
    row_mean = jnp.mean(activ, -1, keepdims=True)
    centred = activ - row_mean
    spread = jnp.mean(centred * centred, -1, keepdims=True)
    return centred * lax.rsqrt(spread + 1e-06) * gain_vec + bias_vec


def heads_of(matrix):
    return matrix.reshape(matrix.shape[0], HEADS, -1)


def dot_float(left, right):
    return jnp.dot(left, right, preferred_element_type=jnp.float32)


def norm_batch(values, gain_vec, bias_vec, number):
    sums = lax.psum((jnp.sum(values, 0), jnp.sum(values * values, 0)), ("dp", "seq"))
    col_mean = sums[0] / number
    col_var = sums[1] / number - col_mean * col_mean
    inv_std = lax.rsqrt(col_var + 1e-05)
    normed = (values - col_mean) * inv_std
    return (normed, inv_std, normed * gain_vec + bias_vec)


def batch_back(d_pre, normed, inv_std, gain_vec, number):
    grad_gain = jnp.sum(d_pre * normed, 0)
    grad_bias = jnp.sum(d_pre, 0)
    d_normed = d_pre * gain_vec
    sums = lax.psum((jnp.sum(d_normed, 0), jnp.sum(d_normed * normed, 0)), ("dp", "seq"))
    d_values = inv_std * (d_normed - sums[0] / number - normed * (sums[1] / number))
    return (d_values, grad_gain, grad_bias)


def conv_fwd(flat_low, weight):
    features = flat_low.shape[1]
    grid_rows = flat_low.shape[0] // SIDE
    grid = flat_low.reshape(grid_rows, SIDE, features)
    padded = padded_2(grid, (("seq", 0),), 1)
    padded = jnp.pad(padded, ((0, 0), (1, 1), (0, 0)))
    total = jnp.zeros((grid_rows * SIDE, features), jnp.float32)
    for row_tap in range(3):
        for col_tap in range(3):
            tap = 3 * row_tap + col_tap
            window = padded[row_tap : row_tap + grid_rows, col_tap : col_tap + SIDE].reshape(
                -1, features
            )
            total = total + dot_float(window, weight[tap * features : (tap + 1) * features])
    return (total, padded)


def send_rim(rim_rows, offset):
    return passed_along(rim_rows.astype(jnp.bfloat16), "seq", offset).astype(rim_rows.dtype)


def conv_back(padded, d_out_low, weight):
    features = d_out_low.shape[1]
    grid_rows = padded.shape[0] - 2
    d_padded = jnp.zeros((grid_rows + 2, SIDE + 2, features), jnp.float32)
    tap_grads = []
    for row_tap in range(3):
        for col_tap in range(3):
            tap = 3 * row_tap + col_tap
            tap_weight = weight[tap * features : (tap + 1) * features]
            window = padded[row_tap : row_tap + grid_rows, col_tap : col_tap + SIDE].reshape(
                -1, features
            )
            tap_grads.append(dot_float(window.T, d_out_low))
            spread = dot_float(d_out_low, tap_weight.T).reshape(grid_rows, SIDE, features)
            d_padded = d_padded + jnp.pad(
                spread, ((row_tap, 2 - row_tap), (col_tap, 2 - col_tap), (0, 0))
            )
    inner = d_padded[1 : grid_rows + 1, 1 : SIDE + 1]
    from_below = send_rim(d_padded[0, 1 : SIDE + 1], -1)
    from_above = send_rim(d_padded[grid_rows + 1, 1 : SIDE + 1], 1)
    inner = inner.at[grid_rows - 1].add(from_below).at[0].add(from_above)
    return (jnp.concatenate(tap_grads, 0), inner.reshape(-1, features))


def attend_block(queries, key_rows, value_rows, allowed, score_scale):
    scores = (
        jnp.einsum("qhd,khd->hqk", queries, key_rows, preferred_element_type=jnp.float32)
        * score_scale
    )
    scores = jnp.where(allowed[None], scores, -1000000000.0)
    row_max = jnp.max(scores, -1, keepdims=True)
    exponent = jnp.exp(scores - row_max)
    row_total = jnp.sum(exponent, -1, keepdims=True)
    softmax = (exponent / row_total).astype(jnp.bfloat16)
    outputs = jnp.einsum("hqk,khd->qhd", softmax, value_rows, preferred_element_type=jnp.float32)
    return (outputs, row_max + jnp.log(row_total))


def attend_back(queries, key_rows, value_rows, allowed, score_scale, grad_out, log_total):
    scores = (
        jnp.einsum("qhd,khd->hqk", queries, key_rows, preferred_element_type=jnp.float32)
        * score_scale
    )
    scores = jnp.where(allowed[None], scores, -1000000000.0)
    softmax = jnp.exp(scores - log_total)
    d_softmax = jnp.einsum("qhd,khd->hqk", grad_out, value_rows, preferred_element_type=jnp.float32)
    row_delta = jnp.sum(softmax * d_softmax, -1, keepdims=True)
    d_scores = (softmax * (d_softmax - row_delta)).astype(jnp.bfloat16)
    d_query = (
        jnp.einsum("hqk,khd->qhd", d_scores, key_rows, preferred_element_type=jnp.float32)
        * score_scale
    )
    d_keys = (
        jnp.einsum("hqk,qhd->khd", d_scores, queries, preferred_element_type=jnp.float32)
        * score_scale
    )
    d_values = jnp.einsum(
        "hqk,qhd->khd", softmax.astype(jnp.bfloat16), grad_out, preferred_element_type=jnp.float32
    )
    return (d_query, d_keys, d_values)


def run_attention(queries, key_rows, value_rows, allow_fn, score_scale):
    row_count = queries.shape[0]
    block_rows = min(512, row_count)
    block_count = row_count // block_rows
    query_blocks = queries.reshape(block_count, block_rows, queries.shape[1], queries.shape[2])
    starts = jnp.arange(block_count, dtype=jnp.int32) * block_rows

    def one_block(block_pair):
        return attend_block(
            block_pair[0], key_rows, value_rows, allow_fn(block_pair[1], block_rows), score_scale
        )

    outputs, log_total = lax.map(one_block, (query_blocks, starts))
    return (outputs.reshape(queries.shape), log_total)


def run_back(queries, key_rows, value_rows, allow_fn, score_scale, grad_out, log_total):
    row_count = queries.shape[0]
    block_rows = min(512, row_count)
    block_count = row_count // block_rows
    query_blocks = queries.reshape(block_count, block_rows, queries.shape[1], queries.shape[2])
    grad_blocks = grad_out.reshape(query_blocks.shape)
    starts = jnp.arange(block_count, dtype=jnp.int32) * block_rows

    def one_block(running, block_items):
        query_part, grad_part, total_part, first_row = block_items
        d_query, d_keys, d_values = attend_back(
            query_part,
            key_rows,
            value_rows,
            allow_fn(first_row, block_rows),
            score_scale,
            grad_part,
            total_part,
        )
        return ((running[0] + d_keys, running[1] + d_values), d_query)

    zero_grads = jnp.zeros(key_rows.shape, jnp.float32)
    sums_kv, d_query = lax.scan(
        one_block, (zero_grads, zero_grads), (query_blocks, grad_blocks, log_total, starts)
    )
    return (d_query.reshape(queries.shape), sums_kv[0], sums_kv[1])


def general_device(
    captions,
    patches,
    prefix,
    prefix_count,
    caption_len,
    cotangent,
    w_patch,
    w_conv,
    w_self_qkv,
    w_self_out,
    w_cross_q,
    w_cross_kv,
    w_cross_out,
    w_up,
    w_down,
    norm_params,
):
    gathered = (
        lax.all_gather(w_patch, "dp", axis=0, tiled=True),
        lax.all_gather(w_conv, "dp", axis=1, tiled=True),
        lax.all_gather(w_self_qkv, "dp", axis=0, tiled=True),
        lax.all_gather(w_self_out, "dp", axis=0, tiled=True),
        lax.all_gather(w_cross_q, "dp", axis=0, tiled=True),
        lax.all_gather(w_cross_kv, "dp", axis=0, tiled=True),
        lax.all_gather(w_cross_out, "dp", axis=0, tiled=True),
        lax.all_gather(w_up, "dp", axis=0, tiled=True),
        lax.all_gather(w_down, "dp", axis=0, tiled=True),
        lax.all_gather(norm_params, "dp", axis=1, tiled=True),
    )
    (
        full_patch,
        full_conv,
        full_qkv,
        full_sout,
        full_cq,
        full_ckv,
        full_cout,
        full_up,
        full_down,
        full_norms,
    ) = gathered
    norms = full_norms.astype(jnp.float32)
    features = full_sout.shape[0]
    score_scale = (features // HEADS) ** (-0.5)
    seq_count = lax.axis_size("seq")
    seq_index = lax.axis_index("seq")
    pixels = patches[0]
    stem_out = dot_float(pixels, full_patch)
    number = stem_out.shape[0] * lax.axis_size("dp") * seq_count
    normed_one, inv_one, pre_one = norm_batch(stem_out, norms[0], norms[1], number)
    first_out = jax.nn.gelu(pre_one)
    first_low = first_out.astype(jnp.bfloat16)
    conv_two, padded_two = conv_fwd(first_low, full_conv[0])
    normed_two, inv_two, pre_two = norm_batch(conv_two, norms[2], norms[3], number)
    second_out = first_out + jax.nn.gelu(pre_two)
    second_low = second_out.astype(jnp.bfloat16)
    conv_three, padded_three = conv_fwd(second_low, full_conv[1])
    normed_three, inv_three, pre_three = norm_batch(conv_three, norms[4], norms[5], number)
    third_out = second_out + jax.nn.gelu(pre_three)
    patch_low = third_out.astype(jnp.bfloat16)
    prefix_low = prefix[0]
    kv_prefix = dot_float(prefix_low, full_ckv).astype(jnp.bfloat16)
    kv_patch = dot_float(patch_low, full_ckv).astype(jnp.bfloat16)
    all_prefix, all_patch = (
        lax.all_gather(kv_prefix, "seq", axis=0, tiled=True),
        lax.all_gather(kv_patch, "seq", axis=0, tiled=True),
    )
    memory_kv = jnp.concatenate([all_prefix, all_patch], 0)
    mem_rows = memory_kv.shape[0]
    prefix_total = all_prefix.shape[0]
    mem_keys = heads_of(memory_kv[:, :features])
    mem_values = heads_of(memory_kv[:, features:])
    slot_ids = jnp.arange(mem_rows, dtype=jnp.int32)
    mem_allowed = (slot_ids >= prefix_total) | (slot_ids < prefix_count[0])

    def cross_allow(first_row, block_rows):
        return jnp.broadcast_to(mem_allowed[None], (block_rows, mem_rows))

    inputs = captions[0].astype(jnp.float32)
    row_count = inputs.shape[0]
    low_one = layer_norm(inputs, norms[6], norms[7]).astype(jnp.bfloat16)
    qkv = dot_float(low_one, full_qkv).astype(jnp.bfloat16)
    queries = heads_of(qkv[:, :features])
    own_keys = heads_of(qkv[:, features : 2 * features])
    own_values = heads_of(qkv[:, 2 * features :])
    key_parts = [own_keys]
    value_parts = [own_values]
    position_parts = [seq_index * row_count + jnp.arange(row_count, dtype=jnp.int32)]
    offset = 1
    got_keys, got_values = passed_along((own_keys, own_values), "seq", offset)
    key_parts.insert(0, got_keys)
    value_parts.insert(0, got_values)
    position_parts.insert(
        0, (seq_index - offset) * row_count + jnp.arange(row_count, dtype=jnp.int32)
    )
    all_keys = jnp.concatenate(key_parts, 0)
    all_values = jnp.concatenate(value_parts, 0)
    key_pos = jnp.concatenate(position_parts, 0)
    length_one = caption_len[0]

    def self_allow(first_row, block_rows):
        query_pos = seq_index * row_count + first_row + jnp.arange(block_rows, dtype=jnp.int32)
        return (
            (key_pos[None] <= query_pos[:, None])
            & (key_pos[None] >= 0)
            & (key_pos[None] < length_one)
        )

    self_out, self_total = run_attention(queries, all_keys, all_values, self_allow, score_scale)
    self_low = self_out.reshape(row_count, features).astype(jnp.bfloat16)
    after_self = inputs + dot_float(self_low, full_sout)
    low_two = layer_norm(after_self, norms[8], norms[9]).astype(jnp.bfloat16)
    cross_flat = dot_float(low_two, full_cq).astype(jnp.bfloat16)
    cross_q = heads_of(cross_flat)
    cross_out, cross_total = run_attention(cross_q, mem_keys, mem_values, cross_allow, score_scale)
    cross_low = cross_out.reshape(row_count, features).astype(jnp.bfloat16)
    after_cross = after_self + dot_float(cross_low, full_cout)
    low_three = layer_norm(after_cross, norms[10], norms[11]).astype(jnp.bfloat16)
    up_proj = dot_float(low_three, full_up)
    hidden_low = jax.nn.gelu(up_proj).astype(jnp.bfloat16)
    result = after_cross + dot_float(hidden_low, full_down)
    back_weights = (
        lax.all_gather(w_patch, "dp", axis=0, tiled=True),
        lax.all_gather(w_conv, "dp", axis=1, tiled=True),
        lax.all_gather(w_self_qkv, "dp", axis=0, tiled=True),
        lax.all_gather(w_self_out, "dp", axis=0, tiled=True),
        lax.all_gather(w_cross_q, "dp", axis=0, tiled=True),
        lax.all_gather(w_cross_kv, "dp", axis=0, tiled=True),
        lax.all_gather(w_cross_out, "dp", axis=0, tiled=True),
        lax.all_gather(w_up, "dp", axis=0, tiled=True),
        lax.all_gather(w_down, "dp", axis=0, tiled=True),
        lax.all_gather(norm_params, "dp", axis=1, tiled=True),
    )
    (
        back_patch,
        back_conv,
        back_qkv,
        back_sout,
        back_cq,
        back_ckv,
        back_cout,
        back_up,
        back_down,
        back_norms,
    ) = back_weights
    bnorms = back_norms.astype(jnp.float32)
    out_grad = cotangent[0].astype(jnp.float32)
    grad_low = cotangent[0]
    grad_down = dot_float(hidden_low.T, grad_low)
    d_hidden = dot_float(grad_low, back_down.T)
    unused_gelu, gelu_back = jax.vjp(jax.nn.gelu, up_proj)
    d_upper = gelu_back(d_hidden)[0].astype(jnp.bfloat16)
    grad_up = dot_float(low_three.T, d_upper)
    unused_three, norm_back_three = jax.vjp(layer_norm, after_cross, bnorms[10], bnorms[11])
    d_three, grad_gain_three, grad_bias_three = norm_back_three(dot_float(d_upper, back_up.T))
    d_after_cross = out_grad + d_three
    cross_grad_low = d_after_cross.astype(jnp.bfloat16)
    grad_cout = dot_float(cross_low.T, cross_grad_low)
    d_cross = heads_of(dot_float(cross_grad_low, back_cout.T).astype(jnp.bfloat16))
    d_cross_q, d_mem_keys, d_mem_values = run_back(
        cross_q, mem_keys, mem_values, cross_allow, score_scale, d_cross, cross_total
    )
    d_cross_low = d_cross_q.reshape(row_count, features).astype(jnp.bfloat16)
    grad_cq = dot_float(low_two.T, d_cross_low)
    unused_two, norm_back_two = jax.vjp(layer_norm, after_self, bnorms[8], bnorms[9])
    d_two, grad_gain_two, grad_bias_two = norm_back_two(dot_float(d_cross_low, back_cq.T))
    d_after_self = d_after_cross + d_two
    d_memory = jnp.concatenate(
        [d_mem_keys.reshape(mem_rows, features), d_mem_values.reshape(mem_rows, features)], 1
    )
    mine_prefix, mine_patch = (
        lax.psum_scatter(
            d_memory[:prefix_total].astype(jnp.bfloat16), "seq", scatter_dimension=0, tiled=True
        ).astype(jnp.float32),
        lax.psum_scatter(
            d_memory[prefix_total:].astype(jnp.bfloat16), "seq", scatter_dimension=0, tiled=True
        ).astype(jnp.float32),
    )
    mine_prefix_low = mine_prefix.astype(jnp.bfloat16)
    mine_patch_low = mine_patch.astype(jnp.bfloat16)
    grad_ckv = dot_float(prefix_low.T, mine_prefix_low) + dot_float(patch_low.T, mine_patch_low)
    prefix_back = dot_float(mine_prefix_low, back_ckv.T)
    d_third = dot_float(mine_patch_low, back_ckv.T)
    unused_act_three, act_back_three = jax.vjp(jax.nn.gelu, pre_three)
    d_conv_three, grad_gain_bn3, grad_bias_bn3 = batch_back(
        act_back_three(d_third)[0], normed_three, inv_three, bnorms[4], number
    )
    grad_conv_one, d_second_in = conv_back(
        padded_three, d_conv_three.astype(jnp.bfloat16), back_conv[1]
    )
    d_second = d_third + d_second_in
    unused_act_two, act_back_two = jax.vjp(jax.nn.gelu, pre_two)
    d_conv_two, grad_gain_bn2, grad_bias_bn2 = batch_back(
        act_back_two(d_second)[0], normed_two, inv_two, bnorms[2], number
    )
    grad_conv_zero, d_first_in = conv_back(
        padded_two, d_conv_two.astype(jnp.bfloat16), back_conv[0]
    )
    d_first = d_second + d_first_in
    unused_act_one, act_back_one = jax.vjp(jax.nn.gelu, pre_one)
    d_stem, grad_gain_bn1, grad_bias_bn1 = batch_back(
        act_back_one(d_first)[0], normed_one, inv_one, bnorms[0], number
    )
    grad_patch = dot_float(pixels.T, d_stem.astype(jnp.bfloat16))
    grad_conv = jnp.stack([grad_conv_zero, grad_conv_one])
    self_grad_low = d_after_self.astype(jnp.bfloat16)
    grad_sout = dot_float(self_low.T, self_grad_low)
    d_self = heads_of(dot_float(self_grad_low, back_sout.T).astype(jnp.bfloat16))
    d_query, d_all_keys, d_all_values = run_back(
        queries, all_keys, all_values, self_allow, score_scale, d_self, self_total
    )
    own_start = (seq_count - 1) * row_count
    own_dkeys = d_all_keys[own_start:]
    own_dvalues = d_all_values[own_start:]
    offset = 1
    piece_start = (seq_count - 1 - offset) * row_count
    back_keys = passed_along(
        d_all_keys[piece_start : piece_start + row_count].astype(jnp.bfloat16), "seq", -offset
    ).astype(jnp.float32)
    back_values = passed_along(
        d_all_values[piece_start : piece_start + row_count].astype(jnp.bfloat16), "seq", -offset
    ).astype(jnp.float32)
    own_dkeys = own_dkeys + back_keys
    own_dvalues = own_dvalues + back_values
    d_qkv = jnp.concatenate(
        [
            d_query.reshape(row_count, features),
            own_dkeys.reshape(row_count, features),
            own_dvalues.reshape(row_count, features),
        ],
        1,
    ).astype(jnp.bfloat16)
    grad_qkv = dot_float(low_one.T, d_qkv)
    unused_one, norm_back_one = jax.vjp(layer_norm, inputs, bnorms[6], bnorms[7])
    d_one, grad_gain_one, grad_bias_one = norm_back_one(dot_float(d_qkv, back_qkv.T))
    d_inputs = d_after_self + d_one
    grad_norms = jnp.stack(
        [
            grad_gain_bn1,
            grad_bias_bn1,
            grad_gain_bn2,
            grad_bias_bn2,
            grad_gain_bn3,
            grad_bias_bn3,
            grad_gain_one,
            grad_bias_one,
            grad_gain_two,
            grad_bias_two,
            grad_gain_three,
            grad_bias_three,
        ]
    )
    shard_sums = (
        lax.psum_scatter(grad_patch, "dp", scatter_dimension=0, tiled=True),
        lax.psum_scatter(grad_conv, "dp", scatter_dimension=1, tiled=True),
        lax.psum_scatter(grad_qkv, "dp", scatter_dimension=0, tiled=True),
        lax.psum_scatter(grad_sout, "dp", scatter_dimension=0, tiled=True),
        lax.psum_scatter(grad_cq, "dp", scatter_dimension=0, tiled=True),
        lax.psum_scatter(grad_ckv, "dp", scatter_dimension=0, tiled=True),
        lax.psum_scatter(grad_cout, "dp", scatter_dimension=0, tiled=True),
        lax.psum_scatter(grad_up, "dp", scatter_dimension=0, tiled=True),
        lax.psum_scatter(grad_down, "dp", scatter_dimension=0, tiled=True),
        lax.psum_scatter(grad_norms, "dp", scatter_dimension=1, tiled=True),
    )
    totals = (
        lax.psum(shard_sums[0].astype(jnp.bfloat16), "seq").astype(jnp.float32),
        lax.psum(shard_sums[1].astype(jnp.bfloat16), "seq").astype(jnp.float32),
        lax.psum(shard_sums[2].astype(jnp.bfloat16), "seq").astype(jnp.float32),
        lax.psum(shard_sums[3].astype(jnp.bfloat16), "seq").astype(jnp.float32),
        lax.psum(shard_sums[4].astype(jnp.bfloat16), "seq").astype(jnp.float32),
        lax.psum(shard_sums[5].astype(jnp.bfloat16), "seq").astype(jnp.float32),
        lax.psum(shard_sums[6].astype(jnp.bfloat16), "seq").astype(jnp.float32),
        lax.psum(shard_sums[7].astype(jnp.bfloat16), "seq").astype(jnp.float32),
        lax.psum(shard_sums[8].astype(jnp.bfloat16), "seq").astype(jnp.float32),
        lax.psum(shard_sums[9].astype(jnp.bfloat16), "seq").astype(jnp.float32),
    )
    return (
        result[None].astype(jnp.bfloat16),
        d_inputs[None].astype(jnp.bfloat16),
        prefix_back[None].astype(jnp.bfloat16),
        totals[0],
        totals[1],
        totals[2],
        totals[3],
        totals[4],
        totals[5],
        totals[6],
        totals[7],
        totals[8],
        totals[9],
    )


PAIR = 128


def head_lanes(array, which, width):
    lanes = lax.broadcasted_iota(jnp.int32, array.shape, 1)
    return jnp.where((lanes >= which * width) & (lanes < (which + 1) * width), array, 0)


def scores_t(keys, q_head):
    return lax.dot_general(
        keys, q_head, (((1,), (1,)), ((), ())), preferred_element_type=jnp.float32
    )


def masked_scores(kind, info_ref, ok_ref, keys, q_head):
    if kind == "cross":
        scores = scores_t(keys, q_head)
        return jnp.where(ok_ref[:, 0:1] > 0, scores, -1e9)
    half = keys.shape[0] // 2
    before = scores_t(keys[:half], q_head)
    own = scores_t(keys[half:], q_head)
    before = jnp.where(info_ref[0] > 0, before, -1e9)
    key_at = lax.broadcasted_iota(jnp.int32, own.shape, 0)
    query_at = lax.broadcasted_iota(jnp.int32, own.shape, 1)
    own = jnp.where((key_at <= query_at) & (key_at < info_ref[1]), own, -1e9)
    return jnp.concatenate([before, own], 0)


def attend_body(kind, width, info_ref, ok_ref, q_ref, k_ref, v_ref, o_ref, lse_ref):
    keys, values = k_ref[...], v_ref[...]
    outs = []
    for which in range(PAIR // width):
        q_head = head_lanes(q_ref[...], which, width)
        scores = masked_scores(kind, info_ref, ok_ref, keys, q_head)
        top = jnp.max(scores, 0, keepdims=True)
        weights = jnp.exp(scores - top)
        total = jnp.sum(weights, 0, keepdims=True)
        lse_ref[0, which : which + 1, :] = top + jnp.log(total)
        out_t = lax.dot_general(
            head_lanes(values, which, width),
            weights.astype(LOW),
            (((0,), (0,)), ((), ())),
            preferred_element_type=jnp.float32,
        )
        outs.append(out_t / total)
    o_ref[...] = (outs[0] + outs[1]).T.astype(o_ref.dtype)


def attend_back_body(
    kind, width, scale, info_ref, ok_ref, q_ref, k_ref, v_ref, do_ref, lse_ref, dq_ref, dk_ref, dv_ref
):
    keys, values = k_ref[...], v_ref[...]
    dq_t, dk, dv = None, None, None
    for which in range(PAIR // width):
        q_head = head_lanes(q_ref[...], which, width)
        do_head = head_lanes(do_ref[...], which, width)
        scores = masked_scores(kind, info_ref, ok_ref, keys, q_head)
        probs = jnp.exp(scores - lse_ref[0, which : which + 1, :])
        d_probs = scores_t(values, do_head)
        delta = jnp.sum(probs * d_probs, 0, keepdims=True)
        ds = (probs * (d_probs - delta)).astype(LOW)
        part_k = jnp.dot(ds, q_head, preferred_element_type=jnp.float32)
        part_v = jnp.dot(probs.astype(LOW), do_head, preferred_element_type=jnp.float32)
        part_q = lax.dot_general(
            head_lanes(keys, which, width),
            ds,
            (((0,), (0,)), ((), ())),
            preferred_element_type=jnp.float32,
        )
        dk = part_k if dk is None else dk + part_k
        dv = part_v if dv is None else dv + part_v
        dq_t = part_q if dq_t is None else dq_t + part_q
    dq_ref[...] = (dq_t * scale).T.astype(dq_ref.dtype)
    dk_ref[...] = dk.astype(dk_ref.dtype)
    dv_ref[...] = dv.astype(dv_ref.dtype)


def attention_specs(rows, keys, ok):
    return [
        pl.BlockSpec(memory_space=pltpu.SMEM),
        pl.BlockSpec(ok.shape, lambda i: (0, 0)),
        pl.BlockSpec((rows, PAIR), lambda i: (0, i)),
        pl.BlockSpec((keys, PAIR), lambda i: (0, i)),
        pl.BlockSpec((keys, PAIR), lambda i: (0, i)),
    ]


def attend(kind, info, ok, q, k, v):
    rows, features = q.shape
    keys = k.shape[0]
    width = features // HEADS
    pairs = features // PAIR
    return pl.pallas_call(
        functools.partial(attend_body, kind, width),
        name=kind + "_attend",
        grid=(pairs,),
        in_specs=attention_specs(rows, keys, ok),
        out_specs=(
            pl.BlockSpec((rows, PAIR), lambda i: (0, i)),
            pl.BlockSpec((1, 8, rows), lambda i: (i, 0, 0)),
        ),
        out_shape=(
            jax.ShapeDtypeStruct((rows, features), LOW),
            jax.ShapeDtypeStruct((pairs, 8, rows), jnp.float32),
        ),
        compiler_params=BIG,
        cost_estimate=pl.CostEstimate(
            flops=4 * rows * keys * features, bytes_accessed=2 * (2 * rows + 2 * keys) * features,
            transcendentals=rows * keys * HEADS,
        ),
    )(info, ok, q, k, v)


def attend_grads(kind, info, ok, q, k, v, d_out, lse, scale):
    rows, features = q.shape
    keys = k.shape[0]
    width = features // HEADS
    pairs = features // PAIR
    return pl.pallas_call(
        functools.partial(attend_back_body, kind, width, scale),
        name=kind + "_attend_back",
        grid=(pairs,),
        in_specs=attention_specs(rows, keys, ok)
        + [
            pl.BlockSpec((rows, PAIR), lambda i: (0, i)),
            pl.BlockSpec((1, 8, rows), lambda i: (i, 0, 0)),
        ],
        out_specs=(
            pl.BlockSpec((rows, PAIR), lambda i: (0, i)),
            pl.BlockSpec((keys, PAIR), lambda i: (0, i)),
            pl.BlockSpec((keys, PAIR), lambda i: (0, i)),
        ),
        out_shape=(
            jax.ShapeDtypeStruct((rows, features), LOW),
            jax.ShapeDtypeStruct((keys, features), jnp.float32),
            jax.ShapeDtypeStruct((keys, features), jnp.float32),
        ),
        compiler_params=BIG,
        cost_estimate=pl.CostEstimate(
            flops=10 * rows * keys * features, bytes_accessed=2 * (3 * rows + 6 * keys) * features,
            transcendentals=rows * keys * HEADS,
        ),
    )(info, ok, q, k, v, d_out, lse)


def low_dot(left, right):
    return dot_float(left, right).astype(LOW)


def dot_t(left, right):
    return lax.dot_general(left, right, (((1,), (1,)), ((), ())), preferred_element_type=jnp.float32)


def t_dot(left, right):
    return lax.dot_general(left, right, (((0,), (0,)), ((), ())), preferred_element_type=jnp.float32)


def stem_weights(w_conv, norm_params, s):
    depth, conv_rows, features = w_conv.shape
    flat = w_conv.reshape(-1, features).T
    blocks = slots_to_devices(flat.reshape(PORTIONS, 32, GROUP, flat.shape[1]))
    blocks = blocks.reshape(16, 2, PORTIONS * GROUP, flat.shape[1])
    blocks = lax.dynamic_index_in_dim(blocks, s, 1, keepdims=False)
    rows = PORTIONS * GROUP
    extra = jnp.pad(norm_params, ((0, rows - norm_params.shape[0]), (0, 0)))
    blocks = jnp.concatenate([blocks, jnp.broadcast_to(extra, (16,) + extra.shape)], 2)
    got = swap_dp(blocks, 0)
    convs = []
    for layer in range(depth):
        part = got[:, :, layer * conv_rows : (layer + 1) * conv_rows]
        part = part.transpose(1, 0, 2).reshape(rows, 9, features).transpose(1, 0, 2)
        convs.append(part.reshape(9 * rows, features))
    norms = got[:, : norm_params.shape[0], depth * conv_rows :]
    return convs, norms.transpose(1, 0, 2).reshape(norm_params.shape[0], -1)


def own_columns(norms):
    bits = my_bits()
    cut = norms.reshape(norms.shape[0], PORTIONS, 32, GROUP)
    parts = [
        lax.dynamic_index_in_dim(cut[:, p], slot_of(bits, p), 1, keepdims=False)
        for p in range(PORTIONS)
    ]
    mine = jnp.concatenate(parts, 1).T
    return jnp.pad(mine, ((0, 0), (0, 128 - mine.shape[1])))


def fast_device(
    captions,
    patches,
    prefix,
    prefix_count,
    caption_len,
    cotangent,
    w_patch,
    w_conv,
    w_self_qkv,
    w_self_out,
    w_cross_q,
    w_cross_kv,
    w_cross_out,
    w_up,
    w_down,
    norm_params,
):
    a_index, s_index = lax.axis_index("dp"), lax.axis_index("seq")
    examples, halves = 16, 2
    features = w_self_out.shape[1]
    score_scale = (features // HEADS) ** (-0.5)

    def chunks(w):
        return [w[:, i * features : (i + 1) * features] for i in range(w.shape[1] // features)]

    first_w = lax.all_gather(
        jnp.stack([w_patch] + chunks(w_self_qkv)), "dp", axis=1, tiled=True
    )
    patch_w, qkv_w = first_w[0], first_w[1:]
    rest_w = lax.all_gather(
        jnp.stack([w_self_out, w_cross_q] + chunks(w_cross_kv) + [w_cross_out] + chunks(w_up)),
        "dp",
        axis=1,
        tiled=True,
    )
    down_w = lax.all_gather(w_down, "dp", axis=0, tiled=True)
    sout_w, cq_w, ck_w, cv_w, cout_w = (rest_w[i] for i in range(5))
    up_ws = [rest_w[5 + i] for i in range(4)]
    down_ws = [down_w[i * features : (i + 1) * features] for i in range(4)]

    convs, norms_low = stem_weights(w_conv, norm_params, s_index)
    norms = norms_low.astype(jnp.float32)
    own_gb = own_columns(norms[:6])
    own_cells = patches.shape[1]
    number = own_cells * examples * halves
    cells = -(-number // CHUNK) * CHUNK
    rows_own = PORTIONS * GROUP
    grid = halves * own_cells
    masks = jnp.asarray(tap_masks(cells, examples))
    late_patches = lax.optimization_barrier((patches[0], down_w))[0]
    pixels = lax.all_gather(late_patches, ("dp", "seq"), axis=0, tiled=True)

    def to_channels(rows_by_channel, cid):
        blocks = slots_to_devices(rows_by_channel.T.reshape(PORTIONS, 32, GROUP, own_cells))
        blocks = exchange_all(blocks.reshape(32, rows_own, own_cells), cid)
        blocks = blocks.transpose(1, 0, 2).reshape(rows_own, number)
        return jnp.pad(blocks, ((0, 0), (0, cells - number)))

    v1 = to_channels(dot_float(patches[0], patch_w), 1)
    n1, r1, y1, x1 = first_block(v1, own_gb, masks, number)
    x1_all = gather_all(x1, 2).reshape(features, cells)
    n2, r2, y2, x2 = conv_block(1, x1_all, convs[0], own_gb, masks, y1, number)
    x2_all = gather_all(x2, 3).reshape(features, cells)
    n3, r3, y3, x3 = conv_block(2, x2_all, convs[1], own_gb, masks, y2, number)
    out_blocks = x3.reshape(rows_own, cells)[:, :number].reshape(rows_own, examples, grid)
    out_blocks = jnp.broadcast_to(
        out_blocks.transpose(1, 0, 2)[:, None], (examples, halves, rows_own, grid)
    )
    in_blocks = exchange_all(out_blocks.reshape(32, rows_own, grid), 4)
    patch_all = devices_to_slots(in_blocks.reshape(32, PORTIONS, GROUP, grid))
    patch_all = patch_all.reshape(features, grid).T

    prefix_own = prefix[0]
    prefix_half = prefix_own.shape[0]
    prefix_other = lax.ppermute(prefix_own, "seq", [(0, 1), (1, 0)])
    first_half = s_index == 0
    prefix_all = jnp.concatenate(
        [
            jnp.where(first_half, prefix_own, prefix_other),
            jnp.where(first_half, prefix_other, prefix_own),
        ],
        0,
    )
    memory = jnp.concatenate([prefix_all, patch_all], 0)
    mem_rows = memory.shape[0]
    prefix_total = prefix_all.shape[0]
    mem_padded = jnp.pad(memory, ((0, -mem_rows % 128), (0, 0)))
    mem_keys = low_dot(mem_padded, ck_w)
    mem_values = low_dot(mem_padded, cv_w)
    slot_ids = jnp.arange(mem_padded.shape[0], dtype=jnp.int32)
    mem_ok = (slot_ids < mem_rows) & ((slot_ids >= prefix_total) | (slot_ids < prefix_count[0]))
    mem_ok = jnp.broadcast_to(mem_ok.astype(jnp.float32)[:, None], (mem_padded.shape[0], 128))

    inputs = captions[0].astype(jnp.float32)
    row_count = inputs.shape[0]
    low_one = layer_norm(inputs, norms[6], norms[7]).astype(LOW)
    queries = (dot_float(low_one, qkv_w[0]).astype(LOW) * score_scale).astype(LOW)
    own_keys, own_values = low_dot(low_one, qkv_w[1]), low_dot(low_one, qkv_w[2])
    got_keys, got_values = passed_along((own_keys, own_values), "seq", 1)
    all_keys = jnp.concatenate([got_keys, own_keys], 0)
    all_values = jnp.concatenate([got_values, own_values], 0)
    info = jnp.stack([s_index, caption_len[0] - s_index * row_count]).astype(jnp.int32)
    no_ok = jnp.zeros((8, 128), jnp.float32)
    self_low, self_lse = attend("self", info, no_ok, queries, all_keys, all_values)
    after_self = inputs + dot_float(self_low, sout_w)
    low_two = layer_norm(after_self, norms[8], norms[9]).astype(LOW)
    cross_q = (dot_float(low_two, cq_w).astype(LOW) * score_scale).astype(LOW)
    cross_low, cross_lse = attend("cross", info, mem_ok, cross_q, mem_keys, mem_values)
    after_cross = after_self + dot_float(cross_low, cout_w)
    low_three = layer_norm(after_cross, norms[10], norms[11]).astype(LOW)
    ups = [dot_float(low_three, w) for w in up_ws]
    hiddens = [jax.nn.gelu(u).astype(LOW) for u in ups]
    result = after_cross
    for h, w in zip(hiddens, down_ws):
        result = result + dot_float(h, w)

    out_grad = cotangent[0].astype(jnp.float32)
    grad_low = cotangent[0]
    grads_down = low_dot(jnp.concatenate(hiddens, 1).T, grad_low)
    d_uppers = []
    for u, w in zip(ups, down_ws):
        d_uppers.append((dot_t(grad_low, w) * gelu_slope(u)).astype(LOW))
    grads_up = [t_dot(low_three, d).astype(LOW) for d in d_uppers]
    d_normed = dot_t(d_uppers[0], up_ws[0])
    for d, w in zip(d_uppers[1:], up_ws[1:]):
        d_normed = d_normed + dot_t(d, w)
    unused_three, norm_back_three = jax.vjp(layer_norm, after_cross, norms[10], norms[11])
    d_three, grad_gain_three, grad_bias_three = norm_back_three(d_normed)
    down_parts = grads_down.reshape(examples, 4, -1, features).transpose(1, 0, 2, 3)
    down_parts = down_parts.reshape(4, features, features)
    late_sums = [
        lax.psum_scatter(
            jnp.concatenate([down_parts, jnp.stack(grads_up)], 0),
            ("dp", "seq"),
            scatter_dimension=1,
            tiled=True,
        )
    ]
    d_after_cross = out_grad + d_three
    cross_grad_low = d_after_cross.astype(LOW)
    grad_cout = t_dot(cross_low, cross_grad_low).astype(LOW)
    d_cross = dot_t(cross_grad_low, cout_w).astype(LOW)
    d_cross_low, d_mem_keys, d_mem_values = attend_grads(
        "cross", info, mem_ok, cross_q, mem_keys, mem_values, d_cross, cross_lse, score_scale
    )
    grad_cq = t_dot(low_two, d_cross_low).astype(LOW)
    unused_two, norm_back_two = jax.vjp(layer_norm, after_self, norms[8], norms[9])
    d_two, grad_gain_two, grad_bias_two = norm_back_two(dot_t(d_cross_low, cq_w))
    d_after_self = d_after_cross + d_two
    d_memory = jnp.concatenate([d_mem_keys, d_mem_values], 1)

    def half_of(array, which):
        return jnp.concatenate(
            [
                lax.dynamic_slice_in_dim(array, which * prefix_half, prefix_half, 0),
                lax.dynamic_slice_in_dim(array, prefix_total + which * own_cells, own_cells, 0),
            ],
            0,
        )

    theirs = pair_swap(half_of(d_memory, 1 - s_index).astype(LOW), 5)
    mine_low = (half_of(d_memory, s_index) + theirs.astype(jnp.float32)).astype(LOW)
    memory_own = half_of(memory, s_index)
    grad_ck = t_dot(memory_own, mine_low[:, :features]).astype(LOW)
    grad_cv = t_dot(memory_own, mine_low[:, features:]).astype(LOW)
    d_mem_rows = dot_t(mine_low[:, :features], ck_w) + dot_t(mine_low[:, features:], cv_w)
    prefix_back = d_mem_rows[:prefix_half]
    d_third = d_mem_rows[prefix_half:].astype(LOW)

    self_grad_low = d_after_self.astype(LOW)
    grad_sout = t_dot(self_low, self_grad_low).astype(LOW)
    d_self = dot_t(self_grad_low, sout_w).astype(LOW)
    d_query, d_all_keys, d_all_values = attend_grads(
        "self", info, no_ok, queries, all_keys, all_values, d_self, self_lse, score_scale
    )
    back_keys, back_values = passed_along(
        (d_all_keys[:row_count].astype(LOW), d_all_values[:row_count].astype(LOW)), "seq", -1
    )
    own_dkeys = d_all_keys[row_count:] + back_keys.astype(jnp.float32)
    own_dvalues = d_all_values[row_count:] + back_values.astype(jnp.float32)
    d_qkv = [g.astype(LOW) for g in (d_query, own_dkeys, own_dvalues)]
    grads_qkv = [t_dot(low_one, g).astype(LOW) for g in d_qkv]
    unused_one, norm_back_one = jax.vjp(layer_norm, inputs, norms[6], norms[7])
    d_normed_one = dot_t(d_qkv[0], qkv_w[0]) + dot_t(d_qkv[1], qkv_w[1]) + dot_t(d_qkv[2], qkv_w[2])
    d_one, grad_gain_one, grad_bias_one = norm_back_one(d_normed_one)
    d_inputs = d_after_self + d_one
    late_sums.append(
        lax.psum_scatter(
            jnp.stack([grad_cout, grad_cq, grad_ck, grad_cv, grad_sout] + grads_qkv),
            ("dp", "seq"),
            scatter_dimension=1,
            tiled=True,
        )
    )

    d_y3 = to_channels(d_third, 6).astype(jnp.float32)

    def back_through(layer, d_y, n, r, x_all, w, cid):
        dx, grad_w, sums = conv_block_back(layer, d_y, n, r, own_gb, masks, x_all, w.T, number)
        total = reduce_all(dx.reshape(PORTIONS, 32, GROUP, cells), cid)
        grad_w = grad_w.reshape(9, rows_own, features).transpose(1, 0, 2)
        grad_w = grad_w.reshape(rows_own, examples, -1).transpose(1, 0, 2)
        return d_y + total.reshape(rows_own, cells), grad_w, sums

    d_y2, grad_conv_one, sums3 = back_through(2, d_y3, n3, r3, x2_all, convs[1], 7)
    d_y1, grad_conv_zero, sums2 = back_through(1, d_y2, n2, r2, x1_all, convs[0], 8)
    grad_patch, sums1 = first_block_back(d_y1, n1, r1, own_gb, pixels, number)
    grad_patch = grad_patch.reshape(rows_own, examples, -1).transpose(1, 0, 2)
    patch_rows = grad_patch.shape[2]
    bn_grads = jnp.concatenate([sums1[:, :2], sums2[:, :2], sums3[:, :2]], 1).astype(LOW)
    ln_grads = jnp.stack(
        [
            grad_gain_one,
            grad_bias_one,
            grad_gain_two,
            grad_bias_two,
            grad_gain_three,
            grad_bias_three,
        ]
    ).astype(LOW)
    ln_count = ln_grads.shape[0]
    ln_blocks = ln_grads.reshape(ln_count, examples, -1).transpose(1, 0, 2)
    ln_blocks = jnp.pad(ln_blocks, ((0, 0), (0, rows_own - ln_count), (0, 0)))
    send_blocks = jnp.concatenate(
        [
            grad_conv_zero,
            grad_conv_one,
            grad_patch,
            jnp.broadcast_to(bn_grads, (examples,) + bn_grads.shape),
            ln_blocks,
        ],
        2,
    )
    sums = jnp.concatenate(late_sums, 0)
    got, sums_both = swap_both(send_blocks, sums, 9)
    got = got.transpose(1, 0, 2, 3).reshape(32, rows_own, -1)
    sums = sums_both.transpose(1, 0, 2, 3).reshape(sums.shape[0], -1, features).astype(jnp.float32)
    conv_rows = w_conv.shape[1]
    width = 2 * conv_rows + patch_rows
    mixed = devices_to_slots(got[:, :, : width + 6].reshape(32, PORTIONS, GROUP, width + 6))
    mixed = mixed.reshape(features, width + 6)
    stem_grads = mixed[:, :width].T.astype(jnp.float32)
    bn_part = lax.dynamic_slice_in_dim(mixed[:, width:], a_index * patch_rows, patch_rows, 0)
    ln_part = jnp.sum(got[:, :ln_count, width + 6 :].astype(jnp.float32), 0)
    norm_grads = jnp.concatenate([bn_part.T.astype(jnp.float32), ln_part], 0)

    down_sum = sums[:4].reshape(w_down.shape)
    up_sum = jnp.concatenate([sums[4 + i] for i in range(4)], 1)
    return (
        result[None].astype(LOW),
        d_inputs[None].astype(LOW),
        prefix_back[None].astype(LOW),
        stem_grads[2 * conv_rows :],
        stem_grads[: 2 * conv_rows].reshape(w_conv.shape),
        jnp.concatenate([sums[13], sums[14], sums[15]], 1),
        sums[12],
        sums[9],
        jnp.concatenate([sums[10], sums[11]], 1),
        sums[8],
        up_sum,
        down_sum,
        norm_grads,
    )


def suits(mesh):
    return mesh.shape["dp"] == 16 and mesh.shape["seq"] == 2


def solution(mesh):
    return jax.shard_map(
        fast_device if suits(mesh) else general_device,
        mesh=mesh,
        in_specs=(
            P("dp", "seq", None),
            P("dp", "seq", None),
            P("dp", "seq", None),
            P("dp"),
            P("dp"),
            P("dp", "seq", None),
            P("dp", None),
            P(None, "dp", None),
            P("dp", None),
            P("dp", None),
            P("dp", None),
            P("dp", None),
            P("dp", None),
            P("dp", None),
            P("dp", None),
            P(None, "dp"),
        ),
        out_specs=(
            P("dp", "seq", None),
            P("dp", "seq", None),
            P("dp", "seq", None),
            P("dp", None),
            P(None, "dp", None),
            P("dp", None),
            P("dp", None),
            P("dp", None),
            P("dp", None),
            P("dp", None),
            P("dp", None),
            P("dp", None),
            P(None, "dp"),
        ),
        check_vma=False,
    )
```

```python
import functools

import jax
import jax.numpy as jnp
import numpy as np
from jax import lax
from jax.experimental import pallas as pl
from jax.experimental.pallas import tpu as pltpu
from jax.sharding import PartitionSpec as P

HEADS = 12
SIDE = 14
MESH = pl.DeviceIdType.MESH
LOW = jnp.bfloat16

STEPS = ((4, 3, 2, 0), (4, 0, 3, 2), (4, 2, 0, 3))
PORTIONS = 3
GROUP = 8


def my_bits():
    a = lax.axis_index("dp")
    return [
        lax.axis_index("seq"),
        lax.rem(a, 2),
        lax.rem(a // 2, 2),
        lax.rem(a // 4, 2),
        lax.rem(a // 8, 2),
    ]


def flipped(bits, which):
    return [1 - b if i == which else b for i, b in enumerate(bits)]


def place(bits):
    return (bits[1] + 2 * bits[2] + 4 * bits[3] + 8 * bits[4], bits[0])


def slot_of(bits, p):
    order = STEPS[p]
    return (
        bits[order[0]] + 2 * bits[order[1]] + 4 * bits[order[2]] + 8 * bits[order[3]] + 16 * bits[1]
    )


def device_of_slot(p):
    owners = np.zeros(32, np.int64)
    for e in range(32):
        bits = [(e >> i) & 1 for i in range(5)]
        owners[int(slot_of(bits, p))] = e
    return owners


def slots_to_devices(array):
    parts = []
    for p in range(PORTIONS):
        rest = array.shape[2:]
        names = [1, STEPS[p][3], STEPS[p][2], STEPS[p][1], STEPS[p][0]]
        cube = array[p].reshape((2,) * 5 + rest)
        perm = [names.index(bit) for bit in (4, 3, 2, 1, 0)]
        cube = cube.transpose(perm + [5 + i for i in range(len(rest))])
        parts.append(cube.reshape((32,) + rest))
    return jnp.stack(parts, 1)


def devices_to_slots(array):
    parts = []
    for p in range(PORTIONS):
        rest = array.shape[2:]
        names = [4, 3, 2, 1, 0]
        cube = array[:, p].reshape((2,) * 5 + rest)
        want = [1, STEPS[p][3], STEPS[p][2], STEPS[p][1], STEPS[p][0]]
        perm = [names.index(bit) for bit in want]
        cube = cube.transpose(perm + [5 + i for i in range(len(rest))])
        parts.append(cube.reshape((32,) + rest))
    return jnp.stack(parts, 0)


def greet(places):
    barrier = pltpu.get_barrier_semaphore()
    for where in places:
        pl.semaphore_signal(barrier, inc=1, device_id=where, device_id_type=MESH)
    pl.semaphore_wait(barrier, len(places))


def arrived(ref, sem):
    pltpu.make_async_remote_copy(
        src_ref=ref,
        dst_ref=ref,
        send_sem=sem,
        recv_sem=sem,
        device_id=(lax.axis_index("dp"), 1 - lax.axis_index("seq")),
        device_id_type=MESH,
    ).wait_recv()


def with_mask(bits, mask):
    return [1 - b if (mask >> i) & 1 else b for i, b in enumerate(bits)]


def number_of(bits):
    return bits[0] + 2 * bits[1] + 4 * bits[2] + 8 * bits[3] + 16 * bits[4]


def stem_part(ref, bits, p):
    return ref.at[p, pl.ds(slot_of(bits, p), 1)]


def stem_own(ref, bits, p):
    return ref.at[pl.ds(p, 1)]


def rows_part(ref, bits, p):
    width = ref.shape[2] // PORTIONS
    return ref.at[number_of(bits), :, pl.ds(p * width, width)]


def rows_own(ref, bits, p):
    width = ref.shape[1] // PORTIONS
    return ref.at[:, pl.ds(p * width, width)]


KINDS = {
    "stem": (stem_own, stem_part),
    "rows": (rows_own, rows_part),
}


def gather_steps(kinds, swaps, pairs, refs):
    count = len(kinds)
    total = count + swaps + pairs
    ins, outs, sems = refs[:total], refs[total : 2 * total], refs[2 * total :]
    send_sem, recv_sem, own_sem, swap_send, swap_recv, pair_send, pair_recv = sems
    bits = my_bits()
    a, s = lax.axis_index("dp"), bits[0]
    dp = ins[count].shape[0] if swaps else 1
    partners = [place(flipped(bits, b)) for b in range(5)]
    partners += [(lax.rem(a + j, dp), s) for j in range(1, dp)]

    def own_of(i, p):
        return KINDS[kinds[i]][0](ins[i], bits, p)

    def part_of(i, p, mask):
        return KINDS[kinds[i]][1](outs[i], with_mask(bits, mask), p)

    def block(i, p, mask, bit):
        return pltpu.make_async_remote_copy(
            src_ref=own_of(i, p) if mask == 0 else part_of(i, p, mask),
            dst_ref=part_of(i, p, mask),
            send_sem=send_sem.at[i, p, mask ^ (1 << bit)],
            recv_sem=recv_sem.at[i, p, mask ^ (1 << bit)],
            device_id=place(flipped(bits, bit)),
            device_id_type=MESH,
        )

    def await_part(i, p, mask):
        arrived(part_of(i, p, mask), recv_sem.at[i, p, mask])

    def own_copy(i, p):
        return pltpu.make_async_copy(own_of(i, p), part_of(i, p, 0), own_sem.at[i, p])

    def swap_own():
        return pltpu.make_async_copy(ins[count].at[a], outs[count].at[a], swap_send.at[0])

    def swap_copy(j):
        to = lax.rem(a + j, dp)
        return pltpu.make_async_remote_copy(
            src_ref=ins[count].at[to],
            dst_ref=outs[count].at[a],
            send_sem=swap_send.at[j],
            recv_sem=swap_recv.at[j],
            device_id=(to, s),
            device_id_type=MESH,
        )

    def pair_copy(j):
        return pltpu.make_async_remote_copy(
            src_ref=ins[count + swaps + j],
            dst_ref=outs[count + swaps + j],
            send_sem=pair_send.at[j],
            recv_sem=pair_recv.at[j],
            device_id=(a, 1 - s),
            device_id_type=MESH,
        )

    every = [(i, p) for i in range(count) for p in range(PORTIONS)]
    held = {p: [0] for p in range(PORTIONS)}
    fresh = {p: [0] for p in range(PORTIONS)}
    sent = []
    steps = []
    for k in range(5):
        plan = []
        for i in range(count):
            for p in range(PORTIONS):
                waits = list(fresh[p]) if k else []
                links = [(mask, STEPS[p][k]) for mask in held[p]] if k < 4 else []
                plan.append((i, p, waits, links))
                sent += [(i, p, mask, bit) for mask, bit in links]
            for p in range(PORTIONS):
                cores = [(mask, 1) for mask in fresh[p]]
                plan.append((i, p, [], cores))
                sent += [(i, p, mask, bit) for mask, bit in cores]

        def run(k=k, plan=plan):
            if k == 0:
                greet(partners)
            for i, p, waits, sends in plan:
                for mask in waits:
                    await_part(i, p, mask)
                for mask, bit in sends:
                    block(i, p, mask, bit).start()
            if k == 0:
                for i, p in every:
                    own_copy(i, p).start()
                for j in range(pairs):
                    pair_copy(j).start()
                if swaps:
                    swap_own().start()
                for j in range(1, dp):
                    swap_copy(j).start()

        steps.append(run)
        if k < 4:
            for p in range(PORTIONS):
                fresh[p] = [mask ^ (1 << STEPS[p][k]) for mask in held[p]]
                held[p] = held[p] + fresh[p]

    def finish():
        for i, p in every:
            for mask in held[p]:
                await_part(i, p, mask ^ 2)
        for j in range(1, dp):
            arrived(outs[count].at[lax.rem(a - j + dp, dp)], swap_recv.at[j])
        for j in range(pairs):
            pair_copy(j).wait()
        for i, p, mask, bit in sent:
            block(i, p, mask, bit).wait_send()
        for j in range(1, dp):
            swap_copy(j).wait_send()
        for i, p in every:
            own_copy(i, p).wait()
        if swaps:
            swap_own().wait()

    steps.append(finish)
    return steps


def gather_body(kinds, swaps, pairs, *refs):
    for step in gather_steps(kinds, swaps, pairs, refs):
        step()


def gather_sems(count, pairs):
    return [
        pltpu.SemaphoreType.DMA((count, PORTIONS, 32)),
        pltpu.SemaphoreType.DMA((count, PORTIONS, 32)),
        pltpu.SemaphoreType.DMA((count, PORTIONS)),
        pltpu.SemaphoreType.DMA((16,)),
        pltpu.SemaphoreType.DMA((16,)),
        pltpu.SemaphoreType.DMA((max(pairs, 1),)),
        pltpu.SemaphoreType.DMA((max(pairs, 1),)),
    ]


def gather_many(stems, rows, swaps, pairs, cid):
    kinds = ["stem"] * len(stems) + ["rows"] * len(rows)
    arrays = list(stems) + list(rows) + list(swaps) + list(pairs)
    shapes = [jax.ShapeDtypeStruct((PORTIONS, 32) + x.shape[1:], x.dtype) for x in stems]
    shapes += [jax.ShapeDtypeStruct((32,) + x.shape, x.dtype) for x in rows]
    shapes += [jax.ShapeDtypeStruct(x.shape, x.dtype) for x in list(swaps) + list(pairs)]
    space = pl.BlockSpec(memory_space=pltpu.HBM)
    return pl.pallas_call(
        functools.partial(gather_body, tuple(kinds), len(swaps), len(pairs)),
        name="gather_many",
        out_shape=tuple(shapes),
        in_specs=[space] * len(arrays),
        out_specs=(space,) * len(arrays),
        scratch_shapes=gather_sems(len(kinds), len(pairs)),
        compiler_params=pltpu.CompilerParams(collective_id=cid, has_side_effects=True),
    )(*arrays)


def attend_gather_body(width, *refs):
    info_ref, ok_ref, q_ref, k_ref, v_ref, x_ref, o_ref, lse_ref, all_ref = refs[:9]
    steps = gather_steps(("stem",), 0, 0, (x_ref, all_ref) + refs[9:])
    for at, step in enumerate(steps[:-1]):

        @pl.when(pl.program_id(0) == at)
        def _():
            step()

    attend_body("self", width, info_ref, ok_ref, q_ref, k_ref, v_ref, o_ref, lse_ref)

    @pl.when(pl.program_id(0) == pl.num_programs(0) - 1)
    def _():
        steps[-1]()


def attend_gather(info, ok, q, k, v, x, cid):
    rows, features = q.shape
    keys = k.shape[0]
    width = features // HEADS
    pairs = features // PAIR
    return pl.pallas_call(
        functools.partial(attend_gather_body, width),
        name="attend_gather",
        grid=(pairs,),
        in_specs=attention_specs(rows, keys, ok) + [pl.BlockSpec(memory_space=pltpu.HBM)],
        out_specs=(
            pl.BlockSpec((rows, PAIR), lambda i: (0, i)),
            pl.BlockSpec((1, 8, rows), lambda i: (i, 0, 0)),
            pl.BlockSpec(memory_space=pltpu.HBM),
        ),
        out_shape=(
            jax.ShapeDtypeStruct((rows, features), LOW),
            jax.ShapeDtypeStruct((pairs, 8, rows), jnp.float32),
            jax.ShapeDtypeStruct((PORTIONS, 32) + x.shape[1:], x.dtype),
        ),
        scratch_shapes=gather_sems(1, 0),
        compiler_params=pltpu.CompilerParams(
            collective_id=cid, has_side_effects=True, vmem_limit_bytes=48 << 20
        ),
    )(info, ok, q, k, v, x)


def pack_body(pieces, *refs):
    ins, o_ref = refs[:-1], refs[-1]
    rows, cols = o_ref.shape[1:]
    for at, (which, row, col) in enumerate(pieces):
        o_ref[at] = ins[which][row : row + rows, col : col + cols]


def pack(pieces, arrays, rows, cols):
    return pl.pallas_call(
        functools.partial(pack_body, tuple(pieces)),
        name="pack",
        out_shape=jax.ShapeDtypeStruct((len(pieces), rows, cols), arrays[0].dtype),
    )(*arrays)


def reduce_body(x_ref, o_ref, r0, r1, r2, r3, r4, send_sem, recv_sem):
    bits = my_bits()
    greet([place(flipped(bits, b)) for b in range(5)])
    started = []
    slots = [slot_of(bits, p) for p in range(PORTIONS)]
    bufs = (r0, r1, r2, r3, r4)

    def send(p, src, dst, bit, k):
        copy = pltpu.make_async_remote_copy(
            src_ref=src,
            dst_ref=dst,
            send_sem=send_sem.at[p, k],
            recv_sem=recv_sem.at[p, k],
            device_id=place(flipped(bits, bit)),
            device_id_type=MESH,
        )
        copy.start()
        started.append(copy)

    for p in range(PORTIONS):
        away = 16 * (1 - bits[1])
        send(p, x_ref.at[p, pl.ds(away, 16)], r0.at[p], 1, 0)
    for k in range(5):
        size = 16 >> k
        for p in range(PORTIONS):
            got = bufs[k].at[p]
            arrived(got, recv_sem.at[p, k])
            if k == 0:
                base, held = 16 * bits[1], x_ref
            else:
                bit = bits[STEPS[p][4 - k]]
                base, held = size * bit, bufs[k - 1]
            if k == 4:
                o_ref[p] = held[p, base].astype(jnp.float32) + bufs[k][p, 0].astype(jnp.float32)
                continue
            for j in range(size):
                total = held[p, base + j].astype(jnp.float32) + bufs[k][p, j].astype(jnp.float32)
                bufs[k][p, j] = total.astype(bufs[k].dtype)
            half = size // 2
            nbit = bits[STEPS[p][3 - k]]
            send(
                p,
                bufs[k].at[p, pl.ds(half * (1 - nbit), half)],
                bufs[k + 1].at[p],
                STEPS[p][3 - k],
                k + 1,
            )
    for copy in started:
        copy.wait_send()


def reduce_all(x, cid):
    rest = x.shape[2:]
    return pl.pallas_call(
        reduce_body,
        name="reduce_all",
        out_shape=jax.ShapeDtypeStruct((PORTIONS,) + rest, jnp.float32),
        in_specs=[pl.BlockSpec(memory_space=pltpu.VMEM)],
        out_specs=pl.BlockSpec(memory_space=pltpu.VMEM),
        scratch_shapes=[pltpu.VMEM((PORTIONS, 16 >> k) + rest, x.dtype) for k in range(5)]
        + [pltpu.SemaphoreType.DMA((PORTIONS, 5)), pltpu.SemaphoreType.DMA((PORTIONS, 5))],
        compiler_params=pltpu.CompilerParams(
            collective_id=cid, has_side_effects=True, vmem_limit_bytes=40 << 20
        ),
    )(x)


def swap_both_body(x_ref, o_ref, send_sem, recv_sem, pass_sem, got_sem, own_sem):
    a, s = lax.axis_index("dp"), lax.axis_index("seq")
    count = x_ref.shape[0]
    greet([(lax.rem(a + j, count), s) for j in range(1, count)] + [(a, 1 - s)])
    own = pltpu.make_async_copy(x_ref.at[a], o_ref.at[s, a], own_sem)
    own.start()
    copies = []

    def pass_on(src, slot, j):
        copy = pltpu.make_async_remote_copy(
            src_ref=src,
            dst_ref=o_ref.at[s, slot],
            send_sem=pass_sem.at[j],
            recv_sem=got_sem.at[j],
            device_id=(a, 1 - s),
            device_id_type=MESH,
        )
        copy.start()
        copies.append(copy)

    pass_on(x_ref.at[a], a, 0)
    for j in range(1, count):
        to = lax.rem(a + j, count)
        copy = pltpu.make_async_remote_copy(
            src_ref=x_ref.at[to],
            dst_ref=o_ref.at[s, a],
            send_sem=send_sem.at[j],
            recv_sem=recv_sem.at[j],
            device_id=(to, s),
            device_id_type=MESH,
        )
        copy.start()
        copies.append(copy)
    for j in range(1, count):
        source = lax.rem(a - j + count, count)
        got = o_ref.at[s, source]
        arrived(got, recv_sem.at[j])
        pass_on(got, source, j)
    for j in range(count):
        got = o_ref.at[1 - s, lax.rem(a - j + count, count)]
        arrived(got, got_sem.at[j])
    for copy in copies:
        copy.wait_send()
    own.wait()


def swap_both(x, cid):
    count = x.shape[0]
    return pl.pallas_call(
        swap_both_body,
        name="swap_both",
        out_shape=jax.ShapeDtypeStruct((2,) + x.shape, x.dtype),
        in_specs=[pl.BlockSpec(memory_space=pltpu.HBM)],
        out_specs=pl.BlockSpec(memory_space=pltpu.HBM),
        scratch_shapes=[pltpu.SemaphoreType.DMA((count,))] * 4 + [pltpu.SemaphoreType.DMA],
        compiler_params=pltpu.CompilerParams(collective_id=cid, has_side_effects=True),
    )(x)


def exchange_body(x_ref, o_ref, send_sem, recv_sem, own_sem):
    e = 2 * lax.axis_index("dp") + lax.axis_index("seq")
    count = x_ref.shape[0]

    def where(number):
        return (number // 2, lax.rem(number, 2))

    greet([where(lax.rem(e + j, count)) for j in range(1, count)])
    own = pltpu.make_async_copy(x_ref.at[e], o_ref.at[e], own_sem)
    own.start()
    copies = []
    for j in range(1, count):
        to = lax.rem(e + j, count)
        copy = pltpu.make_async_remote_copy(
            src_ref=x_ref.at[to],
            dst_ref=o_ref.at[e],
            send_sem=send_sem.at[j],
            recv_sem=recv_sem.at[j],
            device_id=where(to),
            device_id_type=MESH,
        )
        copy.start()
        copies.append(copy)
    for j in range(1, count):
        got = o_ref.at[lax.rem(e - j + count, count)]
        arrived(got, recv_sem.at[j])
    for copy in copies:
        copy.wait_send()
    own.wait()


def exchange_all(x, cid):
    count = x.shape[0]
    return pl.pallas_call(
        exchange_body,
        name="exchange_all",
        out_shape=jax.ShapeDtypeStruct(x.shape, x.dtype),
        in_specs=[pl.BlockSpec(memory_space=pltpu.HBM)],
        out_specs=pl.BlockSpec(memory_space=pltpu.HBM),
        scratch_shapes=[
            pltpu.SemaphoreType.DMA((count,)),
            pltpu.SemaphoreType.DMA((count,)),
            pltpu.SemaphoreType.DMA,
        ],
        compiler_params=pltpu.CompilerParams(collective_id=cid, has_side_effects=True),
    )(x)


GELU_C = 0.7978845608028654
GELU_A = 0.044715


def gelu_of(x):
    return 0.5 * x * (1.0 + jnp.tanh(GELU_C * (x + GELU_A * (x * x * x))))


def gelu_slope(x):
    t = jnp.tanh(GELU_C * (x + GELU_A * (x * x * x)))
    return 0.5 * (1.0 + t) + 0.5 * x * (1.0 - t * t) * (GELU_C * (1.0 + 3.0 * GELU_A * (x * x)))


CHUNK = 640


def tap_masks(cells, examples):
    rows = examples * SIDE * SIDE
    at = np.arange(rows)
    i, j = (at // SIDE) % SIDE, at % SIDE
    out = np.zeros((16, cells), np.float32)
    for r in range(3):
        for c in range(3):
            ok = (i + r - 1 >= 0) & (i + r - 1 < SIDE) & (j + c - 1 >= 0) & (j + c - 1 < SIDE)
            out[3 * r + c, :rows] = ok
    out[9, :rows] = 1.0
    return out


def tap_shift(tap):
    return SIDE * (tap // 3 - 1) + tap % 3 - 1


def norm_act(values, valid, gain, bias, number):
    centre = jnp.sum(values, 1, keepdims=True) / number
    away = jnp.where(valid > 0, values - centre, 0.0)
    rstd = lax.rsqrt(jnp.sum(away * away, 1, keepdims=True) / number + 1e-05)
    normed = away * rstd
    return normed, rstd, gelu_of(normed * gain + bias)


def put_low(x_ref, y):
    for p in range(PORTIONS):
        x_ref[p] = y[GROUP * p : GROUP * (p + 1)].astype(x_ref.dtype)


def first_body(number, p_ref, w_ref, gb_ref, m_ref, n_ref, rstd_ref, y_ref, x_ref, v_ref):
    blocks, size = p_ref.shape[0], p_ref.shape[1]
    v_ref[:, blocks * size :] = jnp.zeros((v_ref.shape[0], v_ref.shape[1] - blocks * size), jnp.float32)
    for block in range(blocks):
        v_ref[:, block * size : (block + 1) * size] = lax.dot_general(
            w_ref[...], p_ref[block], (((1,), (1,)), ((), ())), preferred_element_type=jnp.float32
        )
    normed, rstd, act = norm_act(v_ref[...], m_ref[9:10, :], gb_ref[:, 0:1], gb_ref[:, 1:2], number)
    n_ref[...] = normed
    rstd_ref[...] = jnp.broadcast_to(rstd, rstd_ref.shape)
    y_ref[...] = act
    put_low(x_ref, act)


def conv_body(number, layer, x_in, w_ref, gb_ref, m_ref, y_in, n_ref, rstd_ref, y_ref, x_ref, z_ref):
    cells = x_in.shape[1]
    rows = y_in.shape[0]
    for start in range(0, cells, CHUNK):
        z_ref[:, start : start + CHUNK] = jnp.dot(
            w_ref[...], x_in[:, start : start + CHUNK], preferred_element_type=jnp.float32
        )
    total = jnp.zeros((rows, cells), jnp.float32)
    for tap in range(9):
        moved = z_ref[rows * tap : rows * (tap + 1), :]
        shift = (-tap_shift(tap)) % cells
        if shift:
            moved = pltpu.roll(moved, shift, 1)
        total = total + jnp.where(m_ref[tap : tap + 1, :] > 0, moved, 0.0)
    normed, rstd, act = norm_act(
        total,
        m_ref[9:10, :],
        gb_ref[:, 2 * layer : 2 * layer + 1],
        gb_ref[:, 2 * layer + 1 : 2 * layer + 2],
        number,
    )
    n_ref[...] = normed
    rstd_ref[...] = jnp.broadcast_to(rstd, rstd_ref.shape)
    y = y_in[...] + act
    y_ref[...] = y
    put_low(x_ref, y)


def norm_slope(number, dy, normed, rstd, gain, bias):
    e = dy * gelu_slope(normed * gain + bias)
    d_gain = jnp.sum(e * normed, 1, keepdims=True)
    d_bias = jnp.sum(e, 1, keepdims=True)
    dn = e * gain
    mean_dn = d_bias * gain / number
    mean_dnn = d_gain * gain / number
    return rstd * (dn - mean_dn - normed * mean_dnn), d_gain, d_bias


def conv_back_body(
    number, layer, dy_ref, n_ref, rstd_ref, gb_ref, m_ref, x_in, wt_ref, dx_ref, g_ref, s_ref, d_ref
):
    cells = x_in.shape[1]
    rows = dy_ref.shape[0]
    dv, d_gain, d_bias = norm_slope(
        number,
        dy_ref[...],
        n_ref[...],
        rstd_ref[:, 0:1],
        gb_ref[:, 2 * layer : 2 * layer + 1],
        gb_ref[:, 2 * layer + 1 : 2 * layer + 2],
    )
    lanes = lax.broadcasted_iota(jnp.int32, s_ref.shape, 1)
    s_ref[...] = jnp.where(lanes == 0, d_gain, d_bias)
    for tap in range(9):
        shift = tap_shift(tap) % cells
        moved = pltpu.roll(dv, shift, 1) if shift else dv
        moved = jnp.where(m_ref[8 - tap : 9 - tap, :] > 0, moved, 0.0)
        d_ref[rows * tap : rows * (tap + 1), :] = moved.astype(d_ref.dtype)
    for start in range(0, cells, CHUNK):
        dx_ref[:, start : start + CHUNK] = jnp.dot(
            wt_ref[...], d_ref[:, start : start + CHUNK], preferred_element_type=jnp.float32
        ).astype(dx_ref.dtype)
    for start in range(0, x_in.shape[0], 256):
        g_ref[:, start : start + 256] = lax.dot_general(
            d_ref[...],
            x_in[start : start + 256, :],
            (((1,), (1,)), ((), ())),
            preferred_element_type=jnp.float32,
        ).astype(g_ref.dtype)


def first_back_body(number, dy_ref, n_ref, rstd_ref, gb_ref, p_ref, g_ref, s_ref):
    dv, d_gain, d_bias = norm_slope(
        number, dy_ref[...], n_ref[...], rstd_ref[:, 0:1], gb_ref[:, 0:1], gb_ref[:, 1:2]
    )
    lanes = lax.broadcasted_iota(jnp.int32, s_ref.shape, 1)
    s_ref[...] = jnp.where(lanes == 0, d_gain, d_bias)
    blocks, size = p_ref.shape[0], p_ref.shape[1]
    total = jnp.zeros(g_ref.shape, jnp.float32)
    for block in range(blocks):
        shift = (-block * size) % dv.shape[1]
        piece = (pltpu.roll(dv, shift, 1) if shift else dv)[:, :size]
        total = total + jnp.dot(
            piece.astype(p_ref.dtype), p_ref[block], preferred_element_type=jnp.float32
        )
    g_ref[...] = total.astype(g_ref.dtype)


BIG = pltpu.CompilerParams(vmem_limit_bytes=48 << 20)


def first_block(pixels, w, gb, masks, number):
    rows, cells = w.shape[0], masks.shape[1]
    return pl.pallas_call(
        functools.partial(first_body, number),
        name="stem_first",
        out_shape=(
            jax.ShapeDtypeStruct((rows, cells), jnp.float32),
            jax.ShapeDtypeStruct((rows, 128), jnp.float32),
            jax.ShapeDtypeStruct((rows, cells), jnp.float32),
            jax.ShapeDtypeStruct((PORTIONS, GROUP, cells), LOW),
        ),
        scratch_shapes=[pltpu.VMEM((rows, cells), jnp.float32)],
        compiler_params=BIG,
    )(pixels, w, gb, masks)


def conv_block(layer, x_all, w, gb, masks, y, number):
    rows, cells = y.shape
    return pl.pallas_call(
        functools.partial(conv_body, number, layer),
        name="stem_conv",
        out_shape=(
            jax.ShapeDtypeStruct((rows, cells), jnp.float32),
            jax.ShapeDtypeStruct((rows, 128), jnp.float32),
            jax.ShapeDtypeStruct((rows, cells), jnp.float32),
            jax.ShapeDtypeStruct((PORTIONS, GROUP, cells), LOW),
        ),
        scratch_shapes=[pltpu.VMEM((9 * rows, cells), jnp.float32)],
        compiler_params=BIG,
    )(x_all, w, gb, masks, y)


def conv_block_back(layer, dy, normed, rstd, gb, masks, x_all, w_t, number):
    rows, cells = dy.shape
    features = x_all.shape[0]
    return pl.pallas_call(
        functools.partial(conv_back_body, number, layer),
        name="stem_conv_back",
        out_shape=(
            jax.ShapeDtypeStruct((features, cells), LOW),
            jax.ShapeDtypeStruct((9 * rows, features), LOW),
            jax.ShapeDtypeStruct((rows, 128), jnp.float32),
        ),
        scratch_shapes=[pltpu.VMEM((9 * rows, cells), LOW)],
        compiler_params=BIG,
    )(dy, normed, rstd, gb, masks, x_all, w_t)


def first_block_back(dy, normed, rstd, gb, pixels, number):
    rows, cells = dy.shape
    return pl.pallas_call(
        functools.partial(first_back_body, number),
        name="stem_first_back",
        out_shape=(
            jax.ShapeDtypeStruct((rows, pixels.shape[2]), LOW),
            jax.ShapeDtypeStruct((rows, 128), jnp.float32),
        ),
        compiler_params=BIG,
    )(dy, normed, rstd, gb, pixels)


def padded_2(cells, sides, width):
    for axis, dim in sides:
        count = lax.axis_size(axis)
        ends = count - 1
        head = lax.slice_in_dim(cells, 0, width, axis=dim)
        tail = lax.slice_in_dim(cells, cells.shape[dim] - width, cells.shape[dim], axis=dim)
        cells = jnp.concatenate(
            [
                lax.ppermute(tail, axis, [(i, (i + 1) % count) for i in range(ends)]),
                cells,
                lax.ppermute(head, axis, [((i + 1) % count, i) for i in range(ends)]),
            ],
            axis=dim,
        )
    return cells


def passed_along(array, axis, by):
    length = lax.axis_size(axis)
    pairs = [(i, i + by) for i in range(length) if 0 <= i + by < length]
    return lax.ppermute(array, axis, pairs)


def layer_norm(activ, gain_vec, bias_vec):
    row_mean = jnp.mean(activ, -1, keepdims=True)
    centred = activ - row_mean
    spread = jnp.mean(centred * centred, -1, keepdims=True)
    return centred * lax.rsqrt(spread + 1e-06) * gain_vec + bias_vec


def heads_of(matrix):
    return matrix.reshape(matrix.shape[0], HEADS, -1)


def dot_float(left, right):
    return jnp.dot(left, right, preferred_element_type=jnp.float32)


def norm_batch(values, gain_vec, bias_vec, number):
    sums = lax.psum((jnp.sum(values, 0), jnp.sum(values * values, 0)), ("dp", "seq"))
    col_mean = sums[0] / number
    col_var = sums[1] / number - col_mean * col_mean
    inv_std = lax.rsqrt(col_var + 1e-05)
    normed = (values - col_mean) * inv_std
    return (normed, inv_std, normed * gain_vec + bias_vec)


def batch_back(d_pre, normed, inv_std, gain_vec, number):
    grad_gain = jnp.sum(d_pre * normed, 0)
    grad_bias = jnp.sum(d_pre, 0)
    d_normed = d_pre * gain_vec
    sums = lax.psum((jnp.sum(d_normed, 0), jnp.sum(d_normed * normed, 0)), ("dp", "seq"))
    d_values = inv_std * (d_normed - sums[0] / number - normed * (sums[1] / number))
    return (d_values, grad_gain, grad_bias)


def conv_fwd(flat_low, weight):
    features = flat_low.shape[1]
    grid_rows = flat_low.shape[0] // SIDE
    grid = flat_low.reshape(grid_rows, SIDE, features)
    padded = padded_2(grid, (("seq", 0),), 1)
    padded = jnp.pad(padded, ((0, 0), (1, 1), (0, 0)))
    total = jnp.zeros((grid_rows * SIDE, features), jnp.float32)
    for row_tap in range(3):
        for col_tap in range(3):
            tap = 3 * row_tap + col_tap
            window = padded[row_tap : row_tap + grid_rows, col_tap : col_tap + SIDE].reshape(
                -1, features
            )
            total = total + dot_float(window, weight[tap * features : (tap + 1) * features])
    return (total, padded)


def send_rim(rim_rows, offset):
    return passed_along(rim_rows.astype(jnp.bfloat16), "seq", offset).astype(rim_rows.dtype)


def conv_back(padded, d_out_low, weight):
    features = d_out_low.shape[1]
    grid_rows = padded.shape[0] - 2
    d_padded = jnp.zeros((grid_rows + 2, SIDE + 2, features), jnp.float32)
    tap_grads = []
    for row_tap in range(3):
        for col_tap in range(3):
            tap = 3 * row_tap + col_tap
            tap_weight = weight[tap * features : (tap + 1) * features]
            window = padded[row_tap : row_tap + grid_rows, col_tap : col_tap + SIDE].reshape(
                -1, features
            )
            tap_grads.append(dot_float(window.T, d_out_low))
            spread = dot_float(d_out_low, tap_weight.T).reshape(grid_rows, SIDE, features)
            d_padded = d_padded + jnp.pad(
                spread, ((row_tap, 2 - row_tap), (col_tap, 2 - col_tap), (0, 0))
            )
    inner = d_padded[1 : grid_rows + 1, 1 : SIDE + 1]
    from_below = send_rim(d_padded[0, 1 : SIDE + 1], -1)
    from_above = send_rim(d_padded[grid_rows + 1, 1 : SIDE + 1], 1)
    inner = inner.at[grid_rows - 1].add(from_below).at[0].add(from_above)
    return (jnp.concatenate(tap_grads, 0), inner.reshape(-1, features))


def attend_block(queries, key_rows, value_rows, allowed, score_scale):
    scores = (
        jnp.einsum("qhd,khd->hqk", queries, key_rows, preferred_element_type=jnp.float32)
        * score_scale
    )
    scores = jnp.where(allowed[None], scores, -1000000000.0)
    row_max = jnp.max(scores, -1, keepdims=True)
    exponent = jnp.exp(scores - row_max)
    row_total = jnp.sum(exponent, -1, keepdims=True)
    softmax = (exponent / row_total).astype(jnp.bfloat16)
    outputs = jnp.einsum("hqk,khd->qhd", softmax, value_rows, preferred_element_type=jnp.float32)
    return (outputs, row_max + jnp.log(row_total))


def attend_back(queries, key_rows, value_rows, allowed, score_scale, grad_out, log_total):
    scores = (
        jnp.einsum("qhd,khd->hqk", queries, key_rows, preferred_element_type=jnp.float32)
        * score_scale
    )
    scores = jnp.where(allowed[None], scores, -1000000000.0)
    softmax = jnp.exp(scores - log_total)
    d_softmax = jnp.einsum("qhd,khd->hqk", grad_out, value_rows, preferred_element_type=jnp.float32)
    row_delta = jnp.sum(softmax * d_softmax, -1, keepdims=True)
    d_scores = (softmax * (d_softmax - row_delta)).astype(jnp.bfloat16)
    d_query = (
        jnp.einsum("hqk,khd->qhd", d_scores, key_rows, preferred_element_type=jnp.float32)
        * score_scale
    )
    d_keys = (
        jnp.einsum("hqk,qhd->khd", d_scores, queries, preferred_element_type=jnp.float32)
        * score_scale
    )
    d_values = jnp.einsum(
        "hqk,qhd->khd", softmax.astype(jnp.bfloat16), grad_out, preferred_element_type=jnp.float32
    )
    return (d_query, d_keys, d_values)


def run_attention(queries, key_rows, value_rows, allow_fn, score_scale):
    row_count = queries.shape[0]
    block_rows = min(512, row_count)
    block_count = row_count // block_rows
    query_blocks = queries.reshape(block_count, block_rows, queries.shape[1], queries.shape[2])
    starts = jnp.arange(block_count, dtype=jnp.int32) * block_rows

    def one_block(block_pair):
        return attend_block(
            block_pair[0], key_rows, value_rows, allow_fn(block_pair[1], block_rows), score_scale
        )

    outputs, log_total = lax.map(one_block, (query_blocks, starts))
    return (outputs.reshape(queries.shape), log_total)


def run_back(queries, key_rows, value_rows, allow_fn, score_scale, grad_out, log_total):
    row_count = queries.shape[0]
    block_rows = min(512, row_count)
    block_count = row_count // block_rows
    query_blocks = queries.reshape(block_count, block_rows, queries.shape[1], queries.shape[2])
    grad_blocks = grad_out.reshape(query_blocks.shape)
    starts = jnp.arange(block_count, dtype=jnp.int32) * block_rows

    def one_block(running, block_items):
        query_part, grad_part, total_part, first_row = block_items
        d_query, d_keys, d_values = attend_back(
            query_part,
            key_rows,
            value_rows,
            allow_fn(first_row, block_rows),
            score_scale,
            grad_part,
            total_part,
        )
        return ((running[0] + d_keys, running[1] + d_values), d_query)

    zero_grads = jnp.zeros(key_rows.shape, jnp.float32)
    sums_kv, d_query = lax.scan(
        one_block, (zero_grads, zero_grads), (query_blocks, grad_blocks, log_total, starts)
    )
    return (d_query.reshape(queries.shape), sums_kv[0], sums_kv[1])


def general_device(
    captions,
    patches,
    prefix,
    prefix_count,
    caption_len,
    cotangent,
    w_patch,
    w_conv,
    w_self_qkv,
    w_self_out,
    w_cross_q,
    w_cross_kv,
    w_cross_out,
    w_up,
    w_down,
    norm_params,
):
    gathered = (
        lax.all_gather(w_patch, "dp", axis=0, tiled=True),
        lax.all_gather(w_conv, "dp", axis=1, tiled=True),
        lax.all_gather(w_self_qkv, "dp", axis=0, tiled=True),
        lax.all_gather(w_self_out, "dp", axis=0, tiled=True),
        lax.all_gather(w_cross_q, "dp", axis=0, tiled=True),
        lax.all_gather(w_cross_kv, "dp", axis=0, tiled=True),
        lax.all_gather(w_cross_out, "dp", axis=0, tiled=True),
        lax.all_gather(w_up, "dp", axis=0, tiled=True),
        lax.all_gather(w_down, "dp", axis=0, tiled=True),
        lax.all_gather(norm_params, "dp", axis=1, tiled=True),
    )
    (
        full_patch,
        full_conv,
        full_qkv,
        full_sout,
        full_cq,
        full_ckv,
        full_cout,
        full_up,
        full_down,
        full_norms,
    ) = gathered
    norms = full_norms.astype(jnp.float32)
    features = full_sout.shape[0]
    score_scale = (features // HEADS) ** (-0.5)
    seq_count = lax.axis_size("seq")
    seq_index = lax.axis_index("seq")
    pixels = patches[0]
    stem_out = dot_float(pixels, full_patch)
    number = stem_out.shape[0] * lax.axis_size("dp") * seq_count
    normed_one, inv_one, pre_one = norm_batch(stem_out, norms[0], norms[1], number)
    first_out = jax.nn.gelu(pre_one)
    first_low = first_out.astype(jnp.bfloat16)
    conv_two, padded_two = conv_fwd(first_low, full_conv[0])
    normed_two, inv_two, pre_two = norm_batch(conv_two, norms[2], norms[3], number)
    second_out = first_out + jax.nn.gelu(pre_two)
    second_low = second_out.astype(jnp.bfloat16)
    conv_three, padded_three = conv_fwd(second_low, full_conv[1])
    normed_three, inv_three, pre_three = norm_batch(conv_three, norms[4], norms[5], number)
    third_out = second_out + jax.nn.gelu(pre_three)
    patch_low = third_out.astype(jnp.bfloat16)
    prefix_low = prefix[0]
    kv_prefix = dot_float(prefix_low, full_ckv).astype(jnp.bfloat16)
    kv_patch = dot_float(patch_low, full_ckv).astype(jnp.bfloat16)
    all_prefix, all_patch = (
        lax.all_gather(kv_prefix, "seq", axis=0, tiled=True),
        lax.all_gather(kv_patch, "seq", axis=0, tiled=True),
    )
    memory_kv = jnp.concatenate([all_prefix, all_patch], 0)
    mem_rows = memory_kv.shape[0]
    prefix_total = all_prefix.shape[0]
    mem_keys = heads_of(memory_kv[:, :features])
    mem_values = heads_of(memory_kv[:, features:])
    slot_ids = jnp.arange(mem_rows, dtype=jnp.int32)
    mem_allowed = (slot_ids >= prefix_total) | (slot_ids < prefix_count[0])

    def cross_allow(first_row, block_rows):
        return jnp.broadcast_to(mem_allowed[None], (block_rows, mem_rows))

    inputs = captions[0].astype(jnp.float32)
    row_count = inputs.shape[0]
    low_one = layer_norm(inputs, norms[6], norms[7]).astype(jnp.bfloat16)
    qkv = dot_float(low_one, full_qkv).astype(jnp.bfloat16)
    queries = heads_of(qkv[:, :features])
    own_keys = heads_of(qkv[:, features : 2 * features])
    own_values = heads_of(qkv[:, 2 * features :])
    key_parts = [own_keys]
    value_parts = [own_values]
    position_parts = [seq_index * row_count + jnp.arange(row_count, dtype=jnp.int32)]
    offset = 1
    got_keys, got_values = passed_along((own_keys, own_values), "seq", offset)
    key_parts.insert(0, got_keys)
    value_parts.insert(0, got_values)
    position_parts.insert(
        0, (seq_index - offset) * row_count + jnp.arange(row_count, dtype=jnp.int32)
    )
    all_keys = jnp.concatenate(key_parts, 0)
    all_values = jnp.concatenate(value_parts, 0)
    key_pos = jnp.concatenate(position_parts, 0)
    length_one = caption_len[0]

    def self_allow(first_row, block_rows):
        query_pos = seq_index * row_count + first_row + jnp.arange(block_rows, dtype=jnp.int32)
        return (
            (key_pos[None] <= query_pos[:, None])
            & (key_pos[None] >= 0)
            & (key_pos[None] < length_one)
        )

    self_out, self_total = run_attention(queries, all_keys, all_values, self_allow, score_scale)
    self_low = self_out.reshape(row_count, features).astype(jnp.bfloat16)
    after_self = inputs + dot_float(self_low, full_sout)
    low_two = layer_norm(after_self, norms[8], norms[9]).astype(jnp.bfloat16)
    cross_flat = dot_float(low_two, full_cq).astype(jnp.bfloat16)
    cross_q = heads_of(cross_flat)
    cross_out, cross_total = run_attention(cross_q, mem_keys, mem_values, cross_allow, score_scale)
    cross_low = cross_out.reshape(row_count, features).astype(jnp.bfloat16)
    after_cross = after_self + dot_float(cross_low, full_cout)
    low_three = layer_norm(after_cross, norms[10], norms[11]).astype(jnp.bfloat16)
    up_proj = dot_float(low_three, full_up)
    hidden_low = jax.nn.gelu(up_proj).astype(jnp.bfloat16)
    result = after_cross + dot_float(hidden_low, full_down)
    back_weights = (
        lax.all_gather(w_patch, "dp", axis=0, tiled=True),
        lax.all_gather(w_conv, "dp", axis=1, tiled=True),
        lax.all_gather(w_self_qkv, "dp", axis=0, tiled=True),
        lax.all_gather(w_self_out, "dp", axis=0, tiled=True),
        lax.all_gather(w_cross_q, "dp", axis=0, tiled=True),
        lax.all_gather(w_cross_kv, "dp", axis=0, tiled=True),
        lax.all_gather(w_cross_out, "dp", axis=0, tiled=True),
        lax.all_gather(w_up, "dp", axis=0, tiled=True),
        lax.all_gather(w_down, "dp", axis=0, tiled=True),
        lax.all_gather(norm_params, "dp", axis=1, tiled=True),
    )
    (
        back_patch,
        back_conv,
        back_qkv,
        back_sout,
        back_cq,
        back_ckv,
        back_cout,
        back_up,
        back_down,
        back_norms,
    ) = back_weights
    bnorms = back_norms.astype(jnp.float32)
    out_grad = cotangent[0].astype(jnp.float32)
    grad_low = cotangent[0]
    grad_down = dot_float(hidden_low.T, grad_low)
    d_hidden = dot_float(grad_low, back_down.T)
    unused_gelu, gelu_back = jax.vjp(jax.nn.gelu, up_proj)
    d_upper = gelu_back(d_hidden)[0].astype(jnp.bfloat16)
    grad_up = dot_float(low_three.T, d_upper)
    unused_three, norm_back_three = jax.vjp(layer_norm, after_cross, bnorms[10], bnorms[11])
    d_three, grad_gain_three, grad_bias_three = norm_back_three(dot_float(d_upper, back_up.T))
    d_after_cross = out_grad + d_three
    cross_grad_low = d_after_cross.astype(jnp.bfloat16)
    grad_cout = dot_float(cross_low.T, cross_grad_low)
    d_cross = heads_of(dot_float(cross_grad_low, back_cout.T).astype(jnp.bfloat16))
    d_cross_q, d_mem_keys, d_mem_values = run_back(
        cross_q, mem_keys, mem_values, cross_allow, score_scale, d_cross, cross_total
    )
    d_cross_low = d_cross_q.reshape(row_count, features).astype(jnp.bfloat16)
    grad_cq = dot_float(low_two.T, d_cross_low)
    unused_two, norm_back_two = jax.vjp(layer_norm, after_self, bnorms[8], bnorms[9])
    d_two, grad_gain_two, grad_bias_two = norm_back_two(dot_float(d_cross_low, back_cq.T))
    d_after_self = d_after_cross + d_two
    d_memory = jnp.concatenate(
        [d_mem_keys.reshape(mem_rows, features), d_mem_values.reshape(mem_rows, features)], 1
    )
    mine_prefix, mine_patch = (
        lax.psum_scatter(
            d_memory[:prefix_total].astype(jnp.bfloat16), "seq", scatter_dimension=0, tiled=True
        ).astype(jnp.float32),
        lax.psum_scatter(
            d_memory[prefix_total:].astype(jnp.bfloat16), "seq", scatter_dimension=0, tiled=True
        ).astype(jnp.float32),
    )
    mine_prefix_low = mine_prefix.astype(jnp.bfloat16)
    mine_patch_low = mine_patch.astype(jnp.bfloat16)
    grad_ckv = dot_float(prefix_low.T, mine_prefix_low) + dot_float(patch_low.T, mine_patch_low)
    prefix_back = dot_float(mine_prefix_low, back_ckv.T)
    d_third = dot_float(mine_patch_low, back_ckv.T)
    unused_act_three, act_back_three = jax.vjp(jax.nn.gelu, pre_three)
    d_conv_three, grad_gain_bn3, grad_bias_bn3 = batch_back(
        act_back_three(d_third)[0], normed_three, inv_three, bnorms[4], number
    )
    grad_conv_one, d_second_in = conv_back(
        padded_three, d_conv_three.astype(jnp.bfloat16), back_conv[1]
    )
    d_second = d_third + d_second_in
    unused_act_two, act_back_two = jax.vjp(jax.nn.gelu, pre_two)
    d_conv_two, grad_gain_bn2, grad_bias_bn2 = batch_back(
        act_back_two(d_second)[0], normed_two, inv_two, bnorms[2], number
    )
    grad_conv_zero, d_first_in = conv_back(
        padded_two, d_conv_two.astype(jnp.bfloat16), back_conv[0]
    )
    d_first = d_second + d_first_in
    unused_act_one, act_back_one = jax.vjp(jax.nn.gelu, pre_one)
    d_stem, grad_gain_bn1, grad_bias_bn1 = batch_back(
        act_back_one(d_first)[0], normed_one, inv_one, bnorms[0], number
    )
    grad_patch = dot_float(pixels.T, d_stem.astype(jnp.bfloat16))
    grad_conv = jnp.stack([grad_conv_zero, grad_conv_one])
    self_grad_low = d_after_self.astype(jnp.bfloat16)
    grad_sout = dot_float(self_low.T, self_grad_low)
    d_self = heads_of(dot_float(self_grad_low, back_sout.T).astype(jnp.bfloat16))
    d_query, d_all_keys, d_all_values = run_back(
        queries, all_keys, all_values, self_allow, score_scale, d_self, self_total
    )
    own_start = (seq_count - 1) * row_count
    own_dkeys = d_all_keys[own_start:]
    own_dvalues = d_all_values[own_start:]
    offset = 1
    piece_start = (seq_count - 1 - offset) * row_count
    back_keys = passed_along(
        d_all_keys[piece_start : piece_start + row_count].astype(jnp.bfloat16), "seq", -offset
    ).astype(jnp.float32)
    back_values = passed_along(
        d_all_values[piece_start : piece_start + row_count].astype(jnp.bfloat16), "seq", -offset
    ).astype(jnp.float32)
    own_dkeys = own_dkeys + back_keys
    own_dvalues = own_dvalues + back_values
    d_qkv = jnp.concatenate(
        [
            d_query.reshape(row_count, features),
            own_dkeys.reshape(row_count, features),
            own_dvalues.reshape(row_count, features),
        ],
        1,
    ).astype(jnp.bfloat16)
    grad_qkv = dot_float(low_one.T, d_qkv)
    unused_one, norm_back_one = jax.vjp(layer_norm, inputs, bnorms[6], bnorms[7])
    d_one, grad_gain_one, grad_bias_one = norm_back_one(dot_float(d_qkv, back_qkv.T))
    d_inputs = d_after_self + d_one
    grad_norms = jnp.stack(
        [
            grad_gain_bn1,
            grad_bias_bn1,
            grad_gain_bn2,
            grad_bias_bn2,
            grad_gain_bn3,
            grad_bias_bn3,
            grad_gain_one,
            grad_bias_one,
            grad_gain_two,
            grad_bias_two,
            grad_gain_three,
            grad_bias_three,
        ]
    )
    shard_sums = (
        lax.psum_scatter(grad_patch, "dp", scatter_dimension=0, tiled=True),
        lax.psum_scatter(grad_conv, "dp", scatter_dimension=1, tiled=True),
        lax.psum_scatter(grad_qkv, "dp", scatter_dimension=0, tiled=True),
        lax.psum_scatter(grad_sout, "dp", scatter_dimension=0, tiled=True),
        lax.psum_scatter(grad_cq, "dp", scatter_dimension=0, tiled=True),
        lax.psum_scatter(grad_ckv, "dp", scatter_dimension=0, tiled=True),
        lax.psum_scatter(grad_cout, "dp", scatter_dimension=0, tiled=True),
        lax.psum_scatter(grad_up, "dp", scatter_dimension=0, tiled=True),
        lax.psum_scatter(grad_down, "dp", scatter_dimension=0, tiled=True),
        lax.psum_scatter(grad_norms, "dp", scatter_dimension=1, tiled=True),
    )
    totals = (
        lax.psum(shard_sums[0].astype(jnp.bfloat16), "seq").astype(jnp.float32),
        lax.psum(shard_sums[1].astype(jnp.bfloat16), "seq").astype(jnp.float32),
        lax.psum(shard_sums[2].astype(jnp.bfloat16), "seq").astype(jnp.float32),
        lax.psum(shard_sums[3].astype(jnp.bfloat16), "seq").astype(jnp.float32),
        lax.psum(shard_sums[4].astype(jnp.bfloat16), "seq").astype(jnp.float32),
        lax.psum(shard_sums[5].astype(jnp.bfloat16), "seq").astype(jnp.float32),
        lax.psum(shard_sums[6].astype(jnp.bfloat16), "seq").astype(jnp.float32),
        lax.psum(shard_sums[7].astype(jnp.bfloat16), "seq").astype(jnp.float32),
        lax.psum(shard_sums[8].astype(jnp.bfloat16), "seq").astype(jnp.float32),
        lax.psum(shard_sums[9].astype(jnp.bfloat16), "seq").astype(jnp.float32),
    )
    return (
        result[None].astype(jnp.bfloat16),
        d_inputs[None].astype(jnp.bfloat16),
        prefix_back[None].astype(jnp.bfloat16),
        totals[0],
        totals[1],
        totals[2],
        totals[3],
        totals[4],
        totals[5],
        totals[6],
        totals[7],
        totals[8],
        totals[9],
    )


PAIR = 128


def head_lanes(array, which, width):
    lanes = lax.broadcasted_iota(jnp.int32, array.shape, 1)
    return jnp.where((lanes >= which * width) & (lanes < (which + 1) * width), array, 0)


def scores_t(keys, q_head):
    return lax.dot_general(
        keys, q_head, (((1,), (1,)), ((), ())), preferred_element_type=jnp.float32
    )


def masked_scores(kind, info_ref, ok_ref, keys, q_head):
    if kind == "cross":
        scores = scores_t(keys, q_head)
        return jnp.where(ok_ref[:, 0:1] > 0, scores, -1e9)
    half = keys.shape[0] // 2
    before = scores_t(keys[:half], q_head)
    own = scores_t(keys[half:], q_head)
    before = jnp.where(info_ref[0] > 0, before, -1e9)
    key_at = lax.broadcasted_iota(jnp.int32, own.shape, 0)
    query_at = lax.broadcasted_iota(jnp.int32, own.shape, 1)
    own = jnp.where((key_at <= query_at) & (key_at < info_ref[1]), own, -1e9)
    return jnp.concatenate([before, own], 0)


def attend_body(kind, width, info_ref, ok_ref, q_ref, k_ref, v_ref, o_ref, lse_ref):
    keys, values = k_ref[...], v_ref[...]
    outs = []
    for which in range(PAIR // width):
        q_head = head_lanes(q_ref[...], which, width)
        scores = masked_scores(kind, info_ref, ok_ref, keys, q_head)
        top = jnp.max(scores, 0, keepdims=True)
        weights = jnp.exp(scores - top)
        total = jnp.sum(weights, 0, keepdims=True)
        lse_ref[0, which : which + 1, :] = top + jnp.log(total)
        out_t = lax.dot_general(
            head_lanes(values, which, width),
            weights.astype(LOW),
            (((0,), (0,)), ((), ())),
            preferred_element_type=jnp.float32,
        )
        outs.append(out_t / total)
    o_ref[...] = (outs[0] + outs[1]).T.astype(o_ref.dtype)


def attend_back_body(
    kind, width, scale, info_ref, ok_ref, q_ref, k_ref, v_ref, do_ref, lse_ref, dq_ref, dk_ref, dv_ref
):
    keys, values = k_ref[...], v_ref[...]
    dq_t, dk, dv = None, None, None
    for which in range(PAIR // width):
        q_head = head_lanes(q_ref[...], which, width)
        do_head = head_lanes(do_ref[...], which, width)
        scores = masked_scores(kind, info_ref, ok_ref, keys, q_head)
        probs = jnp.exp(scores - lse_ref[0, which : which + 1, :])
        d_probs = scores_t(values, do_head)
        delta = jnp.sum(probs * d_probs, 0, keepdims=True)
        ds = (probs * (d_probs - delta)).astype(LOW)
        part_k = jnp.dot(ds, q_head, preferred_element_type=jnp.float32)
        part_v = jnp.dot(probs.astype(LOW), do_head, preferred_element_type=jnp.float32)
        part_q = lax.dot_general(
            head_lanes(keys, which, width),
            ds,
            (((0,), (0,)), ((), ())),
            preferred_element_type=jnp.float32,
        )
        dk = part_k if dk is None else dk + part_k
        dv = part_v if dv is None else dv + part_v
        dq_t = part_q if dq_t is None else dq_t + part_q
    dq_ref[...] = (dq_t * scale).T.astype(dq_ref.dtype)
    dk_ref[...] = dk.astype(dk_ref.dtype)
    dv_ref[...] = dv.astype(dv_ref.dtype)


def attention_specs(rows, keys, ok):
    return [
        pl.BlockSpec(memory_space=pltpu.SMEM),
        pl.BlockSpec(ok.shape, lambda i: (0, 0)),
        pl.BlockSpec((rows, PAIR), lambda i: (0, i)),
        pl.BlockSpec((keys, PAIR), lambda i: (0, i)),
        pl.BlockSpec((keys, PAIR), lambda i: (0, i)),
    ]


def attend(kind, info, ok, q, k, v):
    rows, features = q.shape
    keys = k.shape[0]
    width = features // HEADS
    pairs = features // PAIR
    return pl.pallas_call(
        functools.partial(attend_body, kind, width),
        name=kind + "_attend",
        grid=(pairs,),
        in_specs=attention_specs(rows, keys, ok),
        out_specs=(
            pl.BlockSpec((rows, PAIR), lambda i: (0, i)),
            pl.BlockSpec((1, 8, rows), lambda i: (i, 0, 0)),
        ),
        out_shape=(
            jax.ShapeDtypeStruct((rows, features), LOW),
            jax.ShapeDtypeStruct((pairs, 8, rows), jnp.float32),
        ),
        compiler_params=BIG,
        cost_estimate=pl.CostEstimate(
            flops=4 * rows * keys * features, bytes_accessed=2 * (2 * rows + 2 * keys) * features,
            transcendentals=rows * keys * HEADS,
        ),
    )(info, ok, q, k, v)


def attend_grads(kind, info, ok, q, k, v, d_out, lse, scale):
    rows, features = q.shape
    keys = k.shape[0]
    width = features // HEADS
    pairs = features // PAIR
    return pl.pallas_call(
        functools.partial(attend_back_body, kind, width, scale),
        name=kind + "_attend_back",
        grid=(pairs,),
        in_specs=attention_specs(rows, keys, ok)
        + [
            pl.BlockSpec((rows, PAIR), lambda i: (0, i)),
            pl.BlockSpec((1, 8, rows), lambda i: (i, 0, 0)),
        ],
        out_specs=(
            pl.BlockSpec((rows, PAIR), lambda i: (0, i)),
            pl.BlockSpec((keys, PAIR), lambda i: (0, i)),
            pl.BlockSpec((keys, PAIR), lambda i: (0, i)),
        ),
        out_shape=(
            jax.ShapeDtypeStruct((rows, features), LOW),
            jax.ShapeDtypeStruct((keys, features), LOW),
            jax.ShapeDtypeStruct((keys, features), LOW),
        ),
        compiler_params=BIG,
        cost_estimate=pl.CostEstimate(
            flops=10 * rows * keys * features, bytes_accessed=2 * (3 * rows + 6 * keys) * features,
            transcendentals=rows * keys * HEADS,
        ),
    )(info, ok, q, k, v, d_out, lse)


def weight_grads_body(jobs, targets, owners, *refs):
    count = len(refs) - 4
    ins, (o_ref, left_ref, right_ref, sum_ref) = refs[:count], refs[count:]
    step = pl.program_id(0)
    for at, (left, right, rows, row_at, left_col, right_col) in enumerate(jobs):

        @pl.when(step == at)
        def _():
            size = left_ref.shape[1]
            left_ref[:rows] = ins[left][row_at : row_at + rows, left_col : left_col + size]
            right_ref[:rows] = ins[right][row_at : row_at + rows, right_col : right_col + size]
            if rows < left_ref.shape[0]:
                left_ref[rows:] = jnp.zeros((left_ref.shape[0] - rows, size), left_ref.dtype)
                right_ref[rows:] = jnp.zeros((left_ref.shape[0] - rows, size), left_ref.dtype)

    product = lax.dot_general(
        left_ref[...], right_ref[...], (((0,), (0,)), ((), ())), preferred_element_type=jnp.float32
    )
    for at, target in enumerate(targets):
        if at and targets[at - 1] == target:

            @pl.when(step == at)
            def _():
                sum_ref[...] += product

        else:

            @pl.when(step == at)
            def _():
                sum_ref[...] = product

    put_grads(owners, targets, step, o_ref, sum_ref)


def put_grads(owners, targets, step, o_ref, sum_ref):
    total = sum_ref[...].astype(o_ref.dtype)
    if owners == "mlp":
        tall = total.shape[0] // 4

        @pl.when(step < 4)
        def _():
            for part in range(4):
                o_ref[2 * (4 * step + part)] = total[tall * part : tall * (part + 1)]

        @pl.when(step >= 4)
        def _():
            short = total.shape[0] // 16
            start = pl.multiple_of(short * (step - 4), short)
            for a in range(16):
                o_ref[2 * a + 1, pl.ds(start, short)] = total[short * a : short * (a + 1)]

    else:
        first_twice = len(targets) - 4
        target = jnp.where(step < first_twice, step, first_twice + (step - first_twice) // 2)
        short = total.shape[0] // 16
        start = pl.multiple_of(short * lax.rem(target, 4), short)
        for a in range(16):
            o_ref[2 * a + target // 4, pl.ds(start, short)] = total[short * a : short * (a + 1)]


def weight_grads(jobs, targets, owners, arrays, features, rows):
    return pl.pallas_call(
        functools.partial(weight_grads_body, tuple(jobs), tuple(targets), owners),
        name="weight_grads",
        grid=(len(jobs),),
        in_specs=[pl.BlockSpec(memory_space=pltpu.VMEM)] * len(arrays),
        out_specs=pl.BlockSpec(memory_space=pltpu.VMEM),
        out_shape=jax.ShapeDtypeStruct((32, features // 4, features), LOW),
        scratch_shapes=[
            pltpu.VMEM((rows, features), LOW),
            pltpu.VMEM((rows, features), LOW),
            pltpu.VMEM((features, features), jnp.float32),
        ],
        compiler_params=BIG,
        cost_estimate=pl.CostEstimate(
            flops=2 * len(jobs) * rows * features * features,
            bytes_accessed=2 * 8 * features * features,
            transcendentals=0,
        ),
    )(*arrays)


def low_dot(left, right):
    return dot_float(left, right).astype(LOW)


def dot_t(left, right):
    return lax.dot_general(left, right, (((1,), (1,)), ((), ())), preferred_element_type=jnp.float32)


def t_dot(left, right):
    return lax.dot_general(left, right, (((0,), (0,)), ((), ())), preferred_element_type=jnp.float32)


def stem_weight_blocks(w_conv, w_patch, norm_params, s):
    features = w_patch.shape[1]
    flat = jnp.concatenate([w_conv.reshape(-1, features), w_patch], 0).T
    blocks = slots_to_devices(flat.reshape(PORTIONS, 32, GROUP, flat.shape[1]))
    blocks = blocks.reshape(16, 2, PORTIONS * GROUP, flat.shape[1])
    blocks = lax.dynamic_index_in_dim(blocks, s, 1, keepdims=False)
    rows = PORTIONS * GROUP
    extra = jnp.pad(norm_params, ((0, rows - norm_params.shape[0]), (0, 0)))
    blocks = jnp.concatenate([blocks, jnp.broadcast_to(extra, (16,) + extra.shape)], 2)
    return blocks


def stem_weights(got, w_conv, w_patch, norm_params):
    depth, conv_rows, features = w_conv.shape
    rows = PORTIONS * GROUP
    convs = []
    for layer in range(depth):
        part = got[:, :, layer * conv_rows : (layer + 1) * conv_rows]
        part = part.transpose(1, 0, 2).reshape(rows, 9, features).transpose(1, 0, 2)
        convs.append(part.reshape(9 * rows, features))
    at = depth * conv_rows
    patch = got[:, :, at : at + w_patch.shape[0]].transpose(1, 0, 2).reshape(rows, -1)
    norms = got[:, : norm_params.shape[0], at + w_patch.shape[0] :]
    return convs, patch, norms.transpose(1, 0, 2).reshape(norm_params.shape[0], -1)


def own_columns(norms):
    bits = my_bits()
    cut = norms.reshape(norms.shape[0], PORTIONS, 32, GROUP)
    parts = [
        lax.dynamic_index_in_dim(cut[:, p], slot_of(bits, p), 1, keepdims=False)
        for p in range(PORTIONS)
    ]
    mine = jnp.concatenate(parts, 1).T
    return jnp.pad(mine, ((0, 0), (0, 128 - mine.shape[1])))


def fast_device(
    captions,
    patches,
    prefix,
    prefix_count,
    caption_len,
    cotangent,
    w_patch,
    w_conv,
    w_self_qkv,
    w_self_out,
    w_cross_q,
    w_cross_kv,
    w_cross_out,
    w_up,
    w_down,
    norm_params,
):
    a_index, s_index = lax.axis_index("dp"), lax.axis_index("seq")
    examples, halves = 16, 2
    features = w_self_out.shape[1]
    score_scale = (features // HEADS) ** (-0.5)

    def chunks(w):
        return [w[:, i * features : (i + 1) * features] for i in range(w.shape[1] // features)]

    shard_rows = w_patch.shape[0]
    pieces = [(0, 0, features * i) for i in range(3)] + [(1, 0, 0), (2, 0, 0)]
    pieces += [(3, 0, 0), (3, 0, features), (4, 0, 0)]
    pieces += [(5, 0, features * i) for i in range(4)] + [(6, shard_rows * i, 0) for i in range(4)]
    all_w = pack(
        pieces,
        [w_self_qkv, w_self_out, w_cross_q, w_cross_kv, w_cross_out, w_up, w_down],
        shard_rows,
        features,
    )
    all_w = lax.all_gather(all_w, "dp", axis=1, tiled=True)
    qkv_w = all_w[:3]
    sout_w, cq_w, ck_w, cv_w, cout_w = (all_w[3 + i] for i in range(5))
    up_ws = [all_w[8 + i] for i in range(4)]
    down_w = all_w[12:].reshape(4, examples, -1, features).transpose(1, 0, 2, 3)
    down_w = down_w.reshape(4 * features, features)
    pixels, got_blocks, earlier, prefix_other = gather_many(
        [],
        [patches[0]],
        [stem_weight_blocks(w_conv, w_patch, norm_params, s_index)],
        [captions[0], prefix[0]],
        0,
    )

    convs, patch_w, norms_low = stem_weights(got_blocks, w_conv, w_patch, norm_params)
    norms = norms_low.astype(jnp.float32)
    own_gb = own_columns(norms[:6])
    own_cells = patches.shape[1]
    number = own_cells * examples * halves
    cells = -(-number // CHUNK) * CHUNK
    rows_own = PORTIONS * GROUP
    grid = halves * own_cells
    masks = jnp.asarray(tap_masks(cells, examples))
    def to_channels(by_row, cid):
        blocks = slots_to_devices(by_row.T.reshape(PORTIONS, 32, GROUP, by_row.shape[0]))
        return exchange_all(blocks.reshape(32, rows_own, by_row.shape[0]), cid)

    def laid_out(blocks):
        flat = blocks.transpose(1, 0, 2).reshape(rows_own, number)
        return jnp.pad(flat, ((0, 0), (0, cells - number)))

    n1, r1, y1, x1 = first_block(pixels, patch_w, own_gb, masks, number)
    (x1_all,) = gather_many([x1], [], [], [], 2)
    x1_all = x1_all.reshape(features, cells)
    n2, r2, y2, x2 = conv_block(1, x1_all, convs[0], own_gb, masks, y1, number)
    inputs = captions[0].astype(jnp.float32)
    row_count = inputs.shape[0]
    earlier = earlier.astype(jnp.float32)
    low_one = layer_norm(inputs, norms[6], norms[7]).astype(LOW)
    low_all = jnp.concatenate(
        [layer_norm(earlier, norms[6], norms[7]).astype(LOW), low_one], 0
    )
    queries = (dot_float(low_one, qkv_w[0]).astype(LOW) * score_scale).astype(LOW)
    all_keys, all_values = low_dot(low_all, qkv_w[1]), low_dot(low_all, qkv_w[2])
    info = jnp.stack([s_index, caption_len[0] - s_index * row_count]).astype(jnp.int32)
    no_ok = jnp.zeros((8, 128), jnp.float32)
    self_low, self_lse, x2_all = attend_gather(info, no_ok, queries, all_keys, all_values, x2, 3)
    x2_all = x2_all.reshape(features, cells)
    n3, r3, y3, x3 = conv_block(2, x2_all, convs[1], own_gb, masks, y2, number)
    out_blocks = x3.reshape(rows_own, cells)[:, :number].reshape(rows_own, examples, grid)
    out_blocks = jnp.broadcast_to(
        out_blocks.transpose(1, 0, 2)[:, None], (examples, halves, rows_own, grid)
    )
    in_blocks = exchange_all(out_blocks.reshape(32, rows_own, grid), 4)
    patch_all = devices_to_slots(in_blocks.reshape(32, PORTIONS, GROUP, grid))
    patch_all = patch_all.reshape(features, grid).T

    prefix_own = prefix[0]
    prefix_half = prefix_own.shape[0]
    first_half = s_index == 0
    prefix_all = jnp.concatenate(
        [
            jnp.where(first_half, prefix_own, prefix_other),
            jnp.where(first_half, prefix_other, prefix_own),
        ],
        0,
    )
    memory = jnp.concatenate([prefix_all, patch_all], 0)
    mem_rows = memory.shape[0]
    prefix_total = prefix_all.shape[0]
    mem_padded = jnp.pad(memory, ((0, -mem_rows % 128), (0, 0)))
    mem_keys = low_dot(mem_padded, ck_w)
    mem_values = low_dot(mem_padded, cv_w)
    slot_ids = jnp.arange(mem_padded.shape[0], dtype=jnp.int32)
    mem_ok = (slot_ids < mem_rows) & ((slot_ids >= prefix_total) | (slot_ids < prefix_count[0]))
    mem_ok = jnp.broadcast_to(mem_ok.astype(jnp.float32)[:, None], (mem_padded.shape[0], 128))

    after_self = inputs + dot_float(self_low, sout_w)
    low_two = layer_norm(after_self, norms[8], norms[9]).astype(LOW)
    cross_q = (dot_float(low_two, cq_w).astype(LOW) * score_scale).astype(LOW)
    cross_low, cross_lse = attend("cross", info, mem_ok, cross_q, mem_keys, mem_values)
    after_cross = after_self + dot_float(cross_low, cout_w)
    low_three = layer_norm(after_cross, norms[10], norms[11]).astype(LOW)
    up_proj = jnp.concatenate([dot_float(low_three, w) for w in up_ws], 1)
    hidden = jax.nn.gelu(up_proj).astype(LOW)
    result = after_cross + dot_float(hidden, down_w)

    out_grad = cotangent[0].astype(jnp.float32)
    grad_low = cotangent[0]
    d_upper = (dot_t(grad_low, down_w) * gelu_slope(up_proj)).astype(LOW)
    d_normed = sum(dot_t(d, w) for d, w in zip(chunks(d_upper), up_ws))
    unused_three, norm_back_three = jax.vjp(layer_norm, after_cross, norms[10], norms[11])
    d_three, grad_gain_three, grad_bias_three = norm_back_three(d_normed)
    jobs = [(0, 1, row_count, 0, features * q, 0) for q in range(4)]
    jobs += [(2, 3, row_count, 0, 0, features * j) for j in range(4)]
    mlp_parts = weight_grads(
        jobs, range(8), "mlp", [hidden, grad_low, low_three, d_upper], features, row_count
    )
    mlp_parts, d_three = lax.optimization_barrier((mlp_parts, d_three))

    def scattered(parts):
        parts = parts.reshape(examples, -1, features)
        return lax.psum_scatter(parts, "dp", scatter_dimension=0, tiled=True)[0]

    def summed(own):
        other = lax.ppermute(own, "seq", [(0, 1), (1, 0)])
        return own.astype(jnp.float32) + other.astype(jnp.float32)

    mlp_own = scattered(mlp_parts)
    d_after_cross = out_grad + d_three
    cross_grad_low = d_after_cross.astype(LOW)
    d_cross = dot_t(cross_grad_low, cout_w).astype(LOW)
    d_cross_low, d_mem_keys, d_mem_values = attend_grads(
        "cross", info, mem_ok, cross_q, mem_keys, mem_values, d_cross, cross_lse, score_scale
    )
    unused_two, norm_back_two = jax.vjp(layer_norm, after_self, norms[8], norms[9])
    d_two, grad_gain_two, grad_bias_two = norm_back_two(dot_t(d_cross_low, cq_w))
    d_after_self = d_after_cross + d_two
    d_mem_rows = dot_t(d_mem_keys[:mem_rows], ck_w) + dot_t(d_mem_values[:mem_rows], cv_w)
    d_prefix = d_mem_rows[:prefix_total].reshape(halves, prefix_half, features)
    prefix_back = lax.dynamic_index_in_dim(d_prefix, s_index, 0, keepdims=False)
    away = lax.dynamic_index_in_dim(d_prefix, 1 - s_index, 0, keepdims=False).astype(LOW)
    prefix_back = prefix_back + lax.ppermute(away, "seq", [(0, 1), (1, 0)]).astype(jnp.float32)
    d_third = d_mem_rows[prefix_total:].astype(LOW)

    self_grad_low = d_after_self.astype(LOW)
    d_self = dot_t(self_grad_low, sout_w).astype(LOW)
    d_query, d_all_keys, d_all_values = attend_grads(
        "self", info, no_ok, queries, all_keys, all_values, d_self, self_lse, score_scale
    )
    d_normed_all = dot_t(d_all_keys, qkv_w[1]) + dot_t(d_all_values, qkv_w[2])
    from_later = lax.ppermute(d_normed_all[:row_count].astype(LOW), "seq", [(1, 0)])
    d_normed_one = dot_t(d_query, qkv_w[0]) + d_normed_all[row_count:]
    d_normed_one = d_normed_one + from_later.astype(jnp.float32)
    unused_one, norm_back_one = jax.vjp(layer_norm, inputs, norms[6], norms[7])
    d_one, grad_gain_one, grad_bias_one = norm_back_one(d_normed_one)
    d_inputs = d_after_self + d_one
    arrays = [cross_low, cross_grad_low, low_two, d_cross_low, mem_padded, d_mem_keys, d_mem_values]
    arrays += [self_low, self_grad_low, low_all, d_query, d_all_keys, d_all_values, low_one]
    mem_count = mem_padded.shape[0]
    jobs = [
        (0, 1, row_count, 0, 0, 0),
        (2, 3, row_count, 0, 0, 0),
        (4, 5, mem_count, 0, 0, 0),
        (4, 6, mem_count, 0, 0, 0),
        (7, 8, row_count, 0, 0, 0),
        (13, 10, row_count, 0, 0, 0),
        (9, 11, row_count, 0, 0, 0),
        (9, 11, row_count, row_count, 0, 0),
        (9, 12, row_count, 0, 0, 0),
        (9, 12, row_count, row_count, 0, 0),
    ]
    rest_parts = weight_grads(
        jobs, (0, 1, 2, 3, 4, 5, 6, 6, 7, 7), "rest", arrays, features, row_count
    )
    rest_own = scattered(rest_parts)

    d_y3 = to_channels(d_third, 6).astype(jnp.float32)
    d_y3 = laid_out(jnp.sum(d_y3.reshape(examples, halves, rows_own, grid), 1))

    def back_through(layer, d_y, n, r, x_all, w, cid):
        dx, grad_w, sums = conv_block_back(layer, d_y, n, r, own_gb, masks, x_all, w.T, number)
        total = reduce_all(dx.reshape(PORTIONS, 32, GROUP, cells), cid)
        grad_w = grad_w.reshape(9, rows_own, features).transpose(1, 0, 2)
        grad_w = grad_w.reshape(rows_own, examples, -1).transpose(1, 0, 2)
        return d_y + total.reshape(rows_own, cells), grad_w, sums

    d_y2, grad_conv_one, sums3 = back_through(2, d_y3, n3, r3, x2_all, convs[1], 7)
    d_y2, mlp_own = lax.optimization_barrier((d_y2, mlp_own))
    d_y1, grad_conv_zero, sums2 = back_through(1, d_y2, n2, r2, x1_all, convs[0], 8)
    grad_patch, sums1 = first_block_back(d_y1, n1, r1, own_gb, pixels, number)
    grad_patch = grad_patch.reshape(rows_own, examples, -1).transpose(1, 0, 2)
    patch_rows = grad_patch.shape[2]
    bn_grads = jnp.concatenate([sums1[:, :2], sums2[:, :2], sums3[:, :2]], 1).astype(LOW)
    ln_grads = jnp.stack(
        [
            grad_gain_one,
            grad_bias_one,
            grad_gain_two,
            grad_bias_two,
            grad_gain_three,
            grad_bias_three,
        ]
    ).astype(LOW)
    ln_count = ln_grads.shape[0]
    ln_blocks = ln_grads.reshape(ln_count, examples, -1).transpose(1, 0, 2)
    ln_blocks = jnp.pad(ln_blocks, ((0, 0), (0, rows_own - ln_count), (0, 0)))
    send_blocks = jnp.concatenate(
        [
            grad_conv_zero,
            grad_conv_one,
            grad_patch,
            jnp.broadcast_to(bn_grads, (examples,) + bn_grads.shape),
            ln_blocks,
        ],
        2,
    )
    got = swap_both(send_blocks, 9)
    got = got.transpose(1, 0, 2, 3).reshape(32, rows_own, -1)
    conv_rows = w_conv.shape[1]
    width = 2 * conv_rows + patch_rows
    mixed = devices_to_slots(got[:, :, : width + 6].reshape(32, PORTIONS, GROUP, width + 6))
    mixed = mixed.reshape(features, width + 6)
    stem_grads = mixed[:, :width].T.astype(jnp.float32)
    bn_part = lax.dynamic_slice_in_dim(mixed[:, width:], a_index * patch_rows, patch_rows, 0)
    ln_part = jnp.sum(got[:, :ln_count, width + 6 :].astype(jnp.float32), 0)
    norm_grads = jnp.concatenate([bn_part.T.astype(jnp.float32), ln_part], 0)

    mlp_sum, rest_sum = summed(mlp_own), summed(rest_own)
    down_sum = mlp_sum[: 4 * shard_rows]
    up_sum = [mlp_sum[(4 + i) * shard_rows : (5 + i) * shard_rows] for i in range(4)]
    rest = [rest_sum[i * shard_rows : (i + 1) * shard_rows] for i in range(8)]
    return (
        result[None].astype(LOW),
        d_inputs[None].astype(LOW),
        prefix_back[None].astype(LOW),
        stem_grads[2 * conv_rows :],
        stem_grads[: 2 * conv_rows].reshape(w_conv.shape),
        jnp.concatenate(rest[5:], 1),
        rest[4],
        rest[1],
        jnp.concatenate(rest[2:4], 1),
        rest[0],
        jnp.concatenate(up_sum, 1),
        down_sum,
        norm_grads,
    )


def suits(mesh):
    return mesh.shape["dp"] == 16 and mesh.shape["seq"] == 2


def solution(mesh):
    return jax.shard_map(
        fast_device if suits(mesh) else general_device,
        mesh=mesh,
        in_specs=(
            P("dp", "seq", None),
            P("dp", "seq", None),
            P("dp", "seq", None),
            P("dp"),
            P("dp"),
            P("dp", "seq", None),
            P("dp", None),
            P(None, "dp", None),
            P("dp", None),
            P("dp", None),
            P("dp", None),
            P("dp", None),
            P("dp", None),
            P("dp", None),
            P("dp", None),
            P(None, "dp"),
        ),
        out_specs=(
            P("dp", "seq", None),
            P("dp", "seq", None),
            P("dp", "seq", None),
            P("dp", None),
            P(None, "dp", None),
            P("dp", None),
            P("dp", None),
            P("dp", None),
            P("dp", None),
            P("dp", None),
            P("dp", None),
            P("dp", None),
            P(None, "dp"),
        ),
        check_vma=False,
    )
```

```python
import functools

import jax
import jax.numpy as jnp
import numpy as np
from jax import lax
from jax.experimental import pallas as pl
from jax.experimental.pallas import tpu as pltpu
from jax.sharding import PartitionSpec as P

HEADS = 12
SIDE = 14
MESH = pl.DeviceIdType.MESH
LOW = jnp.bfloat16

STEPS = ((4, 3, 2, 0), (4, 0, 3, 2), (4, 2, 0, 3))
PORTIONS = 3
GROUP = 8


def my_bits():
    a = lax.axis_index("dp")
    return [
        lax.axis_index("seq"),
        lax.rem(a, 2),
        lax.rem(a // 2, 2),
        lax.rem(a // 4, 2),
        lax.rem(a // 8, 2),
    ]


def flipped(bits, which):
    return [1 - b if i == which else b for i, b in enumerate(bits)]


def place(bits):
    return (bits[1] + 2 * bits[2] + 4 * bits[3] + 8 * bits[4], bits[0])


def slot_of(bits, p):
    order = STEPS[p]
    return (
        bits[order[0]] + 2 * bits[order[1]] + 4 * bits[order[2]] + 8 * bits[order[3]] + 16 * bits[1]
    )


def device_of_slot(p):
    owners = np.zeros(32, np.int64)
    for e in range(32):
        bits = [(e >> i) & 1 for i in range(5)]
        owners[int(slot_of(bits, p))] = e
    return owners


def slots_to_devices(array):
    parts = []
    for p in range(PORTIONS):
        rest = array.shape[2:]
        names = [1, STEPS[p][3], STEPS[p][2], STEPS[p][1], STEPS[p][0]]
        cube = array[p].reshape((2,) * 5 + rest)
        perm = [names.index(bit) for bit in (4, 3, 2, 1, 0)]
        cube = cube.transpose(perm + [5 + i for i in range(len(rest))])
        parts.append(cube.reshape((32,) + rest))
    return jnp.stack(parts, 1)


def devices_to_slots(array):
    parts = []
    for p in range(PORTIONS):
        rest = array.shape[2:]
        names = [4, 3, 2, 1, 0]
        cube = array[:, p].reshape((2,) * 5 + rest)
        want = [1, STEPS[p][3], STEPS[p][2], STEPS[p][1], STEPS[p][0]]
        perm = [names.index(bit) for bit in want]
        cube = cube.transpose(perm + [5 + i for i in range(len(rest))])
        parts.append(cube.reshape((32,) + rest))
    return jnp.stack(parts, 0)


def greet(places):
    barrier = pltpu.get_barrier_semaphore()
    for where in places:
        pl.semaphore_signal(barrier, inc=1, device_id=where, device_id_type=MESH)
    pl.semaphore_wait(barrier, len(places))


def arrived(ref, sem):
    pltpu.make_async_remote_copy(
        src_ref=ref,
        dst_ref=ref,
        send_sem=sem,
        recv_sem=sem,
        device_id=(lax.axis_index("dp"), 1 - lax.axis_index("seq")),
        device_id_type=MESH,
    ).wait_recv()


def with_mask(bits, mask):
    return [1 - b if (mask >> i) & 1 else b for i, b in enumerate(bits)]


def number_of(bits):
    return bits[0] + 2 * bits[1] + 4 * bits[2] + 8 * bits[3] + 16 * bits[4]


def stem_part(ref, bits, p):
    return ref.at[p, pl.ds(slot_of(bits, p), 1)]


def stem_own(ref, bits, p):
    return ref.at[pl.ds(p, 1)]


def rows_part(ref, bits, p):
    width = ref.shape[2] // PORTIONS
    return ref.at[number_of(bits), :, pl.ds(p * width, width)]


def rows_own(ref, bits, p):
    width = ref.shape[1] // PORTIONS
    return ref.at[:, pl.ds(p * width, width)]


KINDS = {
    "stem": (stem_own, stem_part),
    "rows": (rows_own, rows_part),
}


def gather_steps(kinds, swaps, pairs, refs):
    count = len(kinds)
    total = count + swaps + pairs
    ins, outs, sems = refs[:total], refs[total : 2 * total], refs[2 * total :]
    send_sem, recv_sem, own_sem, swap_send, swap_recv, pair_send, pair_recv = sems
    bits = my_bits()
    a, s = lax.axis_index("dp"), bits[0]
    dp = ins[count].shape[0] if swaps else 1
    partners = [place(flipped(bits, b)) for b in range(5)]
    partners += [(lax.rem(a + j, dp), s) for j in range(1, dp)]

    def own_of(i, p):
        return KINDS[kinds[i]][0](ins[i], bits, p)

    def part_of(i, p, mask):
        return KINDS[kinds[i]][1](outs[i], with_mask(bits, mask), p)

    def block(i, p, mask, bit):
        return pltpu.make_async_remote_copy(
            src_ref=own_of(i, p) if mask == 0 else part_of(i, p, mask),
            dst_ref=part_of(i, p, mask),
            send_sem=send_sem.at[i, p, mask ^ (1 << bit)],
            recv_sem=recv_sem.at[i, p, mask ^ (1 << bit)],
            device_id=place(flipped(bits, bit)),
            device_id_type=MESH,
        )

    def await_part(i, p, mask):
        arrived(part_of(i, p, mask), recv_sem.at[i, p, mask])

    def own_copy(i, p):
        return pltpu.make_async_copy(own_of(i, p), part_of(i, p, 0), own_sem.at[i, p])

    def swap_own():
        return pltpu.make_async_copy(ins[count].at[a], outs[count].at[a], swap_send.at[0])

    def swap_copy(j):
        to = lax.rem(a + j, dp)
        return pltpu.make_async_remote_copy(
            src_ref=ins[count].at[to],
            dst_ref=outs[count].at[a],
            send_sem=swap_send.at[j],
            recv_sem=swap_recv.at[j],
            device_id=(to, s),
            device_id_type=MESH,
        )

    def pair_copy(j):
        return pltpu.make_async_remote_copy(
            src_ref=ins[count + swaps + j],
            dst_ref=outs[count + swaps + j],
            send_sem=pair_send.at[j],
            recv_sem=pair_recv.at[j],
            device_id=(a, 1 - s),
            device_id_type=MESH,
        )

    every = [(i, p) for i in range(count) for p in range(PORTIONS)]
    held = {p: [0] for p in range(PORTIONS)}
    fresh = {p: [0] for p in range(PORTIONS)}
    sent = []
    steps = []
    for k in range(5):
        plan = []
        for i in range(count):
            for p in range(PORTIONS):
                waits = list(fresh[p]) if k else []
                links = [(mask, STEPS[p][k]) for mask in held[p]] if k < 4 else []
                plan.append((i, p, waits, links))
                sent += [(i, p, mask, bit) for mask, bit in links]
            for p in range(PORTIONS):
                cores = [(mask, 1) for mask in fresh[p]]
                plan.append((i, p, [], cores))
                sent += [(i, p, mask, bit) for mask, bit in cores]

        def run(k=k, plan=plan):
            if k == 0:
                greet(partners)
            for i, p, waits, sends in plan:
                for mask in waits:
                    await_part(i, p, mask)
                for mask, bit in sends:
                    block(i, p, mask, bit).start()
            if k == 0:
                for i, p in every:
                    own_copy(i, p).start()
                for j in range(pairs):
                    pair_copy(j).start()
                if swaps:
                    swap_own().start()
                for j in range(1, dp):
                    swap_copy(j).start()

        steps.append(run)
        if k < 4:
            for p in range(PORTIONS):
                fresh[p] = [mask ^ (1 << STEPS[p][k]) for mask in held[p]]
                held[p] = held[p] + fresh[p]

    def finish():
        for i, p in every:
            for mask in held[p]:
                await_part(i, p, mask ^ 2)
        for j in range(1, dp):
            arrived(outs[count].at[lax.rem(a - j + dp, dp)], swap_recv.at[j])
        for j in range(pairs):
            pair_copy(j).wait()
        for i, p, mask, bit in sent:
            block(i, p, mask, bit).wait_send()
        for j in range(1, dp):
            swap_copy(j).wait_send()
        for i, p in every:
            own_copy(i, p).wait()
        if swaps:
            swap_own().wait()

    steps.append(finish)
    return steps


def gather_body(kinds, swaps, pairs, *refs):
    for step in gather_steps(kinds, swaps, pairs, refs):
        step()


def gather_sems(count, pairs):
    return [
        pltpu.SemaphoreType.DMA((count, PORTIONS, 32)),
        pltpu.SemaphoreType.DMA((count, PORTIONS, 32)),
        pltpu.SemaphoreType.DMA((count, PORTIONS)),
        pltpu.SemaphoreType.DMA((16,)),
        pltpu.SemaphoreType.DMA((16,)),
        pltpu.SemaphoreType.DMA((max(pairs, 1),)),
        pltpu.SemaphoreType.DMA((max(pairs, 1),)),
    ]


def gather_many(stems, rows, swaps, pairs, cid):
    kinds = ["stem"] * len(stems) + ["rows"] * len(rows)
    arrays = list(stems) + list(rows) + list(swaps) + list(pairs)
    shapes = [jax.ShapeDtypeStruct((PORTIONS, 32) + x.shape[1:], x.dtype) for x in stems]
    shapes += [jax.ShapeDtypeStruct((32,) + x.shape, x.dtype) for x in rows]
    shapes += [jax.ShapeDtypeStruct(x.shape, x.dtype) for x in list(swaps) + list(pairs)]
    space = pl.BlockSpec(memory_space=pltpu.HBM)
    return pl.pallas_call(
        functools.partial(gather_body, tuple(kinds), len(swaps), len(pairs)),
        name="gather_many",
        out_shape=tuple(shapes),
        in_specs=[space] * len(arrays),
        out_specs=(space,) * len(arrays),
        scratch_shapes=gather_sems(len(kinds), len(pairs)),
        compiler_params=pltpu.CompilerParams(collective_id=cid, has_side_effects=True),
    )(*arrays)


def attend_gather_body(width, *refs):
    info_ref, ok_ref, q_ref, k_ref, v_ref, x_ref, o_ref, lse_ref, all_ref = refs[:9]
    steps = gather_steps(("stem",), 0, 0, (x_ref, all_ref) + refs[9:])
    for at, step in enumerate(steps[:-1]):

        @pl.when(pl.program_id(0) == at)
        def _():
            step()

    attend_body("self", width, info_ref, ok_ref, q_ref, k_ref, v_ref, o_ref, lse_ref)

    @pl.when(pl.program_id(0) == pl.num_programs(0) - 1)
    def _():
        steps[-1]()


def attend_gather(info, ok, q, k, v, x, cid):
    rows, features = q.shape
    keys = k.shape[0]
    width = features // HEADS
    pairs = features // PAIR
    return pl.pallas_call(
        functools.partial(attend_gather_body, width),
        name="attend_gather",
        grid=(pairs,),
        in_specs=attention_specs(rows, keys, ok) + [pl.BlockSpec(memory_space=pltpu.HBM)],
        out_specs=(
            pl.BlockSpec((rows, PAIR), lambda i: (0, i)),
            pl.BlockSpec((1, 8, rows), lambda i: (i, 0, 0)),
            pl.BlockSpec(memory_space=pltpu.HBM),
        ),
        out_shape=(
            jax.ShapeDtypeStruct((rows, features), LOW),
            jax.ShapeDtypeStruct((pairs, 8, rows), jnp.float32),
            jax.ShapeDtypeStruct((PORTIONS, 32) + x.shape[1:], x.dtype),
        ),
        scratch_shapes=gather_sems(1, 0),
        compiler_params=pltpu.CompilerParams(
            collective_id=cid, has_side_effects=True, vmem_limit_bytes=48 << 20
        ),
    )(info, ok, q, k, v, x)


def pack_body(pieces, *refs):
    ins, o_ref = refs[:-1], refs[-1]
    rows, cols = o_ref.shape[1:]
    for at, (which, row, col) in enumerate(pieces):
        o_ref[at] = ins[which][row : row + rows, col : col + cols]


def pack(pieces, arrays, rows, cols):
    return pl.pallas_call(
        functools.partial(pack_body, tuple(pieces)),
        name="pack",
        out_shape=jax.ShapeDtypeStruct((len(pieces), rows, cols), arrays[0].dtype),
    )(*arrays)


def swap_both_steps(x_ref, pair_ref, o_ref, other_ref, sems):
    send_sem, recv_sem, pass_sem, got_sem, own_sem, pair_sem = sems
    a, s = lax.axis_index("dp"), lax.axis_index("seq")
    count = x_ref.shape[0]
    partners = [(lax.rem(a + j, count), s) for j in range(1, count)] + [(a, 1 - s)]

    def own():
        return pltpu.make_async_copy(x_ref.at[a], o_ref.at[s, a], own_sem)

    def direct(j):
        to = lax.rem(a + j, count)
        return pltpu.make_async_remote_copy(
            src_ref=x_ref.at[to],
            dst_ref=o_ref.at[s, a],
            send_sem=send_sem.at[j],
            recv_sem=recv_sem.at[j],
            device_id=(to, s),
            device_id_type=MESH,
        )

    def onward(j):
        source = lax.rem(a - j + count, count)
        return pltpu.make_async_remote_copy(
            src_ref=o_ref.at[s, source] if j else x_ref.at[a],
            dst_ref=o_ref.at[s, source],
            send_sem=pass_sem.at[j],
            recv_sem=got_sem.at[j],
            device_id=(a, 1 - s),
            device_id_type=MESH,
        )

    def paired():
        return pltpu.make_async_remote_copy(
            src_ref=pair_ref,
            dst_ref=other_ref,
            send_sem=pair_sem.at[0],
            recv_sem=pair_sem.at[1],
            device_id=(a, 1 - s),
            device_id_type=MESH,
        )

    def start():
        own().start()
        paired().start()
        onward(0).start()
        for j in range(1, count):
            direct(j).start()

    def pass_on():
        for j in range(1, count):
            arrived(o_ref.at[s, lax.rem(a - j + count, count)], recv_sem.at[j])
            onward(j).start()

    def finish():
        for j in range(count):
            arrived(o_ref.at[1 - s, lax.rem(a - j + count, count)], got_sem.at[j])
        for j in range(1, count):
            direct(j).wait_send()
        for j in range(count):
            onward(j).wait_send()
        own().wait()
        paired().wait()

    return partners, start, pass_on, finish


def swap_both_sems(count):
    return [pltpu.SemaphoreType.DMA((count,))] * 4 + [
        pltpu.SemaphoreType.DMA,
        pltpu.SemaphoreType.DMA((2,)),
    ]


def reduce_body(swaps, *refs):
    count = 1 + swaps
    ins, outs, refs = refs[:count], refs[count : 2 * count], refs[2 * count :]
    x_ref, o_ref = ins[0], outs[0]
    bufs, (send_sem, recv_sem) = refs[:5], refs[5:7]
    bits = my_bits()
    partners = [place(flipped(bits, b)) for b in range(5)]
    if swaps:
        others, start, pass_on, finish = swap_both_steps(*ins[1:], *outs[1:], refs[7:])
        partners += others
    greet(partners)
    started = []

    def send(p, src, dst, bit, k):
        copy = pltpu.make_async_remote_copy(
            src_ref=src,
            dst_ref=dst,
            send_sem=send_sem.at[p, k],
            recv_sem=recv_sem.at[p, k],
            device_id=place(flipped(bits, bit)),
            device_id_type=MESH,
        )
        copy.start()
        started.append(copy)

    for p in range(PORTIONS):
        away = 16 * (1 - bits[1])
        send(p, x_ref.at[p, pl.ds(away, 16)], bufs[0].at[p], 1, 0)
    for k in range(5):
        size = 16 >> k
        if swaps and k == 1:
            start()
        if swaps and k == 4:
            pass_on()
        for p in range(PORTIONS):
            arrived(bufs[k].at[p], recv_sem.at[p, k])
            if k == 0:
                base, held = 16 * bits[1], x_ref
            else:
                base, held = size * bits[STEPS[p][4 - k]], bufs[k - 1]
            if k == 4:
                o_ref[p] = held[p, base].astype(jnp.float32) + bufs[k][p, 0].astype(jnp.float32)
                continue
            for j in range(size):
                total = held[p, base + j].astype(jnp.float32) + bufs[k][p, j].astype(jnp.float32)
                bufs[k][p, j] = total.astype(bufs[k].dtype)
            half = size // 2
            send(
                p,
                bufs[k].at[p, pl.ds(half * (1 - bits[STEPS[p][3 - k]]), half)],
                bufs[k + 1].at[p],
                STEPS[p][3 - k],
                k + 1,
            )
    if swaps:
        finish()
    for copy in started:
        copy.wait_send()


def reduce_all(x, swaps, cid):
    rest = x.shape[2:]
    vmem, hbm = pl.BlockSpec(memory_space=pltpu.VMEM), pl.BlockSpec(memory_space=pltpu.HBM)
    return pl.pallas_call(
        functools.partial(reduce_body, len(swaps)),
        name="reduce_all",
        out_shape=tuple(
            [jax.ShapeDtypeStruct((PORTIONS,) + rest, jnp.float32)]
            + [jax.ShapeDtypeStruct((2,) + g.shape, g.dtype) for g in swaps[:1]]
            + [jax.ShapeDtypeStruct(g.shape, g.dtype) for g in swaps[1:]]
        ),
        in_specs=[vmem] + [hbm] * len(swaps),
        out_specs=tuple([vmem] + [hbm] * len(swaps)),
        scratch_shapes=[pltpu.VMEM((PORTIONS, 16 >> k) + rest, x.dtype) for k in range(5)]
        + [pltpu.SemaphoreType.DMA((PORTIONS, 5)), pltpu.SemaphoreType.DMA((PORTIONS, 5))]
        + (swap_both_sems(swaps[0].shape[0]) if swaps else []),
        compiler_params=pltpu.CompilerParams(
            collective_id=cid, has_side_effects=True, vmem_limit_bytes=40 << 20
        ),
    )(x, *swaps)


def swap_both_body(x_ref, pair_ref, o_ref, other_ref, *sems):
    partners, start, pass_on, finish = swap_both_steps(x_ref, pair_ref, o_ref, other_ref, sems)
    greet(partners)
    start()
    pass_on()
    finish()


def swap_both(x, pair, cid):
    space = pl.BlockSpec(memory_space=pltpu.HBM)
    return pl.pallas_call(
        swap_both_body,
        name="swap_both",
        out_shape=(
            jax.ShapeDtypeStruct((2,) + x.shape, x.dtype),
            jax.ShapeDtypeStruct(pair.shape, pair.dtype),
        ),
        in_specs=[space] * 2,
        out_specs=(space,) * 2,
        scratch_shapes=swap_both_sems(x.shape[0]),
        compiler_params=pltpu.CompilerParams(collective_id=cid, has_side_effects=True),
    )(x, pair)


def exchange_body(x_ref, o_ref, send_sem, recv_sem, own_sem):
    e = 2 * lax.axis_index("dp") + lax.axis_index("seq")
    count = x_ref.shape[0]

    def where(number):
        return (number // 2, lax.rem(number, 2))

    greet([where(lax.rem(e + j, count)) for j in range(1, count)])
    own = pltpu.make_async_copy(x_ref.at[e], o_ref.at[e], own_sem)
    own.start()
    copies = []
    for j in range(1, count):
        to = lax.rem(e + j, count)
        copy = pltpu.make_async_remote_copy(
            src_ref=x_ref.at[to],
            dst_ref=o_ref.at[e],
            send_sem=send_sem.at[j],
            recv_sem=recv_sem.at[j],
            device_id=where(to),
            device_id_type=MESH,
        )
        copy.start()
        copies.append(copy)
    for j in range(1, count):
        got = o_ref.at[lax.rem(e - j + count, count)]
        arrived(got, recv_sem.at[j])
    for copy in copies:
        copy.wait_send()
    own.wait()


def exchange_all(x, cid):
    count = x.shape[0]
    return pl.pallas_call(
        exchange_body,
        name="exchange_all",
        out_shape=jax.ShapeDtypeStruct(x.shape, x.dtype),
        in_specs=[pl.BlockSpec(memory_space=pltpu.HBM)],
        out_specs=pl.BlockSpec(memory_space=pltpu.HBM),
        scratch_shapes=[
            pltpu.SemaphoreType.DMA((count,)),
            pltpu.SemaphoreType.DMA((count,)),
            pltpu.SemaphoreType.DMA,
        ],
        compiler_params=pltpu.CompilerParams(collective_id=cid, has_side_effects=True),
    )(x)


GELU_C = 0.7978845608028654
GELU_A = 0.044715


def gelu_of(x):
    return 0.5 * x * (1.0 + jnp.tanh(GELU_C * (x + GELU_A * (x * x * x))))


def gelu_slope(x):
    t = jnp.tanh(GELU_C * (x + GELU_A * (x * x * x)))
    return 0.5 * (1.0 + t) + 0.5 * x * (1.0 - t * t) * (GELU_C * (1.0 + 3.0 * GELU_A * (x * x)))


CHUNK = 640


def tap_masks(cells, examples):
    rows = examples * SIDE * SIDE
    at = np.arange(rows)
    i, j = (at // SIDE) % SIDE, at % SIDE
    out = np.zeros((16, cells), np.float32)
    for r in range(3):
        for c in range(3):
            ok = (i + r - 1 >= 0) & (i + r - 1 < SIDE) & (j + c - 1 >= 0) & (j + c - 1 < SIDE)
            out[3 * r + c, :rows] = ok
    out[9, :rows] = 1.0
    return out


def tap_shift(tap):
    return SIDE * (tap // 3 - 1) + tap % 3 - 1


def norm_act(values, valid, gain, bias, number):
    centre = jnp.sum(values, 1, keepdims=True) / number
    away = jnp.where(valid > 0, values - centre, 0.0)
    rstd = lax.rsqrt(jnp.sum(away * away, 1, keepdims=True) / number + 1e-05)
    normed = away * rstd
    return normed, rstd, gelu_of(normed * gain + bias)


def put_low(x_ref, y):
    for p in range(PORTIONS):
        x_ref[p] = y[GROUP * p : GROUP * (p + 1)].astype(x_ref.dtype)


def first_body(number, p_ref, w_ref, gb_ref, m_ref, n_ref, rstd_ref, y_ref, x_ref, v_ref):
    blocks, size = p_ref.shape[0], p_ref.shape[1]
    v_ref[:, blocks * size :] = jnp.zeros((v_ref.shape[0], v_ref.shape[1] - blocks * size), jnp.float32)
    for block in range(blocks):
        v_ref[:, block * size : (block + 1) * size] = lax.dot_general(
            w_ref[...], p_ref[block], (((1,), (1,)), ((), ())), preferred_element_type=jnp.float32
        )
    normed, rstd, act = norm_act(v_ref[...], m_ref[9:10, :], gb_ref[:, 0:1], gb_ref[:, 1:2], number)
    n_ref[...] = normed
    rstd_ref[...] = jnp.broadcast_to(rstd, rstd_ref.shape)
    y_ref[...] = act
    put_low(x_ref, act)


def conv_body(number, layer, x_in, w_ref, gb_ref, m_ref, y_in, n_ref, rstd_ref, y_ref, x_ref, z_ref):
    cells = x_in.shape[1]
    rows = y_in.shape[0]
    for start in range(0, cells, CHUNK):
        z_ref[:, start : start + CHUNK] = jnp.dot(
            w_ref[...], x_in[:, start : start + CHUNK], preferred_element_type=jnp.float32
        )
    total = jnp.zeros((rows, cells), jnp.float32)
    for tap in range(9):
        moved = z_ref[rows * tap : rows * (tap + 1), :]
        shift = (-tap_shift(tap)) % cells
        if shift:
            moved = pltpu.roll(moved, shift, 1)
        total = total + jnp.where(m_ref[tap : tap + 1, :] > 0, moved, 0.0)
    normed, rstd, act = norm_act(
        total,
        m_ref[9:10, :],
        gb_ref[:, 2 * layer : 2 * layer + 1],
        gb_ref[:, 2 * layer + 1 : 2 * layer + 2],
        number,
    )
    n_ref[...] = normed
    rstd_ref[...] = jnp.broadcast_to(rstd, rstd_ref.shape)
    y = y_in[...] + act
    y_ref[...] = y
    put_low(x_ref, y)


def norm_slope(number, dy, normed, rstd, gain, bias):
    e = dy * gelu_slope(normed * gain + bias)
    d_gain = jnp.sum(e * normed, 1, keepdims=True)
    d_bias = jnp.sum(e, 1, keepdims=True)
    dn = e * gain
    mean_dn = d_bias * gain / number
    mean_dnn = d_gain * gain / number
    return rstd * (dn - mean_dn - normed * mean_dnn), d_gain, d_bias


def conv_back_body(
    number, layer, dy_ref, n_ref, rstd_ref, gb_ref, m_ref, x_in, wt_ref, dx_ref, g_ref, s_ref, d_ref
):
    cells = x_in.shape[1]
    rows = dy_ref.shape[0]
    dv, d_gain, d_bias = norm_slope(
        number,
        dy_ref[...],
        n_ref[...],
        rstd_ref[:, 0:1],
        gb_ref[:, 2 * layer : 2 * layer + 1],
        gb_ref[:, 2 * layer + 1 : 2 * layer + 2],
    )
    lanes = lax.broadcasted_iota(jnp.int32, s_ref.shape, 1)
    s_ref[...] = jnp.where(lanes == 0, d_gain, d_bias)
    for tap in range(9):
        shift = tap_shift(tap) % cells
        moved = pltpu.roll(dv, shift, 1) if shift else dv
        moved = jnp.where(m_ref[8 - tap : 9 - tap, :] > 0, moved, 0.0)
        d_ref[rows * tap : rows * (tap + 1), :] = moved.astype(d_ref.dtype)
    for start in range(0, cells, CHUNK):
        dx_ref[:, start : start + CHUNK] = jnp.dot(
            wt_ref[...], d_ref[:, start : start + CHUNK], preferred_element_type=jnp.float32
        ).astype(dx_ref.dtype)
    for start in range(0, x_in.shape[0], 256):
        g_ref[:, start : start + 256] = lax.dot_general(
            d_ref[...],
            x_in[start : start + 256, :],
            (((1,), (1,)), ((), ())),
            preferred_element_type=jnp.float32,
        ).astype(g_ref.dtype)


def first_back_body(number, dy_ref, n_ref, rstd_ref, gb_ref, p_ref, g_ref, s_ref):
    dv, d_gain, d_bias = norm_slope(
        number, dy_ref[...], n_ref[...], rstd_ref[:, 0:1], gb_ref[:, 0:1], gb_ref[:, 1:2]
    )
    lanes = lax.broadcasted_iota(jnp.int32, s_ref.shape, 1)
    s_ref[...] = jnp.where(lanes == 0, d_gain, d_bias)
    blocks, size = p_ref.shape[0], p_ref.shape[1]
    total = jnp.zeros(g_ref.shape, jnp.float32)
    for block in range(blocks):
        shift = (-block * size) % dv.shape[1]
        piece = (pltpu.roll(dv, shift, 1) if shift else dv)[:, :size]
        total = total + jnp.dot(
            piece.astype(p_ref.dtype), p_ref[block], preferred_element_type=jnp.float32
        )
    g_ref[...] = total.astype(g_ref.dtype)


BIG = pltpu.CompilerParams(vmem_limit_bytes=48 << 20)


def first_block(pixels, w, gb, masks, number):
    rows, cells = w.shape[0], masks.shape[1]
    return pl.pallas_call(
        functools.partial(first_body, number),
        name="stem_first",
        out_shape=(
            jax.ShapeDtypeStruct((rows, cells), jnp.float32),
            jax.ShapeDtypeStruct((rows, 128), jnp.float32),
            jax.ShapeDtypeStruct((rows, cells), jnp.float32),
            jax.ShapeDtypeStruct((PORTIONS, GROUP, cells), LOW),
        ),
        scratch_shapes=[pltpu.VMEM((rows, cells), jnp.float32)],
        compiler_params=BIG,
    )(pixels, w, gb, masks)


def conv_block(layer, x_all, w, gb, masks, y, number):
    rows, cells = y.shape
    return pl.pallas_call(
        functools.partial(conv_body, number, layer),
        name="stem_conv",
        out_shape=(
            jax.ShapeDtypeStruct((rows, cells), jnp.float32),
            jax.ShapeDtypeStruct((rows, 128), jnp.float32),
            jax.ShapeDtypeStruct((rows, cells), jnp.float32),
            jax.ShapeDtypeStruct((PORTIONS, GROUP, cells), LOW),
        ),
        scratch_shapes=[pltpu.VMEM((9 * rows, cells), jnp.float32)],
        compiler_params=BIG,
    )(x_all, w, gb, masks, y)


def conv_block_back(layer, dy, normed, rstd, gb, masks, x_all, w_t, number):
    rows, cells = dy.shape
    features = x_all.shape[0]
    return pl.pallas_call(
        functools.partial(conv_back_body, number, layer),
        name="stem_conv_back",
        out_shape=(
            jax.ShapeDtypeStruct((features, cells), LOW),
            jax.ShapeDtypeStruct((9 * rows, features), LOW),
            jax.ShapeDtypeStruct((rows, 128), jnp.float32),
        ),
        scratch_shapes=[pltpu.VMEM((9 * rows, cells), LOW)],
        compiler_params=BIG,
    )(dy, normed, rstd, gb, masks, x_all, w_t)


def first_block_back(dy, normed, rstd, gb, pixels, number):
    rows, cells = dy.shape
    return pl.pallas_call(
        functools.partial(first_back_body, number),
        name="stem_first_back",
        out_shape=(
            jax.ShapeDtypeStruct((rows, pixels.shape[2]), LOW),
            jax.ShapeDtypeStruct((rows, 128), jnp.float32),
        ),
        compiler_params=BIG,
    )(dy, normed, rstd, gb, pixels)


def padded_2(cells, sides, width):
    for axis, dim in sides:
        count = lax.axis_size(axis)
        ends = count - 1
        head = lax.slice_in_dim(cells, 0, width, axis=dim)
        tail = lax.slice_in_dim(cells, cells.shape[dim] - width, cells.shape[dim], axis=dim)
        cells = jnp.concatenate(
            [
                lax.ppermute(tail, axis, [(i, (i + 1) % count) for i in range(ends)]),
                cells,
                lax.ppermute(head, axis, [((i + 1) % count, i) for i in range(ends)]),
            ],
            axis=dim,
        )
    return cells


def passed_along(array, axis, by):
    length = lax.axis_size(axis)
    pairs = [(i, i + by) for i in range(length) if 0 <= i + by < length]
    return lax.ppermute(array, axis, pairs)


def layer_norm(activ, gain_vec, bias_vec):
    row_mean = jnp.mean(activ, -1, keepdims=True)
    centred = activ - row_mean
    spread = jnp.mean(centred * centred, -1, keepdims=True)
    return centred * lax.rsqrt(spread + 1e-06) * gain_vec + bias_vec


def heads_of(matrix):
    return matrix.reshape(matrix.shape[0], HEADS, -1)


def dot_float(left, right):
    return jnp.dot(left, right, preferred_element_type=jnp.float32)


def norm_batch(values, gain_vec, bias_vec, number):
    sums = lax.psum((jnp.sum(values, 0), jnp.sum(values * values, 0)), ("dp", "seq"))
    col_mean = sums[0] / number
    col_var = sums[1] / number - col_mean * col_mean
    inv_std = lax.rsqrt(col_var + 1e-05)
    normed = (values - col_mean) * inv_std
    return (normed, inv_std, normed * gain_vec + bias_vec)


def batch_back(d_pre, normed, inv_std, gain_vec, number):
    grad_gain = jnp.sum(d_pre * normed, 0)
    grad_bias = jnp.sum(d_pre, 0)
    d_normed = d_pre * gain_vec
    sums = lax.psum((jnp.sum(d_normed, 0), jnp.sum(d_normed * normed, 0)), ("dp", "seq"))
    d_values = inv_std * (d_normed - sums[0] / number - normed * (sums[1] / number))
    return (d_values, grad_gain, grad_bias)


def conv_fwd(flat_low, weight):
    features = flat_low.shape[1]
    grid_rows = flat_low.shape[0] // SIDE
    grid = flat_low.reshape(grid_rows, SIDE, features)
    padded = padded_2(grid, (("seq", 0),), 1)
    padded = jnp.pad(padded, ((0, 0), (1, 1), (0, 0)))
    total = jnp.zeros((grid_rows * SIDE, features), jnp.float32)
    for row_tap in range(3):
        for col_tap in range(3):
            tap = 3 * row_tap + col_tap
            window = padded[row_tap : row_tap + grid_rows, col_tap : col_tap + SIDE].reshape(
                -1, features
            )
            total = total + dot_float(window, weight[tap * features : (tap + 1) * features])
    return (total, padded)


def send_rim(rim_rows, offset):
    return passed_along(rim_rows.astype(jnp.bfloat16), "seq", offset).astype(rim_rows.dtype)


def conv_back(padded, d_out_low, weight):
    features = d_out_low.shape[1]
    grid_rows = padded.shape[0] - 2
    d_padded = jnp.zeros((grid_rows + 2, SIDE + 2, features), jnp.float32)
    tap_grads = []
    for row_tap in range(3):
        for col_tap in range(3):
            tap = 3 * row_tap + col_tap
            tap_weight = weight[tap * features : (tap + 1) * features]
            window = padded[row_tap : row_tap + grid_rows, col_tap : col_tap + SIDE].reshape(
                -1, features
            )
            tap_grads.append(dot_float(window.T, d_out_low))
            spread = dot_float(d_out_low, tap_weight.T).reshape(grid_rows, SIDE, features)
            d_padded = d_padded + jnp.pad(
                spread, ((row_tap, 2 - row_tap), (col_tap, 2 - col_tap), (0, 0))
            )
    inner = d_padded[1 : grid_rows + 1, 1 : SIDE + 1]
    from_below = send_rim(d_padded[0, 1 : SIDE + 1], -1)
    from_above = send_rim(d_padded[grid_rows + 1, 1 : SIDE + 1], 1)
    inner = inner.at[grid_rows - 1].add(from_below).at[0].add(from_above)
    return (jnp.concatenate(tap_grads, 0), inner.reshape(-1, features))


def attend_block(queries, key_rows, value_rows, allowed, score_scale):
    scores = (
        jnp.einsum("qhd,khd->hqk", queries, key_rows, preferred_element_type=jnp.float32)
        * score_scale
    )
    scores = jnp.where(allowed[None], scores, -1000000000.0)
    row_max = jnp.max(scores, -1, keepdims=True)
    exponent = jnp.exp(scores - row_max)
    row_total = jnp.sum(exponent, -1, keepdims=True)
    softmax = (exponent / row_total).astype(jnp.bfloat16)
    outputs = jnp.einsum("hqk,khd->qhd", softmax, value_rows, preferred_element_type=jnp.float32)
    return (outputs, row_max + jnp.log(row_total))


def attend_back(queries, key_rows, value_rows, allowed, score_scale, grad_out, log_total):
    scores = (
        jnp.einsum("qhd,khd->hqk", queries, key_rows, preferred_element_type=jnp.float32)
        * score_scale
    )
    scores = jnp.where(allowed[None], scores, -1000000000.0)
    softmax = jnp.exp(scores - log_total)
    d_softmax = jnp.einsum("qhd,khd->hqk", grad_out, value_rows, preferred_element_type=jnp.float32)
    row_delta = jnp.sum(softmax * d_softmax, -1, keepdims=True)
    d_scores = (softmax * (d_softmax - row_delta)).astype(jnp.bfloat16)
    d_query = (
        jnp.einsum("hqk,khd->qhd", d_scores, key_rows, preferred_element_type=jnp.float32)
        * score_scale
    )
    d_keys = (
        jnp.einsum("hqk,qhd->khd", d_scores, queries, preferred_element_type=jnp.float32)
        * score_scale
    )
    d_values = jnp.einsum(
        "hqk,qhd->khd", softmax.astype(jnp.bfloat16), grad_out, preferred_element_type=jnp.float32
    )
    return (d_query, d_keys, d_values)


def run_attention(queries, key_rows, value_rows, allow_fn, score_scale):
    row_count = queries.shape[0]
    block_rows = min(512, row_count)
    block_count = row_count // block_rows
    query_blocks = queries.reshape(block_count, block_rows, queries.shape[1], queries.shape[2])
    starts = jnp.arange(block_count, dtype=jnp.int32) * block_rows

    def one_block(block_pair):
        return attend_block(
            block_pair[0], key_rows, value_rows, allow_fn(block_pair[1], block_rows), score_scale
        )

    outputs, log_total = lax.map(one_block, (query_blocks, starts))
    return (outputs.reshape(queries.shape), log_total)


def run_back(queries, key_rows, value_rows, allow_fn, score_scale, grad_out, log_total):
    row_count = queries.shape[0]
    block_rows = min(512, row_count)
    block_count = row_count // block_rows
    query_blocks = queries.reshape(block_count, block_rows, queries.shape[1], queries.shape[2])
    grad_blocks = grad_out.reshape(query_blocks.shape)
    starts = jnp.arange(block_count, dtype=jnp.int32) * block_rows

    def one_block(running, block_items):
        query_part, grad_part, total_part, first_row = block_items
        d_query, d_keys, d_values = attend_back(
            query_part,
            key_rows,
            value_rows,
            allow_fn(first_row, block_rows),
            score_scale,
            grad_part,
            total_part,
        )
        return ((running[0] + d_keys, running[1] + d_values), d_query)

    zero_grads = jnp.zeros(key_rows.shape, jnp.float32)
    sums_kv, d_query = lax.scan(
        one_block, (zero_grads, zero_grads), (query_blocks, grad_blocks, log_total, starts)
    )
    return (d_query.reshape(queries.shape), sums_kv[0], sums_kv[1])


def general_device(
    captions,
    patches,
    prefix,
    prefix_count,
    caption_len,
    cotangent,
    w_patch,
    w_conv,
    w_self_qkv,
    w_self_out,
    w_cross_q,
    w_cross_kv,
    w_cross_out,
    w_up,
    w_down,
    norm_params,
):
    gathered = (
        lax.all_gather(w_patch, "dp", axis=0, tiled=True),
        lax.all_gather(w_conv, "dp", axis=1, tiled=True),
        lax.all_gather(w_self_qkv, "dp", axis=0, tiled=True),
        lax.all_gather(w_self_out, "dp", axis=0, tiled=True),
        lax.all_gather(w_cross_q, "dp", axis=0, tiled=True),
        lax.all_gather(w_cross_kv, "dp", axis=0, tiled=True),
        lax.all_gather(w_cross_out, "dp", axis=0, tiled=True),
        lax.all_gather(w_up, "dp", axis=0, tiled=True),
        lax.all_gather(w_down, "dp", axis=0, tiled=True),
        lax.all_gather(norm_params, "dp", axis=1, tiled=True),
    )
    (
        full_patch,
        full_conv,
        full_qkv,
        full_sout,
        full_cq,
        full_ckv,
        full_cout,
        full_up,
        full_down,
        full_norms,
    ) = gathered
    norms = full_norms.astype(jnp.float32)
    features = full_sout.shape[0]
    score_scale = (features // HEADS) ** (-0.5)
    seq_count = lax.axis_size("seq")
    seq_index = lax.axis_index("seq")
    pixels = patches[0]
    stem_out = dot_float(pixels, full_patch)
    number = stem_out.shape[0] * lax.axis_size("dp") * seq_count
    normed_one, inv_one, pre_one = norm_batch(stem_out, norms[0], norms[1], number)
    first_out = jax.nn.gelu(pre_one)
    first_low = first_out.astype(jnp.bfloat16)
    conv_two, padded_two = conv_fwd(first_low, full_conv[0])
    normed_two, inv_two, pre_two = norm_batch(conv_two, norms[2], norms[3], number)
    second_out = first_out + jax.nn.gelu(pre_two)
    second_low = second_out.astype(jnp.bfloat16)
    conv_three, padded_three = conv_fwd(second_low, full_conv[1])
    normed_three, inv_three, pre_three = norm_batch(conv_three, norms[4], norms[5], number)
    third_out = second_out + jax.nn.gelu(pre_three)
    patch_low = third_out.astype(jnp.bfloat16)
    prefix_low = prefix[0]
    kv_prefix = dot_float(prefix_low, full_ckv).astype(jnp.bfloat16)
    kv_patch = dot_float(patch_low, full_ckv).astype(jnp.bfloat16)
    all_prefix, all_patch = (
        lax.all_gather(kv_prefix, "seq", axis=0, tiled=True),
        lax.all_gather(kv_patch, "seq", axis=0, tiled=True),
    )
    memory_kv = jnp.concatenate([all_prefix, all_patch], 0)
    mem_rows = memory_kv.shape[0]
    prefix_total = all_prefix.shape[0]
    mem_keys = heads_of(memory_kv[:, :features])
    mem_values = heads_of(memory_kv[:, features:])
    slot_ids = jnp.arange(mem_rows, dtype=jnp.int32)
    mem_allowed = (slot_ids >= prefix_total) | (slot_ids < prefix_count[0])

    def cross_allow(first_row, block_rows):
        return jnp.broadcast_to(mem_allowed[None], (block_rows, mem_rows))

    inputs = captions[0].astype(jnp.float32)
    row_count = inputs.shape[0]
    low_one = layer_norm(inputs, norms[6], norms[7]).astype(jnp.bfloat16)
    qkv = dot_float(low_one, full_qkv).astype(jnp.bfloat16)
    queries = heads_of(qkv[:, :features])
    own_keys = heads_of(qkv[:, features : 2 * features])
    own_values = heads_of(qkv[:, 2 * features :])
    key_parts = [own_keys]
    value_parts = [own_values]
    position_parts = [seq_index * row_count + jnp.arange(row_count, dtype=jnp.int32)]
    offset = 1
    got_keys, got_values = passed_along((own_keys, own_values), "seq", offset)
    key_parts.insert(0, got_keys)
    value_parts.insert(0, got_values)
    position_parts.insert(
        0, (seq_index - offset) * row_count + jnp.arange(row_count, dtype=jnp.int32)
    )
    all_keys = jnp.concatenate(key_parts, 0)
    all_values = jnp.concatenate(value_parts, 0)
    key_pos = jnp.concatenate(position_parts, 0)
    length_one = caption_len[0]

    def self_allow(first_row, block_rows):
        query_pos = seq_index * row_count + first_row + jnp.arange(block_rows, dtype=jnp.int32)
        return (
            (key_pos[None] <= query_pos[:, None])
            & (key_pos[None] >= 0)
            & (key_pos[None] < length_one)
        )

    self_out, self_total = run_attention(queries, all_keys, all_values, self_allow, score_scale)
    self_low = self_out.reshape(row_count, features).astype(jnp.bfloat16)
    after_self = inputs + dot_float(self_low, full_sout)
    low_two = layer_norm(after_self, norms[8], norms[9]).astype(jnp.bfloat16)
    cross_flat = dot_float(low_two, full_cq).astype(jnp.bfloat16)
    cross_q = heads_of(cross_flat)
    cross_out, cross_total = run_attention(cross_q, mem_keys, mem_values, cross_allow, score_scale)
    cross_low = cross_out.reshape(row_count, features).astype(jnp.bfloat16)
    after_cross = after_self + dot_float(cross_low, full_cout)
    low_three = layer_norm(after_cross, norms[10], norms[11]).astype(jnp.bfloat16)
    up_proj = dot_float(low_three, full_up)
    hidden_low = jax.nn.gelu(up_proj).astype(jnp.bfloat16)
    result = after_cross + dot_float(hidden_low, full_down)
    back_weights = (
        lax.all_gather(w_patch, "dp", axis=0, tiled=True),
        lax.all_gather(w_conv, "dp", axis=1, tiled=True),
        lax.all_gather(w_self_qkv, "dp", axis=0, tiled=True),
        lax.all_gather(w_self_out, "dp", axis=0, tiled=True),
        lax.all_gather(w_cross_q, "dp", axis=0, tiled=True),
        lax.all_gather(w_cross_kv, "dp", axis=0, tiled=True),
        lax.all_gather(w_cross_out, "dp", axis=0, tiled=True),
        lax.all_gather(w_up, "dp", axis=0, tiled=True),
        lax.all_gather(w_down, "dp", axis=0, tiled=True),
        lax.all_gather(norm_params, "dp", axis=1, tiled=True),
    )
    (
        back_patch,
        back_conv,
        back_qkv,
        back_sout,
        back_cq,
        back_ckv,
        back_cout,
        back_up,
        back_down,
        back_norms,
    ) = back_weights
    bnorms = back_norms.astype(jnp.float32)
    out_grad = cotangent[0].astype(jnp.float32)
    grad_low = cotangent[0]
    grad_down = dot_float(hidden_low.T, grad_low)
    d_hidden = dot_float(grad_low, back_down.T)
    unused_gelu, gelu_back = jax.vjp(jax.nn.gelu, up_proj)
    d_upper = gelu_back(d_hidden)[0].astype(jnp.bfloat16)
    grad_up = dot_float(low_three.T, d_upper)
    unused_three, norm_back_three = jax.vjp(layer_norm, after_cross, bnorms[10], bnorms[11])
    d_three, grad_gain_three, grad_bias_three = norm_back_three(dot_float(d_upper, back_up.T))
    d_after_cross = out_grad + d_three
    cross_grad_low = d_after_cross.astype(jnp.bfloat16)
    grad_cout = dot_float(cross_low.T, cross_grad_low)
    d_cross = heads_of(dot_float(cross_grad_low, back_cout.T).astype(jnp.bfloat16))
    d_cross_q, d_mem_keys, d_mem_values = run_back(
        cross_q, mem_keys, mem_values, cross_allow, score_scale, d_cross, cross_total
    )
    d_cross_low = d_cross_q.reshape(row_count, features).astype(jnp.bfloat16)
    grad_cq = dot_float(low_two.T, d_cross_low)
    unused_two, norm_back_two = jax.vjp(layer_norm, after_self, bnorms[8], bnorms[9])
    d_two, grad_gain_two, grad_bias_two = norm_back_two(dot_float(d_cross_low, back_cq.T))
    d_after_self = d_after_cross + d_two
    d_memory = jnp.concatenate(
        [d_mem_keys.reshape(mem_rows, features), d_mem_values.reshape(mem_rows, features)], 1
    )
    mine_prefix, mine_patch = (
        lax.psum_scatter(
            d_memory[:prefix_total].astype(jnp.bfloat16), "seq", scatter_dimension=0, tiled=True
        ).astype(jnp.float32),
        lax.psum_scatter(
            d_memory[prefix_total:].astype(jnp.bfloat16), "seq", scatter_dimension=0, tiled=True
        ).astype(jnp.float32),
    )
    mine_prefix_low = mine_prefix.astype(jnp.bfloat16)
    mine_patch_low = mine_patch.astype(jnp.bfloat16)
    grad_ckv = dot_float(prefix_low.T, mine_prefix_low) + dot_float(patch_low.T, mine_patch_low)
    prefix_back = dot_float(mine_prefix_low, back_ckv.T)
    d_third = dot_float(mine_patch_low, back_ckv.T)
    unused_act_three, act_back_three = jax.vjp(jax.nn.gelu, pre_three)
    d_conv_three, grad_gain_bn3, grad_bias_bn3 = batch_back(
        act_back_three(d_third)[0], normed_three, inv_three, bnorms[4], number
    )
    grad_conv_one, d_second_in = conv_back(
        padded_three, d_conv_three.astype(jnp.bfloat16), back_conv[1]
    )
    d_second = d_third + d_second_in
    unused_act_two, act_back_two = jax.vjp(jax.nn.gelu, pre_two)
    d_conv_two, grad_gain_bn2, grad_bias_bn2 = batch_back(
        act_back_two(d_second)[0], normed_two, inv_two, bnorms[2], number
    )
    grad_conv_zero, d_first_in = conv_back(
        padded_two, d_conv_two.astype(jnp.bfloat16), back_conv[0]
    )
    d_first = d_second + d_first_in
    unused_act_one, act_back_one = jax.vjp(jax.nn.gelu, pre_one)
    d_stem, grad_gain_bn1, grad_bias_bn1 = batch_back(
        act_back_one(d_first)[0], normed_one, inv_one, bnorms[0], number
    )
    grad_patch = dot_float(pixels.T, d_stem.astype(jnp.bfloat16))
    grad_conv = jnp.stack([grad_conv_zero, grad_conv_one])
    self_grad_low = d_after_self.astype(jnp.bfloat16)
    grad_sout = dot_float(self_low.T, self_grad_low)
    d_self = heads_of(dot_float(self_grad_low, back_sout.T).astype(jnp.bfloat16))
    d_query, d_all_keys, d_all_values = run_back(
        queries, all_keys, all_values, self_allow, score_scale, d_self, self_total
    )
    own_start = (seq_count - 1) * row_count
    own_dkeys = d_all_keys[own_start:]
    own_dvalues = d_all_values[own_start:]
    offset = 1
    piece_start = (seq_count - 1 - offset) * row_count
    back_keys = passed_along(
        d_all_keys[piece_start : piece_start + row_count].astype(jnp.bfloat16), "seq", -offset
    ).astype(jnp.float32)
    back_values = passed_along(
        d_all_values[piece_start : piece_start + row_count].astype(jnp.bfloat16), "seq", -offset
    ).astype(jnp.float32)
    own_dkeys = own_dkeys + back_keys
    own_dvalues = own_dvalues + back_values
    d_qkv = jnp.concatenate(
        [
            d_query.reshape(row_count, features),
            own_dkeys.reshape(row_count, features),
            own_dvalues.reshape(row_count, features),
        ],
        1,
    ).astype(jnp.bfloat16)
    grad_qkv = dot_float(low_one.T, d_qkv)
    unused_one, norm_back_one = jax.vjp(layer_norm, inputs, bnorms[6], bnorms[7])
    d_one, grad_gain_one, grad_bias_one = norm_back_one(dot_float(d_qkv, back_qkv.T))
    d_inputs = d_after_self + d_one
    grad_norms = jnp.stack(
        [
            grad_gain_bn1,
            grad_bias_bn1,
            grad_gain_bn2,
            grad_bias_bn2,
            grad_gain_bn3,
            grad_bias_bn3,
            grad_gain_one,
            grad_bias_one,
            grad_gain_two,
            grad_bias_two,
            grad_gain_three,
            grad_bias_three,
        ]
    )
    shard_sums = (
        lax.psum_scatter(grad_patch, "dp", scatter_dimension=0, tiled=True),
        lax.psum_scatter(grad_conv, "dp", scatter_dimension=1, tiled=True),
        lax.psum_scatter(grad_qkv, "dp", scatter_dimension=0, tiled=True),
        lax.psum_scatter(grad_sout, "dp", scatter_dimension=0, tiled=True),
        lax.psum_scatter(grad_cq, "dp", scatter_dimension=0, tiled=True),
        lax.psum_scatter(grad_ckv, "dp", scatter_dimension=0, tiled=True),
        lax.psum_scatter(grad_cout, "dp", scatter_dimension=0, tiled=True),
        lax.psum_scatter(grad_up, "dp", scatter_dimension=0, tiled=True),
        lax.psum_scatter(grad_down, "dp", scatter_dimension=0, tiled=True),
        lax.psum_scatter(grad_norms, "dp", scatter_dimension=1, tiled=True),
    )
    totals = (
        lax.psum(shard_sums[0].astype(jnp.bfloat16), "seq").astype(jnp.float32),
        lax.psum(shard_sums[1].astype(jnp.bfloat16), "seq").astype(jnp.float32),
        lax.psum(shard_sums[2].astype(jnp.bfloat16), "seq").astype(jnp.float32),
        lax.psum(shard_sums[3].astype(jnp.bfloat16), "seq").astype(jnp.float32),
        lax.psum(shard_sums[4].astype(jnp.bfloat16), "seq").astype(jnp.float32),
        lax.psum(shard_sums[5].astype(jnp.bfloat16), "seq").astype(jnp.float32),
        lax.psum(shard_sums[6].astype(jnp.bfloat16), "seq").astype(jnp.float32),
        lax.psum(shard_sums[7].astype(jnp.bfloat16), "seq").astype(jnp.float32),
        lax.psum(shard_sums[8].astype(jnp.bfloat16), "seq").astype(jnp.float32),
        lax.psum(shard_sums[9].astype(jnp.bfloat16), "seq").astype(jnp.float32),
    )
    return (
        result[None].astype(jnp.bfloat16),
        d_inputs[None].astype(jnp.bfloat16),
        prefix_back[None].astype(jnp.bfloat16),
        totals[0],
        totals[1],
        totals[2],
        totals[3],
        totals[4],
        totals[5],
        totals[6],
        totals[7],
        totals[8],
        totals[9],
    )


PAIR = 128


def head_lanes(array, which, width):
    lanes = lax.broadcasted_iota(jnp.int32, array.shape, 1)
    return jnp.where((lanes >= which * width) & (lanes < (which + 1) * width), array, 0)


def scores_t(keys, q_head):
    return lax.dot_general(
        keys, q_head, (((1,), (1,)), ((), ())), preferred_element_type=jnp.float32
    )


def masked_scores(kind, info_ref, ok_ref, keys, q_head):
    if kind == "cross":
        scores = scores_t(keys, q_head)
        return jnp.where(ok_ref[:, 0:1] > 0, scores, -1e9)
    half = keys.shape[0] // 2
    before = scores_t(keys[:half], q_head)
    own = scores_t(keys[half:], q_head)
    before = jnp.where(info_ref[0] > 0, before, -1e9)
    key_at = lax.broadcasted_iota(jnp.int32, own.shape, 0)
    query_at = lax.broadcasted_iota(jnp.int32, own.shape, 1)
    own = jnp.where((key_at <= query_at) & (key_at < info_ref[1]), own, -1e9)
    return jnp.concatenate([before, own], 0)


def attend_body(kind, width, info_ref, ok_ref, q_ref, k_ref, v_ref, o_ref, lse_ref):
    keys, values = k_ref[...], v_ref[...]
    outs = []
    for which in range(PAIR // width):
        q_head = head_lanes(q_ref[...], which, width)
        scores = masked_scores(kind, info_ref, ok_ref, keys, q_head)
        top = jnp.max(scores, 0, keepdims=True)
        weights = jnp.exp(scores - top)
        total = jnp.sum(weights, 0, keepdims=True)
        lse_ref[0, which : which + 1, :] = top + jnp.log(total)
        out_t = lax.dot_general(
            head_lanes(values, which, width),
            weights.astype(LOW),
            (((0,), (0,)), ((), ())),
            preferred_element_type=jnp.float32,
        )
        outs.append(out_t / total)
    o_ref[...] = (outs[0] + outs[1]).T.astype(o_ref.dtype)


def attend_back_body(
    kind, width, scale, info_ref, ok_ref, q_ref, k_ref, v_ref, do_ref, lse_ref, dq_ref, dk_ref, dv_ref
):
    keys, values = k_ref[...], v_ref[...]
    dq_t, dk, dv = None, None, None
    for which in range(PAIR // width):
        q_head = head_lanes(q_ref[...], which, width)
        do_head = head_lanes(do_ref[...], which, width)
        scores = masked_scores(kind, info_ref, ok_ref, keys, q_head)
        probs = jnp.exp(scores - lse_ref[0, which : which + 1, :])
        d_probs = scores_t(values, do_head)
        delta = jnp.sum(probs * d_probs, 0, keepdims=True)
        ds = (probs * (d_probs - delta)).astype(LOW)
        part_k = jnp.dot(ds, q_head, preferred_element_type=jnp.float32)
        part_v = jnp.dot(probs.astype(LOW), do_head, preferred_element_type=jnp.float32)
        part_q = lax.dot_general(
            head_lanes(keys, which, width),
            ds,
            (((0,), (0,)), ((), ())),
            preferred_element_type=jnp.float32,
        )
        dk = part_k if dk is None else dk + part_k
        dv = part_v if dv is None else dv + part_v
        dq_t = part_q if dq_t is None else dq_t + part_q
    dq_ref[...] = (dq_t * scale).T.astype(dq_ref.dtype)
    dk_ref[...] = dk.astype(dk_ref.dtype)
    dv_ref[...] = dv.astype(dv_ref.dtype)


def attention_specs(rows, keys, ok):
    return [
        pl.BlockSpec(memory_space=pltpu.SMEM),
        pl.BlockSpec(ok.shape, lambda i: (0, 0)),
        pl.BlockSpec((rows, PAIR), lambda i: (0, i)),
        pl.BlockSpec((keys, PAIR), lambda i: (0, i)),
        pl.BlockSpec((keys, PAIR), lambda i: (0, i)),
    ]


def attend(kind, info, ok, q, k, v):
    rows, features = q.shape
    keys = k.shape[0]
    width = features // HEADS
    pairs = features // PAIR
    return pl.pallas_call(
        functools.partial(attend_body, kind, width),
        name=kind + "_attend",
        grid=(pairs,),
        in_specs=attention_specs(rows, keys, ok),
        out_specs=(
            pl.BlockSpec((rows, PAIR), lambda i: (0, i)),
            pl.BlockSpec((1, 8, rows), lambda i: (i, 0, 0)),
        ),
        out_shape=(
            jax.ShapeDtypeStruct((rows, features), LOW),
            jax.ShapeDtypeStruct((pairs, 8, rows), jnp.float32),
        ),
        compiler_params=BIG,
        cost_estimate=pl.CostEstimate(
            flops=4 * rows * keys * features, bytes_accessed=2 * (2 * rows + 2 * keys) * features,
            transcendentals=rows * keys * HEADS,
        ),
    )(info, ok, q, k, v)


def attend_grads(kind, info, ok, q, k, v, d_out, lse, scale):
    rows, features = q.shape
    keys = k.shape[0]
    width = features // HEADS
    pairs = features // PAIR
    return pl.pallas_call(
        functools.partial(attend_back_body, kind, width, scale),
        name=kind + "_attend_back",
        grid=(pairs,),
        in_specs=attention_specs(rows, keys, ok)
        + [
            pl.BlockSpec((rows, PAIR), lambda i: (0, i)),
            pl.BlockSpec((1, 8, rows), lambda i: (i, 0, 0)),
        ],
        out_specs=(
            pl.BlockSpec((rows, PAIR), lambda i: (0, i)),
            pl.BlockSpec((keys, PAIR), lambda i: (0, i)),
            pl.BlockSpec((keys, PAIR), lambda i: (0, i)),
        ),
        out_shape=(
            jax.ShapeDtypeStruct((rows, features), LOW),
            jax.ShapeDtypeStruct((keys, features), LOW),
            jax.ShapeDtypeStruct((keys, features), LOW),
        ),
        compiler_params=BIG,
        cost_estimate=pl.CostEstimate(
            flops=10 * rows * keys * features, bytes_accessed=2 * (3 * rows + 6 * keys) * features,
            transcendentals=rows * keys * HEADS,
        ),
    )(info, ok, q, k, v, d_out, lse)


def weight_grads_body(jobs, targets, owners, *refs):
    count = len(refs) - 4
    ins, (o_ref, left_ref, right_ref, sum_ref) = refs[:count], refs[count:]
    step = pl.program_id(0)
    for at, (left, right, rows, row_at, left_col, right_col) in enumerate(jobs):

        @pl.when(step == at)
        def _():
            size = left_ref.shape[1]
            left_ref[:rows] = ins[left][row_at : row_at + rows, left_col : left_col + size]
            right_ref[:rows] = ins[right][row_at : row_at + rows, right_col : right_col + size]
            if rows < left_ref.shape[0]:
                left_ref[rows:] = jnp.zeros((left_ref.shape[0] - rows, size), left_ref.dtype)
                right_ref[rows:] = jnp.zeros((left_ref.shape[0] - rows, size), left_ref.dtype)

    product = lax.dot_general(
        left_ref[...], right_ref[...], (((0,), (0,)), ((), ())), preferred_element_type=jnp.float32
    )
    for at, target in enumerate(targets):
        if at and targets[at - 1] == target:

            @pl.when(step == at)
            def _():
                sum_ref[...] += product

        else:

            @pl.when(step == at)
            def _():
                sum_ref[...] = product

    put_grads(owners, targets, step, o_ref, sum_ref)


def put_grads(owners, targets, step, o_ref, sum_ref):
    total = sum_ref[...].astype(o_ref.dtype)
    if owners == "mlp":
        tall = total.shape[0] // 4

        @pl.when(step < 4)
        def _():
            for part in range(4):
                o_ref[2 * (4 * step + part)] = total[tall * part : tall * (part + 1)]

        @pl.when(step >= 4)
        def _():
            short = total.shape[0] // 16
            start = pl.multiple_of(short * (step - 4), short)
            for a in range(16):
                o_ref[2 * a + 1, pl.ds(start, short)] = total[short * a : short * (a + 1)]

    else:
        first_twice = len(targets) - 4
        target = jnp.where(step < first_twice, step, first_twice + (step - first_twice) // 2)
        short = total.shape[0] // 16
        start = pl.multiple_of(short * lax.rem(target, 4), short)
        for a in range(16):
            o_ref[2 * a + target // 4, pl.ds(start, short)] = total[short * a : short * (a + 1)]


def weight_grads(jobs, targets, owners, arrays, features, rows):
    return pl.pallas_call(
        functools.partial(weight_grads_body, tuple(jobs), tuple(targets), owners),
        name="weight_grads",
        grid=(len(jobs),),
        in_specs=[pl.BlockSpec(memory_space=pltpu.VMEM)] * len(arrays),
        out_specs=pl.BlockSpec(memory_space=pltpu.VMEM),
        out_shape=jax.ShapeDtypeStruct((32, features // 4, features), LOW),
        scratch_shapes=[
            pltpu.VMEM((rows, features), LOW),
            pltpu.VMEM((rows, features), LOW),
            pltpu.VMEM((features, features), jnp.float32),
        ],
        compiler_params=BIG,
        cost_estimate=pl.CostEstimate(
            flops=2 * len(jobs) * rows * features * features,
            bytes_accessed=2 * 8 * features * features,
            transcendentals=0,
        ),
    )(*arrays)


def low_dot(left, right):
    return dot_float(left, right).astype(LOW)


def dot_t(left, right):
    return lax.dot_general(left, right, (((1,), (1,)), ((), ())), preferred_element_type=jnp.float32)


def t_dot(left, right):
    return lax.dot_general(left, right, (((0,), (0,)), ((), ())), preferred_element_type=jnp.float32)


def stem_weight_blocks(w_conv, w_patch, norm_params, s):
    features = w_patch.shape[1]
    flat = jnp.concatenate([w_conv.reshape(-1, features), w_patch], 0).T
    blocks = slots_to_devices(flat.reshape(PORTIONS, 32, GROUP, flat.shape[1]))
    blocks = blocks.reshape(16, 2, PORTIONS * GROUP, flat.shape[1])
    blocks = lax.dynamic_index_in_dim(blocks, s, 1, keepdims=False)
    rows = PORTIONS * GROUP
    extra = jnp.pad(norm_params, ((0, rows - norm_params.shape[0]), (0, 0)))
    blocks = jnp.concatenate([blocks, jnp.broadcast_to(extra, (16,) + extra.shape)], 2)
    return blocks


def stem_weights(got, w_conv, w_patch, norm_params):
    depth, conv_rows, features = w_conv.shape
    rows = PORTIONS * GROUP
    convs = []
    for layer in range(depth):
        part = got[:, :, layer * conv_rows : (layer + 1) * conv_rows]
        part = part.transpose(1, 0, 2).reshape(rows, 9, features).transpose(1, 0, 2)
        convs.append(part.reshape(9 * rows, features))
    at = depth * conv_rows
    patch = got[:, :, at : at + w_patch.shape[0]].transpose(1, 0, 2).reshape(rows, -1)
    norms = got[:, : norm_params.shape[0], at + w_patch.shape[0] :]
    return convs, patch, norms.transpose(1, 0, 2).reshape(norm_params.shape[0], -1)


def own_columns(norms):
    bits = my_bits()
    cut = norms.reshape(norms.shape[0], PORTIONS, 32, GROUP)
    parts = [
        lax.dynamic_index_in_dim(cut[:, p], slot_of(bits, p), 1, keepdims=False)
        for p in range(PORTIONS)
    ]
    mine = jnp.concatenate(parts, 1).T
    return jnp.pad(mine, ((0, 0), (0, 128 - mine.shape[1])))


def fast_device(
    captions,
    patches,
    prefix,
    prefix_count,
    caption_len,
    cotangent,
    w_patch,
    w_conv,
    w_self_qkv,
    w_self_out,
    w_cross_q,
    w_cross_kv,
    w_cross_out,
    w_up,
    w_down,
    norm_params,
):
    a_index, s_index = lax.axis_index("dp"), lax.axis_index("seq")
    examples, halves = 16, 2
    features = w_self_out.shape[1]
    score_scale = (features // HEADS) ** (-0.5)

    def chunks(w):
        return [w[:, i * features : (i + 1) * features] for i in range(w.shape[1] // features)]

    shard_rows = w_patch.shape[0]
    pieces = [(0, 0, features * i) for i in range(3)] + [(1, 0, 0), (2, 0, 0)]
    pieces += [(3, 0, 0), (3, 0, features), (4, 0, 0)]
    pieces += [(5, 0, features * i) for i in range(4)] + [(6, shard_rows * i, 0) for i in range(4)]
    all_w = pack(
        pieces,
        [w_self_qkv, w_self_out, w_cross_q, w_cross_kv, w_cross_out, w_up, w_down],
        shard_rows,
        features,
    )
    all_w = lax.all_gather(all_w, "dp", axis=1, tiled=True)
    qkv_w = all_w[:3]
    sout_w, cq_w, ck_w, cv_w, cout_w = (all_w[3 + i] for i in range(5))
    up_ws = [all_w[8 + i] for i in range(4)]
    down_w = all_w[12:].reshape(4, examples, -1, features).transpose(1, 0, 2, 3)
    down_w = down_w.reshape(4 * features, features)
    pixels, got_blocks, earlier, prefix_other = gather_many(
        [],
        [patches[0]],
        [stem_weight_blocks(w_conv, w_patch, norm_params, s_index)],
        [captions[0], prefix[0]],
        0,
    )

    convs, patch_w, norms_low = stem_weights(got_blocks, w_conv, w_patch, norm_params)
    norms = norms_low.astype(jnp.float32)
    own_gb = own_columns(norms[:6])
    own_cells = patches.shape[1]
    number = own_cells * examples * halves
    cells = -(-number // CHUNK) * CHUNK
    rows_own = PORTIONS * GROUP
    grid = halves * own_cells
    masks = jnp.asarray(tap_masks(cells, examples))
    def to_channels(by_row, cid):
        blocks = slots_to_devices(by_row.T.reshape(PORTIONS, 32, GROUP, by_row.shape[0]))
        return exchange_all(blocks.reshape(32, rows_own, by_row.shape[0]), cid)

    def laid_out(blocks):
        flat = blocks.transpose(1, 0, 2).reshape(rows_own, number)
        return jnp.pad(flat, ((0, 0), (0, cells - number)))

    n1, r1, y1, x1 = first_block(pixels, patch_w, own_gb, masks, number)
    (x1_all,) = gather_many([x1], [], [], [], 2)
    x1_all = x1_all.reshape(features, cells)
    n2, r2, y2, x2 = conv_block(1, x1_all, convs[0], own_gb, masks, y1, number)
    inputs = captions[0].astype(jnp.float32)
    row_count = inputs.shape[0]
    earlier = earlier.astype(jnp.float32)
    low_one = layer_norm(inputs, norms[6], norms[7]).astype(LOW)
    low_all = jnp.concatenate(
        [layer_norm(earlier, norms[6], norms[7]).astype(LOW), low_one], 0
    )
    queries = (dot_float(low_one, qkv_w[0]).astype(LOW) * score_scale).astype(LOW)
    all_keys, all_values = low_dot(low_all, qkv_w[1]), low_dot(low_all, qkv_w[2])
    info = jnp.stack([s_index, caption_len[0] - s_index * row_count]).astype(jnp.int32)
    no_ok = jnp.zeros((8, 128), jnp.float32)
    self_low, self_lse, x2_all = attend_gather(info, no_ok, queries, all_keys, all_values, x2, 3)
    x2_all = x2_all.reshape(features, cells)
    n3, r3, y3, x3 = conv_block(2, x2_all, convs[1], own_gb, masks, y2, number)
    out_blocks = x3.reshape(rows_own, cells)[:, :number].reshape(rows_own, examples, grid)
    out_blocks = jnp.broadcast_to(
        out_blocks.transpose(1, 0, 2)[:, None], (examples, halves, rows_own, grid)
    )
    in_blocks = exchange_all(out_blocks.reshape(32, rows_own, grid), 4)
    patch_all = devices_to_slots(in_blocks.reshape(32, PORTIONS, GROUP, grid))
    patch_all = patch_all.reshape(features, grid).T

    prefix_own = prefix[0]
    prefix_half = prefix_own.shape[0]
    first_half = s_index == 0
    prefix_all = jnp.concatenate(
        [
            jnp.where(first_half, prefix_own, prefix_other),
            jnp.where(first_half, prefix_other, prefix_own),
        ],
        0,
    )
    memory = jnp.concatenate([prefix_all, patch_all], 0)
    mem_rows = memory.shape[0]
    prefix_total = prefix_all.shape[0]
    mem_padded = jnp.pad(memory, ((0, -mem_rows % 128), (0, 0)))
    mem_keys = low_dot(mem_padded, ck_w)
    mem_values = low_dot(mem_padded, cv_w)
    slot_ids = jnp.arange(mem_padded.shape[0], dtype=jnp.int32)
    mem_ok = (slot_ids < mem_rows) & ((slot_ids >= prefix_total) | (slot_ids < prefix_count[0]))
    mem_ok = jnp.broadcast_to(mem_ok.astype(jnp.float32)[:, None], (mem_padded.shape[0], 128))

    after_self = inputs + dot_float(self_low, sout_w)
    low_two = layer_norm(after_self, norms[8], norms[9]).astype(LOW)
    cross_q = (dot_float(low_two, cq_w).astype(LOW) * score_scale).astype(LOW)
    cross_low, cross_lse = attend("cross", info, mem_ok, cross_q, mem_keys, mem_values)
    after_cross = after_self + dot_float(cross_low, cout_w)
    low_three = layer_norm(after_cross, norms[10], norms[11]).astype(LOW)
    up_proj = jnp.concatenate([dot_float(low_three, w) for w in up_ws], 1)
    hidden = jax.nn.gelu(up_proj).astype(LOW)
    result = after_cross + dot_float(hidden, down_w)

    out_grad = cotangent[0].astype(jnp.float32)
    grad_low = cotangent[0]
    d_upper = (dot_t(grad_low, down_w) * gelu_slope(up_proj)).astype(LOW)
    jobs = [(0, 1, row_count, 0, features * q, 0) for q in range(4)]
    jobs += [(2, 3, row_count, 0, 0, features * j) for j in range(4)]
    mlp_parts = weight_grads(
        jobs, range(8), "mlp", [hidden, grad_low, low_three, d_upper], features, row_count
    )
    mlp_parts, d_upper = lax.optimization_barrier((mlp_parts, d_upper))
    d_normed = sum(dot_t(d, w) for d, w in zip(chunks(d_upper), up_ws))
    unused_three, norm_back_three = jax.vjp(layer_norm, after_cross, norms[10], norms[11])
    d_three, grad_gain_three, grad_bias_three = norm_back_three(d_normed)

    def scattered(parts):
        parts = parts.reshape(examples, -1, features)
        return lax.psum_scatter(parts, "dp", scatter_dimension=0, tiled=True)[0]

    mlp_own = scattered(mlp_parts)
    d_after_cross = out_grad + d_three
    cross_grad_low = d_after_cross.astype(LOW)
    d_cross = dot_t(cross_grad_low, cout_w).astype(LOW)
    d_cross_low, d_mem_keys, d_mem_values = attend_grads(
        "cross", info, mem_ok, cross_q, mem_keys, mem_values, d_cross, cross_lse, score_scale
    )
    unused_two, norm_back_two = jax.vjp(layer_norm, after_self, norms[8], norms[9])
    d_two, grad_gain_two, grad_bias_two = norm_back_two(dot_t(d_cross_low, cq_w))
    d_after_self = d_after_cross + d_two
    d_mem_rows = dot_t(d_mem_keys[:mem_rows], ck_w) + dot_t(d_mem_values[:mem_rows], cv_w)
    d_prefix = d_mem_rows[:prefix_total].reshape(halves, prefix_half, features)
    prefix_back = lax.dynamic_index_in_dim(d_prefix, s_index, 0, keepdims=False)
    away = lax.dynamic_index_in_dim(d_prefix, 1 - s_index, 0, keepdims=False).astype(LOW)
    d_third = d_mem_rows[prefix_total:].astype(LOW)

    self_grad_low = d_after_self.astype(LOW)
    d_self = dot_t(self_grad_low, sout_w).astype(LOW)
    d_query, d_all_keys, d_all_values = attend_grads(
        "self", info, no_ok, queries, all_keys, all_values, d_self, self_lse, score_scale
    )
    d_normed_all = dot_t(d_all_keys, qkv_w[1]) + dot_t(d_all_values, qkv_w[2])
    from_later = lax.ppermute(d_normed_all[:row_count].astype(LOW), "seq", [(1, 0)])
    arrays = [cross_low, cross_grad_low, low_two, d_cross_low, mem_padded, d_mem_keys, d_mem_values]
    arrays += [self_low, self_grad_low, low_all, d_query, d_all_keys, d_all_values, low_one]
    mem_count = mem_padded.shape[0]
    jobs = [
        (0, 1, row_count, 0, 0, 0),
        (2, 3, row_count, 0, 0, 0),
        (4, 5, mem_count, 0, 0, 0),
        (4, 6, mem_count, 0, 0, 0),
        (7, 8, row_count, 0, 0, 0),
        (13, 10, row_count, 0, 0, 0),
        (9, 11, row_count, 0, 0, 0),
        (9, 11, row_count, row_count, 0, 0),
        (9, 12, row_count, 0, 0, 0),
        (9, 12, row_count, row_count, 0, 0),
    ]
    rest_parts = weight_grads(
        jobs, (0, 1, 2, 3, 4, 5, 6, 6, 7, 7), "rest", arrays, features, row_count
    )
    rest_own = scattered(rest_parts)

    d_y3 = to_channels(d_third, 6).astype(jnp.float32)
    d_y3 = laid_out(jnp.sum(d_y3.reshape(examples, halves, rows_own, grid), 1))

    def back_through(layer, d_y, n, r, x_all, w, swaps, cid):
        dx, grad_w, sums = conv_block_back(layer, d_y, n, r, own_gb, masks, x_all, w.T, number)
        total, *got = reduce_all(dx.reshape(PORTIONS, 32, GROUP, cells), swaps, cid)
        grad_w = grad_w.reshape(9, rows_own, features).transpose(1, 0, 2)
        grad_w = grad_w.reshape(rows_own, examples, -1).transpose(1, 0, 2)
        return d_y + total.reshape(rows_own, cells), grad_w, sums, got

    d_y2, grad_conv_one, sums3, _ = back_through(2, d_y3, n3, r3, x2_all, convs[1], [], 7)
    d_y2, mlp_own = lax.optimization_barrier((d_y2, mlp_own))
    d_y1, grad_conv_zero, sums2, got = back_through(
        1, d_y2, n2, r2, x1_all, convs[0], [grad_conv_one, away], 8
    )
    got_one, prefix_part = got
    prefix_back = prefix_back + prefix_part.astype(jnp.float32)
    from_later, d_y1 = lax.optimization_barrier((from_later, d_y1))
    d_normed_one = dot_t(d_query, qkv_w[0]) + d_normed_all[row_count:]
    d_normed_one = d_normed_one + from_later.astype(jnp.float32)
    unused_one, norm_back_one = jax.vjp(layer_norm, inputs, norms[6], norms[7])
    d_one, grad_gain_one, grad_bias_one = norm_back_one(d_normed_one)
    d_inputs = d_after_self + d_one
    grad_patch, sums1 = first_block_back(d_y1, n1, r1, own_gb, pixels, number)
    grad_patch = grad_patch.reshape(rows_own, examples, -1).transpose(1, 0, 2)
    patch_rows = grad_patch.shape[2]
    bn_grads = jnp.concatenate([sums1[:, :2], sums2[:, :2], sums3[:, :2]], 1).astype(LOW)
    ln_grads = jnp.stack(
        [
            grad_gain_one,
            grad_bias_one,
            grad_gain_two,
            grad_bias_two,
            grad_gain_three,
            grad_bias_three,
        ]
    ).astype(LOW)
    ln_count = ln_grads.shape[0]
    ln_blocks = ln_grads.reshape(ln_count, examples, -1).transpose(1, 0, 2)
    ln_blocks = jnp.pad(ln_blocks, ((0, 0), (0, rows_own - ln_count), (0, 0)))
    send_blocks = jnp.concatenate(
        [
            grad_conv_zero,
            grad_patch,
            jnp.broadcast_to(bn_grads, (examples,) + bn_grads.shape),
            ln_blocks,
        ],
        2,
    )
    def by_sender(blocks):
        return blocks.transpose(1, 0, 2, 3).reshape(32, rows_own, -1)

    def channels_last(blocks):
        mixed = devices_to_slots(blocks.reshape(32, PORTIONS, GROUP, -1))
        return mixed.reshape(features, -1)

    mlp_other = lax.ppermute(mlp_own, "seq", [(0, 1), (1, 0)])
    got, rest_other = swap_both(send_blocks, rest_own, 9)
    got = by_sender(got)
    width = w_conv.shape[1] + patch_rows
    mixed = channels_last(got[:, :, : width + 6])
    conv_rows = w_conv.shape[1]
    stem_grads = jnp.concatenate(
        [mixed[:, :conv_rows], channels_last(by_sender(got_one)), mixed[:, conv_rows:width]], 1
    )
    stem_grads = stem_grads.T.astype(jnp.float32)
    bn_part = lax.dynamic_slice_in_dim(mixed[:, width:], a_index * patch_rows, patch_rows, 0)
    ln_part = jnp.sum(got[:, :ln_count, width + 6 :].astype(jnp.float32), 0)
    norm_grads = jnp.concatenate([bn_part.T.astype(jnp.float32), ln_part], 0)

    mlp_sum = mlp_own.astype(jnp.float32) + mlp_other.astype(jnp.float32)
    rest_sum = rest_own.astype(jnp.float32) + rest_other.astype(jnp.float32)
    down_sum = mlp_sum[: 4 * shard_rows]
    up_sum = [mlp_sum[(4 + i) * shard_rows : (5 + i) * shard_rows] for i in range(4)]
    rest = [rest_sum[i * shard_rows : (i + 1) * shard_rows] for i in range(8)]
    return (
        result[None].astype(LOW),
        d_inputs[None].astype(LOW),
        prefix_back[None].astype(LOW),
        stem_grads[2 * conv_rows :],
        stem_grads[: 2 * conv_rows].reshape(w_conv.shape),
        jnp.concatenate(rest[5:], 1),
        rest[4],
        rest[1],
        jnp.concatenate(rest[2:4], 1),
        rest[0],
        jnp.concatenate(up_sum, 1),
        down_sum,
        norm_grads,
    )


def suits(mesh):
    return mesh.shape["dp"] == 16 and mesh.shape["seq"] == 2


def solution(mesh):
    return jax.shard_map(
        fast_device if suits(mesh) else general_device,
        mesh=mesh,
        in_specs=(
            P("dp", "seq", None),
            P("dp", "seq", None),
            P("dp", "seq", None),
            P("dp"),
            P("dp"),
            P("dp", "seq", None),
            P("dp", None),
            P(None, "dp", None),
            P("dp", None),
            P("dp", None),
            P("dp", None),
            P("dp", None),
            P("dp", None),
            P("dp", None),
            P("dp", None),
            P(None, "dp"),
        ),
        out_specs=(
            P("dp", "seq", None),
            P("dp", "seq", None),
            P("dp", "seq", None),
            P("dp", None),
            P(None, "dp", None),
            P("dp", None),
            P("dp", None),
            P("dp", None),
            P("dp", None),
            P("dp", None),
            P("dp", None),
            P("dp", None),
            P(None, "dp"),
        ),
        check_vma=False,
    )
```

```python
import functools

import jax
import jax.numpy as jnp
import numpy as np
from jax import lax
from jax.experimental import pallas as pl
from jax.experimental.pallas import tpu as pltpu
from jax.sharding import PartitionSpec as P

HEADS = 12
SIDE = 14
MESH = pl.DeviceIdType.MESH
LOW = jnp.bfloat16

STEPS = ((4, 3, 2, 0), (4, 0, 3, 2), (4, 2, 0, 3))
PORTIONS = 3
GROUP = 8


def my_bits():
    a = lax.axis_index("dp")
    return [
        lax.axis_index("seq"),
        lax.rem(a, 2),
        lax.rem(a // 2, 2),
        lax.rem(a // 4, 2),
        lax.rem(a // 8, 2),
    ]


def flipped(bits, which):
    return [1 - b if i == which else b for i, b in enumerate(bits)]


def place(bits):
    return (bits[1] + 2 * bits[2] + 4 * bits[3] + 8 * bits[4], bits[0])


def slot_of(bits, p):
    order = STEPS[p]
    return (
        bits[order[0]] + 2 * bits[order[1]] + 4 * bits[order[2]] + 8 * bits[order[3]] + 16 * bits[1]
    )


def device_of_slot(p):
    owners = np.zeros(32, np.int64)
    for e in range(32):
        bits = [(e >> i) & 1 for i in range(5)]
        owners[int(slot_of(bits, p))] = e
    return owners


def slots_to_devices(array):
    parts = []
    for p in range(PORTIONS):
        rest = array.shape[2:]
        names = [1, STEPS[p][3], STEPS[p][2], STEPS[p][1], STEPS[p][0]]
        cube = array[p].reshape((2,) * 5 + rest)
        perm = [names.index(bit) for bit in (4, 3, 2, 1, 0)]
        cube = cube.transpose(perm + [5 + i for i in range(len(rest))])
        parts.append(cube.reshape((32,) + rest))
    return jnp.stack(parts, 1)


def devices_to_slots(array):
    parts = []
    for p in range(PORTIONS):
        rest = array.shape[2:]
        names = [4, 3, 2, 1, 0]
        cube = array[:, p].reshape((2,) * 5 + rest)
        want = [1, STEPS[p][3], STEPS[p][2], STEPS[p][1], STEPS[p][0]]
        perm = [names.index(bit) for bit in want]
        cube = cube.transpose(perm + [5 + i for i in range(len(rest))])
        parts.append(cube.reshape((32,) + rest))
    return jnp.stack(parts, 0)


def greet(places):
    barrier = pltpu.get_barrier_semaphore()
    for where in places:
        pl.semaphore_signal(barrier, inc=1, device_id=where, device_id_type=MESH)
    pl.semaphore_wait(barrier, len(places))


def arrived(ref, sem):
    pltpu.make_async_remote_copy(
        src_ref=ref,
        dst_ref=ref,
        send_sem=sem,
        recv_sem=sem,
        device_id=(lax.axis_index("dp"), 1 - lax.axis_index("seq")),
        device_id_type=MESH,
    ).wait_recv()


def with_mask(bits, mask):
    return [1 - b if (mask >> i) & 1 else b for i, b in enumerate(bits)]


def number_of(bits):
    return bits[0] + 2 * bits[1] + 4 * bits[2] + 8 * bits[3] + 16 * bits[4]


def stem_part(ref, bits, p):
    return ref.at[p, pl.ds(slot_of(bits, p), 1)]


def stem_own(ref, bits, p):
    return ref.at[pl.ds(p, 1)]


def rows_part(ref, bits, p):
    width = ref.shape[2] // PORTIONS
    return ref.at[number_of(bits), :, pl.ds(p * width, width)]


def rows_own(ref, bits, p):
    width = ref.shape[1] // PORTIONS
    return ref.at[:, pl.ds(p * width, width)]


KINDS = {
    "stem": (stem_own, stem_part),
    "rows": (rows_own, rows_part),
}


def gather_steps(kinds, swaps, pairs, refs):
    count = len(kinds)
    total = count + swaps + pairs
    ins, outs, sems = refs[:total], refs[total : 2 * total], refs[2 * total :]
    send_sem, recv_sem, own_sem, swap_send, swap_recv, pair_send, pair_recv = sems
    bits = my_bits()
    a, s = lax.axis_index("dp"), bits[0]
    dp = ins[count].shape[0] if swaps else 1
    partners = [place(flipped(bits, b)) for b in range(5)]
    partners += [(lax.rem(a + j, dp), s) for j in range(1, dp)]

    def own_of(i, p):
        return KINDS[kinds[i]][0](ins[i], bits, p)

    def part_of(i, p, mask):
        return KINDS[kinds[i]][1](outs[i], with_mask(bits, mask), p)

    def block(i, p, mask, bit):
        return pltpu.make_async_remote_copy(
            src_ref=own_of(i, p) if mask == 0 else part_of(i, p, mask),
            dst_ref=part_of(i, p, mask),
            send_sem=send_sem.at[i, p, mask ^ (1 << bit)],
            recv_sem=recv_sem.at[i, p, mask ^ (1 << bit)],
            device_id=place(flipped(bits, bit)),
            device_id_type=MESH,
        )

    def await_part(i, p, mask):
        arrived(part_of(i, p, mask), recv_sem.at[i, p, mask])

    def own_copy(i, p):
        return pltpu.make_async_copy(own_of(i, p), part_of(i, p, 0), own_sem.at[i, p])

    def swap_own():
        return pltpu.make_async_copy(ins[count].at[a], outs[count].at[a], swap_send.at[0])

    def swap_copy(j):
        to = lax.rem(a + j, dp)
        return pltpu.make_async_remote_copy(
            src_ref=ins[count].at[to],
            dst_ref=outs[count].at[a],
            send_sem=swap_send.at[j],
            recv_sem=swap_recv.at[j],
            device_id=(to, s),
            device_id_type=MESH,
        )

    def pair_copy(j):
        return pltpu.make_async_remote_copy(
            src_ref=ins[count + swaps + j],
            dst_ref=outs[count + swaps + j],
            send_sem=pair_send.at[j],
            recv_sem=pair_recv.at[j],
            device_id=(a, 1 - s),
            device_id_type=MESH,
        )

    def pair_own():
        return pltpu.make_async_copy(
            ins[count + swaps], outs[count + swaps], pair_send.at[pairs]
        )

    every = [(i, p) for i in range(count) for p in range(PORTIONS)]
    held = {p: [0] for p in range(PORTIONS)}
    fresh = {p: [0] for p in range(PORTIONS)}
    sent = []
    steps = []
    for k in range(5):
        plan = []
        for i in range(count):
            for p in range(PORTIONS):
                waits = list(fresh[p]) if k else []
                links = [(mask, STEPS[p][k]) for mask in held[p]] if k < 4 else []
                plan.append((i, p, waits, links))
                sent += [(i, p, mask, bit) for mask, bit in links]
            for p in range(PORTIONS):
                cores = [(mask, 1) for mask in fresh[p]]
                plan.append((i, p, [], cores))
                sent += [(i, p, mask, bit) for mask, bit in cores]

        def run(k=k, plan=plan):
            if k == 0:
                greet(partners)
            for i, p, waits, sends in plan:
                for mask in waits:
                    await_part(i, p, mask)
                for mask, bit in sends:
                    block(i, p, mask, bit).start()
            if k == 0:
                for i, p in every:
                    own_copy(i, p).start()
                for j in range(1, pairs):
                    pair_copy(j).start()
                if pairs:

                    @pl.when(s == 0)
                    def _():
                        pair_copy(0).start()
                        pair_own().start()

                if swaps:
                    swap_own().start()
                for j in range(1, dp):
                    swap_copy(j).start()

        steps.append(run)
        if k < 4:
            for p in range(PORTIONS):
                fresh[p] = [mask ^ (1 << STEPS[p][k]) for mask in held[p]]
                held[p] = held[p] + fresh[p]

    def finish():
        for i, p in every:
            for mask in held[p]:
                await_part(i, p, mask ^ 2)
        for j in range(1, dp):
            arrived(outs[count].at[lax.rem(a - j + dp, dp)], swap_recv.at[j])
        for j in range(1, pairs):
            pair_copy(j).wait()
        if pairs:

            @pl.when(s == 0)
            def _():
                pair_copy(0).wait_send()
                pair_own().wait()

            @pl.when(s != 0)
            def _():
                arrived(outs[count + swaps], pair_recv.at[0])

        for i, p, mask, bit in sent:
            block(i, p, mask, bit).wait_send()
        for j in range(1, dp):
            swap_copy(j).wait_send()
        for i, p in every:
            own_copy(i, p).wait()
        if swaps:
            swap_own().wait()

    steps.append(finish)
    return steps


def gather_body(kinds, swaps, pairs, *refs):
    for step in gather_steps(kinds, swaps, pairs, refs):
        step()


def gather_sems(count, pairs):
    return [
        pltpu.SemaphoreType.DMA((count, PORTIONS, 32)),
        pltpu.SemaphoreType.DMA((count, PORTIONS, 32)),
        pltpu.SemaphoreType.DMA((count, PORTIONS)),
        pltpu.SemaphoreType.DMA((16,)),
        pltpu.SemaphoreType.DMA((16,)),
        pltpu.SemaphoreType.DMA((pairs + 1,)),
        pltpu.SemaphoreType.DMA((pairs + 1,)),
    ]


def gather_many(stems, rows, swaps, pairs, cid):
    kinds = ["stem"] * len(stems) + ["rows"] * len(rows)
    arrays = list(stems) + list(rows) + list(swaps) + list(pairs)
    shapes = [jax.ShapeDtypeStruct((PORTIONS, 32) + x.shape[1:], x.dtype) for x in stems]
    shapes += [jax.ShapeDtypeStruct((32,) + x.shape, x.dtype) for x in rows]
    shapes += [jax.ShapeDtypeStruct(x.shape, x.dtype) for x in list(swaps) + list(pairs)]
    space = pl.BlockSpec(memory_space=pltpu.HBM)
    return pl.pallas_call(
        functools.partial(gather_body, tuple(kinds), len(swaps), len(pairs)),
        name="gather_many",
        out_shape=tuple(shapes),
        in_specs=[space] * len(arrays),
        out_specs=(space,) * len(arrays),
        scratch_shapes=gather_sems(len(kinds), len(pairs)),
        compiler_params=pltpu.CompilerParams(collective_id=cid, has_side_effects=True),
    )(*arrays)


def attend_gather_body(width, *refs):
    info_ref, ok_ref, q_ref, k_ref, v_ref, x_ref, o_ref, lse_ref, all_ref = refs[:9]
    steps = gather_steps(("stem",), 0, 0, (x_ref, all_ref) + refs[9:])
    for at, step in enumerate(steps[:-1]):

        @pl.when(pl.program_id(0) == at)
        def _():
            step()

    attend_body("self", width, info_ref, ok_ref, q_ref, k_ref, v_ref, o_ref, lse_ref)

    @pl.when(pl.program_id(0) == pl.num_programs(0) - 1)
    def _():
        steps[-1]()


def attend_gather(info, ok, q, k, v, x, cid):
    rows, features = q.shape
    keys = k.shape[0]
    width = features // HEADS
    pairs = features // PAIR
    return pl.pallas_call(
        functools.partial(attend_gather_body, width),
        name="attend_gather",
        grid=(pairs,),
        in_specs=attention_specs(rows, keys, ok) + [pl.BlockSpec(memory_space=pltpu.HBM)],
        out_specs=(
            pl.BlockSpec((rows, PAIR), lambda i: (0, i)),
            pl.BlockSpec((1, 8, rows), lambda i: (i, 0, 0)),
            pl.BlockSpec(memory_space=pltpu.HBM),
        ),
        out_shape=(
            jax.ShapeDtypeStruct((rows, features), LOW),
            jax.ShapeDtypeStruct((pairs, 8, rows), jnp.float32),
            jax.ShapeDtypeStruct((PORTIONS, 32) + x.shape[1:], x.dtype),
        ),
        scratch_shapes=gather_sems(1, 0),
        compiler_params=pltpu.CompilerParams(
            collective_id=cid, has_side_effects=True, vmem_limit_bytes=48 << 20
        ),
    )(info, ok, q, k, v, x)


def pack_body(pieces, *refs):
    ins, o_ref = refs[:-1], refs[-1]
    rows, cols = o_ref.shape[1:]
    for at, (which, row, col) in enumerate(pieces):
        o_ref[at] = ins[which][row : row + rows, col : col + cols]


def pack(pieces, arrays, rows, cols):
    return pl.pallas_call(
        functools.partial(pack_body, tuple(pieces)),
        name="pack",
        out_shape=jax.ShapeDtypeStruct((len(pieces), rows, cols), arrays[0].dtype),
    )(*arrays)


def swap_both_steps(x_ref, pair_ref, o_ref, other_ref, sems):
    send_sem, recv_sem, pass_sem, got_sem, own_sem, pair_sem = sems
    a, s = lax.axis_index("dp"), lax.axis_index("seq")
    count = x_ref.shape[0]
    partners = [(lax.rem(a + j, count), s) for j in range(1, count)] + [(a, 1 - s)]

    def own():
        return pltpu.make_async_copy(x_ref.at[a], o_ref.at[s, a], own_sem)

    def direct(j):
        to = lax.rem(a + j, count)
        return pltpu.make_async_remote_copy(
            src_ref=x_ref.at[to],
            dst_ref=o_ref.at[s, a],
            send_sem=send_sem.at[j],
            recv_sem=recv_sem.at[j],
            device_id=(to, s),
            device_id_type=MESH,
        )

    def onward(j):
        source = lax.rem(a - j + count, count)
        return pltpu.make_async_remote_copy(
            src_ref=o_ref.at[s, source] if j else x_ref.at[a],
            dst_ref=o_ref.at[s, source],
            send_sem=pass_sem.at[j],
            recv_sem=got_sem.at[j],
            device_id=(a, 1 - s),
            device_id_type=MESH,
        )

    def paired():
        return pltpu.make_async_remote_copy(
            src_ref=pair_ref,
            dst_ref=other_ref,
            send_sem=pair_sem.at[0],
            recv_sem=pair_sem.at[1],
            device_id=(a, 1 - s),
            device_id_type=MESH,
        )

    def start():
        own().start()
        paired().start()
        onward(0).start()
        for j in range(1, count):
            direct(j).start()

    def pass_on():
        for j in range(1, count):
            arrived(o_ref.at[s, lax.rem(a - j + count, count)], recv_sem.at[j])
            onward(j).start()

    def finish():
        for j in range(count):
            arrived(o_ref.at[1 - s, lax.rem(a - j + count, count)], got_sem.at[j])
        for j in range(1, count):
            direct(j).wait_send()
        for j in range(count):
            onward(j).wait_send()
        own().wait()
        paired().wait()

    return partners, start, pass_on, finish


def swap_both_sems(count):
    return [pltpu.SemaphoreType.DMA((count,))] * 4 + [
        pltpu.SemaphoreType.DMA,
        pltpu.SemaphoreType.DMA((2,)),
    ]


def reduce_body(swaps, *refs):
    count = 1 + swaps
    ins, outs, refs = refs[:count], refs[count : 2 * count], refs[2 * count :]
    x_ref, o_ref = ins[0], outs[0]
    bufs, (send_sem, recv_sem) = refs[:5], refs[5:7]
    bits = my_bits()
    partners = [place(flipped(bits, b)) for b in range(5)]
    if swaps:
        others, start, pass_on, finish = swap_both_steps(*ins[1:], *outs[1:], refs[7:])
        partners += others
    greet(partners)
    started = []

    def send(p, src, dst, bit, k):
        copy = pltpu.make_async_remote_copy(
            src_ref=src,
            dst_ref=dst,
            send_sem=send_sem.at[p, k],
            recv_sem=recv_sem.at[p, k],
            device_id=place(flipped(bits, bit)),
            device_id_type=MESH,
        )
        copy.start()
        started.append(copy)

    for p in range(PORTIONS):
        away = 16 * (1 - bits[1])
        send(p, x_ref.at[p, pl.ds(away, 16)], bufs[0].at[p], 1, 0)
    for k in range(5):
        size = 16 >> k
        if swaps and k == 1:
            start()
        if swaps and k == 4:
            pass_on()
        for p in range(PORTIONS):
            arrived(bufs[k].at[p], recv_sem.at[p, k])
            if k == 0:
                base, held = 16 * bits[1], x_ref
            else:
                base, held = size * bits[STEPS[p][4 - k]], bufs[k - 1]
            if k == 4:
                o_ref[p] = held[p, base].astype(jnp.float32) + bufs[k][p, 0].astype(jnp.float32)
                continue
            for j in range(size):
                total = held[p, base + j].astype(jnp.float32) + bufs[k][p, j].astype(jnp.float32)
                bufs[k][p, j] = total.astype(bufs[k].dtype)
            half = size // 2
            send(
                p,
                bufs[k].at[p, pl.ds(half * (1 - bits[STEPS[p][3 - k]]), half)],
                bufs[k + 1].at[p],
                STEPS[p][3 - k],
                k + 1,
            )
    if swaps:
        finish()
    for copy in started:
        copy.wait_send()


def reduce_all(x, swaps, cid):
    rest = x.shape[2:]
    vmem, hbm = pl.BlockSpec(memory_space=pltpu.VMEM), pl.BlockSpec(memory_space=pltpu.HBM)
    return pl.pallas_call(
        functools.partial(reduce_body, len(swaps)),
        name="reduce_all",
        out_shape=tuple(
            [jax.ShapeDtypeStruct((PORTIONS,) + rest, jnp.float32)]
            + [jax.ShapeDtypeStruct((2,) + g.shape, g.dtype) for g in swaps[:1]]
            + [jax.ShapeDtypeStruct(g.shape, g.dtype) for g in swaps[1:]]
        ),
        in_specs=[vmem] + [hbm] * len(swaps),
        out_specs=tuple([vmem] + [hbm] * len(swaps)),
        scratch_shapes=[pltpu.VMEM((PORTIONS, 16 >> k) + rest, x.dtype) for k in range(5)]
        + [pltpu.SemaphoreType.DMA((PORTIONS, 5)), pltpu.SemaphoreType.DMA((PORTIONS, 5))]
        + (swap_both_sems(swaps[0].shape[0]) if swaps else []),
        compiler_params=pltpu.CompilerParams(
            collective_id=cid, has_side_effects=True, vmem_limit_bytes=40 << 20
        ),
    )(x, *swaps)


def swap_both_body(x_ref, pair_ref, o_ref, other_ref, *sems):
    partners, start, pass_on, finish = swap_both_steps(x_ref, pair_ref, o_ref, other_ref, sems)
    greet(partners)
    start()
    pass_on()
    finish()


def swap_both(x, pair, cid):
    space = pl.BlockSpec(memory_space=pltpu.HBM)
    return pl.pallas_call(
        swap_both_body,
        name="swap_both",
        out_shape=(
            jax.ShapeDtypeStruct((2,) + x.shape, x.dtype),
            jax.ShapeDtypeStruct(pair.shape, pair.dtype),
        ),
        in_specs=[space] * 2,
        out_specs=(space,) * 2,
        scratch_shapes=swap_both_sems(x.shape[0]),
        compiler_params=pltpu.CompilerParams(collective_id=cid, has_side_effects=True),
    )(x, pair)


def exchange_body(x_ref, o_ref, send_sem, recv_sem, own_sem):
    e = 2 * lax.axis_index("dp") + lax.axis_index("seq")
    count = x_ref.shape[0]

    def where(number):
        return (number // 2, lax.rem(number, 2))

    greet([where(lax.rem(e + j, count)) for j in range(1, count)])
    own = pltpu.make_async_copy(x_ref.at[e], o_ref.at[e], own_sem)
    own.start()
    copies = []
    for j in range(1, count):
        to = lax.rem(e + j, count)
        copy = pltpu.make_async_remote_copy(
            src_ref=x_ref.at[to],
            dst_ref=o_ref.at[e],
            send_sem=send_sem.at[j],
            recv_sem=recv_sem.at[j],
            device_id=where(to),
            device_id_type=MESH,
        )
        copy.start()
        copies.append(copy)
    for j in range(1, count):
        got = o_ref.at[lax.rem(e - j + count, count)]
        arrived(got, recv_sem.at[j])
    for copy in copies:
        copy.wait_send()
    own.wait()


def exchange_all(x, cid):
    count = x.shape[0]
    return pl.pallas_call(
        exchange_body,
        name="exchange_all",
        out_shape=jax.ShapeDtypeStruct(x.shape, x.dtype),
        in_specs=[pl.BlockSpec(memory_space=pltpu.HBM)],
        out_specs=pl.BlockSpec(memory_space=pltpu.HBM),
        scratch_shapes=[
            pltpu.SemaphoreType.DMA((count,)),
            pltpu.SemaphoreType.DMA((count,)),
            pltpu.SemaphoreType.DMA,
        ],
        compiler_params=pltpu.CompilerParams(collective_id=cid, has_side_effects=True),
    )(x)


GELU_C = 0.7978845608028654
GELU_A = 0.044715


def gelu_of(x):
    return 0.5 * x * (1.0 + jnp.tanh(GELU_C * (x + GELU_A * (x * x * x))))


def gelu_slope(x):
    t = jnp.tanh(GELU_C * (x + GELU_A * (x * x * x)))
    return 0.5 * (1.0 + t) + 0.5 * x * (1.0 - t * t) * (GELU_C * (1.0 + 3.0 * GELU_A * (x * x)))


CHUNK = 640


def tap_masks(cells, examples):
    rows = examples * SIDE * SIDE
    at = np.arange(rows)
    i, j = (at // SIDE) % SIDE, at % SIDE
    out = np.zeros((16, cells), np.float32)
    for r in range(3):
        for c in range(3):
            ok = (i + r - 1 >= 0) & (i + r - 1 < SIDE) & (j + c - 1 >= 0) & (j + c - 1 < SIDE)
            out[3 * r + c, :rows] = ok
    out[9, :rows] = 1.0
    return out


def tap_shift(tap):
    return SIDE * (tap // 3 - 1) + tap % 3 - 1


def norm_act(values, valid, gain, bias, number):
    centre = jnp.sum(values, 1, keepdims=True) / number
    away = jnp.where(valid > 0, values - centre, 0.0)
    rstd = lax.rsqrt(jnp.sum(away * away, 1, keepdims=True) / number + 1e-05)
    normed = away * rstd
    return normed, rstd, gelu_of(normed * gain + bias)


def put_low(x_ref, y):
    for p in range(PORTIONS):
        x_ref[p] = y[GROUP * p : GROUP * (p + 1)].astype(x_ref.dtype)


def first_body(number, p_ref, w_ref, gb_ref, m_ref, n_ref, rstd_ref, y_ref, x_ref, v_ref):
    blocks, size = p_ref.shape[0], p_ref.shape[1]
    v_ref[:, blocks * size :] = jnp.zeros((v_ref.shape[0], v_ref.shape[1] - blocks * size), jnp.float32)
    for block in range(blocks):
        v_ref[:, block * size : (block + 1) * size] = lax.dot_general(
            w_ref[...], p_ref[block], (((1,), (1,)), ((), ())), preferred_element_type=jnp.float32
        )
    normed, rstd, act = norm_act(v_ref[...], m_ref[9:10, :], gb_ref[:, 0:1], gb_ref[:, 1:2], number)
    n_ref[...] = normed
    rstd_ref[...] = jnp.broadcast_to(rstd, rstd_ref.shape)
    y_ref[...] = act
    put_low(x_ref, act)


def conv_body(number, layer, x_in, w_ref, gb_ref, m_ref, y_in, n_ref, rstd_ref, y_ref, x_ref, z_ref):
    cells = x_in.shape[1]
    rows = y_in.shape[0]
    for start in range(0, cells, CHUNK):
        z_ref[:, start : start + CHUNK] = jnp.dot(
            w_ref[...], x_in[:, start : start + CHUNK], preferred_element_type=jnp.float32
        )
    total = jnp.zeros((rows, cells), jnp.float32)
    for tap in range(9):
        moved = z_ref[rows * tap : rows * (tap + 1), :]
        shift = (-tap_shift(tap)) % cells
        if shift:
            moved = pltpu.roll(moved, shift, 1)
        total = total + jnp.where(m_ref[tap : tap + 1, :] > 0, moved, 0.0)
    normed, rstd, act = norm_act(
        total,
        m_ref[9:10, :],
        gb_ref[:, 2 * layer : 2 * layer + 1],
        gb_ref[:, 2 * layer + 1 : 2 * layer + 2],
        number,
    )
    n_ref[...] = normed
    rstd_ref[...] = jnp.broadcast_to(rstd, rstd_ref.shape)
    y = y_in[...] + act
    y_ref[...] = y
    put_low(x_ref, y)


def norm_slope(number, dy, normed, rstd, gain, bias):
    e = dy * gelu_slope(normed * gain + bias)
    d_gain = jnp.sum(e * normed, 1, keepdims=True)
    d_bias = jnp.sum(e, 1, keepdims=True)
    dn = e * gain
    mean_dn = d_bias * gain / number
    mean_dnn = d_gain * gain / number
    return rstd * (dn - mean_dn - normed * mean_dnn), d_gain, d_bias


def conv_back_body(
    number, layer, dy_ref, n_ref, rstd_ref, gb_ref, m_ref, x_in, wt_ref, dx_ref, g_ref, s_ref, d_ref
):
    cells = x_in.shape[1]
    rows = dy_ref.shape[0]
    dv, d_gain, d_bias = norm_slope(
        number,
        dy_ref[...],
        n_ref[...],
        rstd_ref[:, 0:1],
        gb_ref[:, 2 * layer : 2 * layer + 1],
        gb_ref[:, 2 * layer + 1 : 2 * layer + 2],
    )
    lanes = lax.broadcasted_iota(jnp.int32, s_ref.shape, 1)
    s_ref[...] = jnp.where(lanes == 0, d_gain, d_bias)
    for tap in range(9):
        shift = tap_shift(tap) % cells
        moved = pltpu.roll(dv, shift, 1) if shift else dv
        moved = jnp.where(m_ref[8 - tap : 9 - tap, :] > 0, moved, 0.0)
        d_ref[rows * tap : rows * (tap + 1), :] = moved.astype(d_ref.dtype)
    for start in range(0, cells, CHUNK):
        dx_ref[:, start : start + CHUNK] = jnp.dot(
            wt_ref[...], d_ref[:, start : start + CHUNK], preferred_element_type=jnp.float32
        ).astype(dx_ref.dtype)
    for start in range(0, x_in.shape[0], 256):
        g_ref[:, start : start + 256] = lax.dot_general(
            d_ref[...],
            x_in[start : start + 256, :],
            (((1,), (1,)), ((), ())),
            preferred_element_type=jnp.float32,
        ).astype(g_ref.dtype)


def first_back_body(number, dy_ref, n_ref, rstd_ref, gb_ref, p_ref, g_ref, s_ref):
    dv, d_gain, d_bias = norm_slope(
        number, dy_ref[...], n_ref[...], rstd_ref[:, 0:1], gb_ref[:, 0:1], gb_ref[:, 1:2]
    )
    lanes = lax.broadcasted_iota(jnp.int32, s_ref.shape, 1)
    s_ref[...] = jnp.where(lanes == 0, d_gain, d_bias)
    blocks, size = p_ref.shape[0], p_ref.shape[1]
    total = jnp.zeros(g_ref.shape, jnp.float32)
    for block in range(blocks):
        shift = (-block * size) % dv.shape[1]
        piece = (pltpu.roll(dv, shift, 1) if shift else dv)[:, :size]
        total = total + jnp.dot(
            piece.astype(p_ref.dtype), p_ref[block], preferred_element_type=jnp.float32
        )
    g_ref[...] = total.astype(g_ref.dtype)


BIG = pltpu.CompilerParams(vmem_limit_bytes=48 << 20)


def first_block(pixels, w, gb, masks, number):
    rows, cells = w.shape[0], masks.shape[1]
    return pl.pallas_call(
        functools.partial(first_body, number),
        name="stem_first",
        out_shape=(
            jax.ShapeDtypeStruct((rows, cells), jnp.float32),
            jax.ShapeDtypeStruct((rows, 128), jnp.float32),
            jax.ShapeDtypeStruct((rows, cells), jnp.float32),
            jax.ShapeDtypeStruct((PORTIONS, GROUP, cells), LOW),
        ),
        scratch_shapes=[pltpu.VMEM((rows, cells), jnp.float32)],
        compiler_params=BIG,
    )(pixels, w, gb, masks)


def conv_block(layer, x_all, w, gb, masks, y, number):
    rows, cells = y.shape
    return pl.pallas_call(
        functools.partial(conv_body, number, layer),
        name="stem_conv",
        out_shape=(
            jax.ShapeDtypeStruct((rows, cells), jnp.float32),
            jax.ShapeDtypeStruct((rows, 128), jnp.float32),
            jax.ShapeDtypeStruct((rows, cells), jnp.float32),
            jax.ShapeDtypeStruct((PORTIONS, GROUP, cells), LOW),
        ),
        scratch_shapes=[pltpu.VMEM((9 * rows, cells), jnp.float32)],
        compiler_params=BIG,
    )(x_all, w, gb, masks, y)


def conv_block_back(layer, dy, normed, rstd, gb, masks, x_all, w_t, number):
    rows, cells = dy.shape
    features = x_all.shape[0]
    return pl.pallas_call(
        functools.partial(conv_back_body, number, layer),
        name="stem_conv_back",
        out_shape=(
            jax.ShapeDtypeStruct((features, cells), LOW),
            jax.ShapeDtypeStruct((9 * rows, features), LOW),
            jax.ShapeDtypeStruct((rows, 128), jnp.float32),
        ),
        scratch_shapes=[pltpu.VMEM((9 * rows, cells), LOW)],
        compiler_params=BIG,
    )(dy, normed, rstd, gb, masks, x_all, w_t)


def first_block_back(dy, normed, rstd, gb, pixels, number):
    rows, cells = dy.shape
    return pl.pallas_call(
        functools.partial(first_back_body, number),
        name="stem_first_back",
        out_shape=(
            jax.ShapeDtypeStruct((rows, pixels.shape[2]), LOW),
            jax.ShapeDtypeStruct((rows, 128), jnp.float32),
        ),
        compiler_params=BIG,
    )(dy, normed, rstd, gb, pixels)


def padded_2(cells, sides, width):
    for axis, dim in sides:
        count = lax.axis_size(axis)
        ends = count - 1
        head = lax.slice_in_dim(cells, 0, width, axis=dim)
        tail = lax.slice_in_dim(cells, cells.shape[dim] - width, cells.shape[dim], axis=dim)
        cells = jnp.concatenate(
            [
                lax.ppermute(tail, axis, [(i, (i + 1) % count) for i in range(ends)]),
                cells,
                lax.ppermute(head, axis, [((i + 1) % count, i) for i in range(ends)]),
            ],
            axis=dim,
        )
    return cells


def passed_along(array, axis, by):
    length = lax.axis_size(axis)
    pairs = [(i, i + by) for i in range(length) if 0 <= i + by < length]
    return lax.ppermute(array, axis, pairs)


def layer_norm(activ, gain_vec, bias_vec):
    row_mean = jnp.mean(activ, -1, keepdims=True)
    centred = activ - row_mean
    spread = jnp.mean(centred * centred, -1, keepdims=True)
    return centred * lax.rsqrt(spread + 1e-06) * gain_vec + bias_vec


def heads_of(matrix):
    return matrix.reshape(matrix.shape[0], HEADS, -1)


def dot_float(left, right):
    return jnp.dot(left, right, preferred_element_type=jnp.float32)


def norm_batch(values, gain_vec, bias_vec, number):
    sums = lax.psum((jnp.sum(values, 0), jnp.sum(values * values, 0)), ("dp", "seq"))
    col_mean = sums[0] / number
    col_var = sums[1] / number - col_mean * col_mean
    inv_std = lax.rsqrt(col_var + 1e-05)
    normed = (values - col_mean) * inv_std
    return (normed, inv_std, normed * gain_vec + bias_vec)


def batch_back(d_pre, normed, inv_std, gain_vec, number):
    grad_gain = jnp.sum(d_pre * normed, 0)
    grad_bias = jnp.sum(d_pre, 0)
    d_normed = d_pre * gain_vec
    sums = lax.psum((jnp.sum(d_normed, 0), jnp.sum(d_normed * normed, 0)), ("dp", "seq"))
    d_values = inv_std * (d_normed - sums[0] / number - normed * (sums[1] / number))
    return (d_values, grad_gain, grad_bias)


def conv_fwd(flat_low, weight):
    features = flat_low.shape[1]
    grid_rows = flat_low.shape[0] // SIDE
    grid = flat_low.reshape(grid_rows, SIDE, features)
    padded = padded_2(grid, (("seq", 0),), 1)
    padded = jnp.pad(padded, ((0, 0), (1, 1), (0, 0)))
    total = jnp.zeros((grid_rows * SIDE, features), jnp.float32)
    for row_tap in range(3):
        for col_tap in range(3):
            tap = 3 * row_tap + col_tap
            window = padded[row_tap : row_tap + grid_rows, col_tap : col_tap + SIDE].reshape(
                -1, features
            )
            total = total + dot_float(window, weight[tap * features : (tap + 1) * features])
    return (total, padded)


def send_rim(rim_rows, offset):
    return passed_along(rim_rows.astype(jnp.bfloat16), "seq", offset).astype(rim_rows.dtype)


def conv_back(padded, d_out_low, weight):
    features = d_out_low.shape[1]
    grid_rows = padded.shape[0] - 2
    d_padded = jnp.zeros((grid_rows + 2, SIDE + 2, features), jnp.float32)
    tap_grads = []
    for row_tap in range(3):
        for col_tap in range(3):
            tap = 3 * row_tap + col_tap
            tap_weight = weight[tap * features : (tap + 1) * features]
            window = padded[row_tap : row_tap + grid_rows, col_tap : col_tap + SIDE].reshape(
                -1, features
            )
            tap_grads.append(dot_float(window.T, d_out_low))
            spread = dot_float(d_out_low, tap_weight.T).reshape(grid_rows, SIDE, features)
            d_padded = d_padded + jnp.pad(
                spread, ((row_tap, 2 - row_tap), (col_tap, 2 - col_tap), (0, 0))
            )
    inner = d_padded[1 : grid_rows + 1, 1 : SIDE + 1]
    from_below = send_rim(d_padded[0, 1 : SIDE + 1], -1)
    from_above = send_rim(d_padded[grid_rows + 1, 1 : SIDE + 1], 1)
    inner = inner.at[grid_rows - 1].add(from_below).at[0].add(from_above)
    return (jnp.concatenate(tap_grads, 0), inner.reshape(-1, features))


def attend_block(queries, key_rows, value_rows, allowed, score_scale):
    scores = (
        jnp.einsum("qhd,khd->hqk", queries, key_rows, preferred_element_type=jnp.float32)
        * score_scale
    )
    scores = jnp.where(allowed[None], scores, -1000000000.0)
    row_max = jnp.max(scores, -1, keepdims=True)
    exponent = jnp.exp(scores - row_max)
    row_total = jnp.sum(exponent, -1, keepdims=True)
    softmax = (exponent / row_total).astype(jnp.bfloat16)
    outputs = jnp.einsum("hqk,khd->qhd", softmax, value_rows, preferred_element_type=jnp.float32)
    return (outputs, row_max + jnp.log(row_total))


def attend_back(queries, key_rows, value_rows, allowed, score_scale, grad_out, log_total):
    scores = (
        jnp.einsum("qhd,khd->hqk", queries, key_rows, preferred_element_type=jnp.float32)
        * score_scale
    )
    scores = jnp.where(allowed[None], scores, -1000000000.0)
    softmax = jnp.exp(scores - log_total)
    d_softmax = jnp.einsum("qhd,khd->hqk", grad_out, value_rows, preferred_element_type=jnp.float32)
    row_delta = jnp.sum(softmax * d_softmax, -1, keepdims=True)
    d_scores = (softmax * (d_softmax - row_delta)).astype(jnp.bfloat16)
    d_query = (
        jnp.einsum("hqk,khd->qhd", d_scores, key_rows, preferred_element_type=jnp.float32)
        * score_scale
    )
    d_keys = (
        jnp.einsum("hqk,qhd->khd", d_scores, queries, preferred_element_type=jnp.float32)
        * score_scale
    )
    d_values = jnp.einsum(
        "hqk,qhd->khd", softmax.astype(jnp.bfloat16), grad_out, preferred_element_type=jnp.float32
    )
    return (d_query, d_keys, d_values)


def run_attention(queries, key_rows, value_rows, allow_fn, score_scale):
    row_count = queries.shape[0]
    block_rows = min(512, row_count)
    block_count = row_count // block_rows
    query_blocks = queries.reshape(block_count, block_rows, queries.shape[1], queries.shape[2])
    starts = jnp.arange(block_count, dtype=jnp.int32) * block_rows

    def one_block(block_pair):
        return attend_block(
            block_pair[0], key_rows, value_rows, allow_fn(block_pair[1], block_rows), score_scale
        )

    outputs, log_total = lax.map(one_block, (query_blocks, starts))
    return (outputs.reshape(queries.shape), log_total)


def run_back(queries, key_rows, value_rows, allow_fn, score_scale, grad_out, log_total):
    row_count = queries.shape[0]
    block_rows = min(512, row_count)
    block_count = row_count // block_rows
    query_blocks = queries.reshape(block_count, block_rows, queries.shape[1], queries.shape[2])
    grad_blocks = grad_out.reshape(query_blocks.shape)
    starts = jnp.arange(block_count, dtype=jnp.int32) * block_rows

    def one_block(running, block_items):
        query_part, grad_part, total_part, first_row = block_items
        d_query, d_keys, d_values = attend_back(
            query_part,
            key_rows,
            value_rows,
            allow_fn(first_row, block_rows),
            score_scale,
            grad_part,
            total_part,
        )
        return ((running[0] + d_keys, running[1] + d_values), d_query)

    zero_grads = jnp.zeros(key_rows.shape, jnp.float32)
    sums_kv, d_query = lax.scan(
        one_block, (zero_grads, zero_grads), (query_blocks, grad_blocks, log_total, starts)
    )
    return (d_query.reshape(queries.shape), sums_kv[0], sums_kv[1])


def general_device(
    captions,
    patches,
    prefix,
    prefix_count,
    caption_len,
    cotangent,
    w_patch,
    w_conv,
    w_self_qkv,
    w_self_out,
    w_cross_q,
    w_cross_kv,
    w_cross_out,
    w_up,
    w_down,
    norm_params,
):
    gathered = (
        lax.all_gather(w_patch, "dp", axis=0, tiled=True),
        lax.all_gather(w_conv, "dp", axis=1, tiled=True),
        lax.all_gather(w_self_qkv, "dp", axis=0, tiled=True),
        lax.all_gather(w_self_out, "dp", axis=0, tiled=True),
        lax.all_gather(w_cross_q, "dp", axis=0, tiled=True),
        lax.all_gather(w_cross_kv, "dp", axis=0, tiled=True),
        lax.all_gather(w_cross_out, "dp", axis=0, tiled=True),
        lax.all_gather(w_up, "dp", axis=0, tiled=True),
        lax.all_gather(w_down, "dp", axis=0, tiled=True),
        lax.all_gather(norm_params, "dp", axis=1, tiled=True),
    )
    (
        full_patch,
        full_conv,
        full_qkv,
        full_sout,
        full_cq,
        full_ckv,
        full_cout,
        full_up,
        full_down,
        full_norms,
    ) = gathered
    norms = full_norms.astype(jnp.float32)
    features = full_sout.shape[0]
    score_scale = (features // HEADS) ** (-0.5)
    seq_count = lax.axis_size("seq")
    seq_index = lax.axis_index("seq")
    pixels = patches[0]
    stem_out = dot_float(pixels, full_patch)
    number = stem_out.shape[0] * lax.axis_size("dp") * seq_count
    normed_one, inv_one, pre_one = norm_batch(stem_out, norms[0], norms[1], number)
    first_out = jax.nn.gelu(pre_one)
    first_low = first_out.astype(jnp.bfloat16)
    conv_two, padded_two = conv_fwd(first_low, full_conv[0])
    normed_two, inv_two, pre_two = norm_batch(conv_two, norms[2], norms[3], number)
    second_out = first_out + jax.nn.gelu(pre_two)
    second_low = second_out.astype(jnp.bfloat16)
    conv_three, padded_three = conv_fwd(second_low, full_conv[1])
    normed_three, inv_three, pre_three = norm_batch(conv_three, norms[4], norms[5], number)
    third_out = second_out + jax.nn.gelu(pre_three)
    patch_low = third_out.astype(jnp.bfloat16)
    prefix_low = prefix[0]
    kv_prefix = dot_float(prefix_low, full_ckv).astype(jnp.bfloat16)
    kv_patch = dot_float(patch_low, full_ckv).astype(jnp.bfloat16)
    all_prefix, all_patch = (
        lax.all_gather(kv_prefix, "seq", axis=0, tiled=True),
        lax.all_gather(kv_patch, "seq", axis=0, tiled=True),
    )
    memory_kv = jnp.concatenate([all_prefix, all_patch], 0)
    mem_rows = memory_kv.shape[0]
    prefix_total = all_prefix.shape[0]
    mem_keys = heads_of(memory_kv[:, :features])
    mem_values = heads_of(memory_kv[:, features:])
    slot_ids = jnp.arange(mem_rows, dtype=jnp.int32)
    mem_allowed = (slot_ids >= prefix_total) | (slot_ids < prefix_count[0])

    def cross_allow(first_row, block_rows):
        return jnp.broadcast_to(mem_allowed[None], (block_rows, mem_rows))

    inputs = captions[0].astype(jnp.float32)
    row_count = inputs.shape[0]
    low_one = layer_norm(inputs, norms[6], norms[7]).astype(jnp.bfloat16)
    qkv = dot_float(low_one, full_qkv).astype(jnp.bfloat16)
    queries = heads_of(qkv[:, :features])
    own_keys = heads_of(qkv[:, features : 2 * features])
    own_values = heads_of(qkv[:, 2 * features :])
    key_parts = [own_keys]
    value_parts = [own_values]
    position_parts = [seq_index * row_count + jnp.arange(row_count, dtype=jnp.int32)]
    offset = 1
    got_keys, got_values = passed_along((own_keys, own_values), "seq", offset)
    key_parts.insert(0, got_keys)
    value_parts.insert(0, got_values)
    position_parts.insert(
        0, (seq_index - offset) * row_count + jnp.arange(row_count, dtype=jnp.int32)
    )
    all_keys = jnp.concatenate(key_parts, 0)
    all_values = jnp.concatenate(value_parts, 0)
    key_pos = jnp.concatenate(position_parts, 0)
    length_one = caption_len[0]

    def self_allow(first_row, block_rows):
        query_pos = seq_index * row_count + first_row + jnp.arange(block_rows, dtype=jnp.int32)
        return (
            (key_pos[None] <= query_pos[:, None])
            & (key_pos[None] >= 0)
            & (key_pos[None] < length_one)
        )

    self_out, self_total = run_attention(queries, all_keys, all_values, self_allow, score_scale)
    self_low = self_out.reshape(row_count, features).astype(jnp.bfloat16)
    after_self = inputs + dot_float(self_low, full_sout)
    low_two = layer_norm(after_self, norms[8], norms[9]).astype(jnp.bfloat16)
    cross_flat = dot_float(low_two, full_cq).astype(jnp.bfloat16)
    cross_q = heads_of(cross_flat)
    cross_out, cross_total = run_attention(cross_q, mem_keys, mem_values, cross_allow, score_scale)
    cross_low = cross_out.reshape(row_count, features).astype(jnp.bfloat16)
    after_cross = after_self + dot_float(cross_low, full_cout)
    low_three = layer_norm(after_cross, norms[10], norms[11]).astype(jnp.bfloat16)
    up_proj = dot_float(low_three, full_up)
    hidden_low = jax.nn.gelu(up_proj).astype(jnp.bfloat16)
    result = after_cross + dot_float(hidden_low, full_down)
    back_weights = (
        lax.all_gather(w_patch, "dp", axis=0, tiled=True),
        lax.all_gather(w_conv, "dp", axis=1, tiled=True),
        lax.all_gather(w_self_qkv, "dp", axis=0, tiled=True),
        lax.all_gather(w_self_out, "dp", axis=0, tiled=True),
        lax.all_gather(w_cross_q, "dp", axis=0, tiled=True),
        lax.all_gather(w_cross_kv, "dp", axis=0, tiled=True),
        lax.all_gather(w_cross_out, "dp", axis=0, tiled=True),
        lax.all_gather(w_up, "dp", axis=0, tiled=True),
        lax.all_gather(w_down, "dp", axis=0, tiled=True),
        lax.all_gather(norm_params, "dp", axis=1, tiled=True),
    )
    (
        back_patch,
        back_conv,
        back_qkv,
        back_sout,
        back_cq,
        back_ckv,
        back_cout,
        back_up,
        back_down,
        back_norms,
    ) = back_weights
    bnorms = back_norms.astype(jnp.float32)
    out_grad = cotangent[0].astype(jnp.float32)
    grad_low = cotangent[0]
    grad_down = dot_float(hidden_low.T, grad_low)
    d_hidden = dot_float(grad_low, back_down.T)
    unused_gelu, gelu_back = jax.vjp(jax.nn.gelu, up_proj)
    d_upper = gelu_back(d_hidden)[0].astype(jnp.bfloat16)
    grad_up = dot_float(low_three.T, d_upper)
    unused_three, norm_back_three = jax.vjp(layer_norm, after_cross, bnorms[10], bnorms[11])
    d_three, grad_gain_three, grad_bias_three = norm_back_three(dot_float(d_upper, back_up.T))
    d_after_cross = out_grad + d_three
    cross_grad_low = d_after_cross.astype(jnp.bfloat16)
    grad_cout = dot_float(cross_low.T, cross_grad_low)
    d_cross = heads_of(dot_float(cross_grad_low, back_cout.T).astype(jnp.bfloat16))
    d_cross_q, d_mem_keys, d_mem_values = run_back(
        cross_q, mem_keys, mem_values, cross_allow, score_scale, d_cross, cross_total
    )
    d_cross_low = d_cross_q.reshape(row_count, features).astype(jnp.bfloat16)
    grad_cq = dot_float(low_two.T, d_cross_low)
    unused_two, norm_back_two = jax.vjp(layer_norm, after_self, bnorms[8], bnorms[9])
    d_two, grad_gain_two, grad_bias_two = norm_back_two(dot_float(d_cross_low, back_cq.T))
    d_after_self = d_after_cross + d_two
    d_memory = jnp.concatenate(
        [d_mem_keys.reshape(mem_rows, features), d_mem_values.reshape(mem_rows, features)], 1
    )
    mine_prefix, mine_patch = (
        lax.psum_scatter(
            d_memory[:prefix_total].astype(jnp.bfloat16), "seq", scatter_dimension=0, tiled=True
        ).astype(jnp.float32),
        lax.psum_scatter(
            d_memory[prefix_total:].astype(jnp.bfloat16), "seq", scatter_dimension=0, tiled=True
        ).astype(jnp.float32),
    )
    mine_prefix_low = mine_prefix.astype(jnp.bfloat16)
    mine_patch_low = mine_patch.astype(jnp.bfloat16)
    grad_ckv = dot_float(prefix_low.T, mine_prefix_low) + dot_float(patch_low.T, mine_patch_low)
    prefix_back = dot_float(mine_prefix_low, back_ckv.T)
    d_third = dot_float(mine_patch_low, back_ckv.T)
    unused_act_three, act_back_three = jax.vjp(jax.nn.gelu, pre_three)
    d_conv_three, grad_gain_bn3, grad_bias_bn3 = batch_back(
        act_back_three(d_third)[0], normed_three, inv_three, bnorms[4], number
    )
    grad_conv_one, d_second_in = conv_back(
        padded_three, d_conv_three.astype(jnp.bfloat16), back_conv[1]
    )
    d_second = d_third + d_second_in
    unused_act_two, act_back_two = jax.vjp(jax.nn.gelu, pre_two)
    d_conv_two, grad_gain_bn2, grad_bias_bn2 = batch_back(
        act_back_two(d_second)[0], normed_two, inv_two, bnorms[2], number
    )
    grad_conv_zero, d_first_in = conv_back(
        padded_two, d_conv_two.astype(jnp.bfloat16), back_conv[0]
    )
    d_first = d_second + d_first_in
    unused_act_one, act_back_one = jax.vjp(jax.nn.gelu, pre_one)
    d_stem, grad_gain_bn1, grad_bias_bn1 = batch_back(
        act_back_one(d_first)[0], normed_one, inv_one, bnorms[0], number
    )
    grad_patch = dot_float(pixels.T, d_stem.astype(jnp.bfloat16))
    grad_conv = jnp.stack([grad_conv_zero, grad_conv_one])
    self_grad_low = d_after_self.astype(jnp.bfloat16)
    grad_sout = dot_float(self_low.T, self_grad_low)
    d_self = heads_of(dot_float(self_grad_low, back_sout.T).astype(jnp.bfloat16))
    d_query, d_all_keys, d_all_values = run_back(
        queries, all_keys, all_values, self_allow, score_scale, d_self, self_total
    )
    own_start = (seq_count - 1) * row_count
    own_dkeys = d_all_keys[own_start:]
    own_dvalues = d_all_values[own_start:]
    offset = 1
    piece_start = (seq_count - 1 - offset) * row_count
    back_keys = passed_along(
        d_all_keys[piece_start : piece_start + row_count].astype(jnp.bfloat16), "seq", -offset
    ).astype(jnp.float32)
    back_values = passed_along(
        d_all_values[piece_start : piece_start + row_count].astype(jnp.bfloat16), "seq", -offset
    ).astype(jnp.float32)
    own_dkeys = own_dkeys + back_keys
    own_dvalues = own_dvalues + back_values
    d_qkv = jnp.concatenate(
        [
            d_query.reshape(row_count, features),
            own_dkeys.reshape(row_count, features),
            own_dvalues.reshape(row_count, features),
        ],
        1,
    ).astype(jnp.bfloat16)
    grad_qkv = dot_float(low_one.T, d_qkv)
    unused_one, norm_back_one = jax.vjp(layer_norm, inputs, bnorms[6], bnorms[7])
    d_one, grad_gain_one, grad_bias_one = norm_back_one(dot_float(d_qkv, back_qkv.T))
    d_inputs = d_after_self + d_one
    grad_norms = jnp.stack(
        [
            grad_gain_bn1,
            grad_bias_bn1,
            grad_gain_bn2,
            grad_bias_bn2,
            grad_gain_bn3,
            grad_bias_bn3,
            grad_gain_one,
            grad_bias_one,
            grad_gain_two,
            grad_bias_two,
            grad_gain_three,
            grad_bias_three,
        ]
    )
    shard_sums = (
        lax.psum_scatter(grad_patch, "dp", scatter_dimension=0, tiled=True),
        lax.psum_scatter(grad_conv, "dp", scatter_dimension=1, tiled=True),
        lax.psum_scatter(grad_qkv, "dp", scatter_dimension=0, tiled=True),
        lax.psum_scatter(grad_sout, "dp", scatter_dimension=0, tiled=True),
        lax.psum_scatter(grad_cq, "dp", scatter_dimension=0, tiled=True),
        lax.psum_scatter(grad_ckv, "dp", scatter_dimension=0, tiled=True),
        lax.psum_scatter(grad_cout, "dp", scatter_dimension=0, tiled=True),
        lax.psum_scatter(grad_up, "dp", scatter_dimension=0, tiled=True),
        lax.psum_scatter(grad_down, "dp", scatter_dimension=0, tiled=True),
        lax.psum_scatter(grad_norms, "dp", scatter_dimension=1, tiled=True),
    )
    totals = (
        lax.psum(shard_sums[0].astype(jnp.bfloat16), "seq").astype(jnp.float32),
        lax.psum(shard_sums[1].astype(jnp.bfloat16), "seq").astype(jnp.float32),
        lax.psum(shard_sums[2].astype(jnp.bfloat16), "seq").astype(jnp.float32),
        lax.psum(shard_sums[3].astype(jnp.bfloat16), "seq").astype(jnp.float32),
        lax.psum(shard_sums[4].astype(jnp.bfloat16), "seq").astype(jnp.float32),
        lax.psum(shard_sums[5].astype(jnp.bfloat16), "seq").astype(jnp.float32),
        lax.psum(shard_sums[6].astype(jnp.bfloat16), "seq").astype(jnp.float32),
        lax.psum(shard_sums[7].astype(jnp.bfloat16), "seq").astype(jnp.float32),
        lax.psum(shard_sums[8].astype(jnp.bfloat16), "seq").astype(jnp.float32),
        lax.psum(shard_sums[9].astype(jnp.bfloat16), "seq").astype(jnp.float32),
    )
    return (
        result[None].astype(jnp.bfloat16),
        d_inputs[None].astype(jnp.bfloat16),
        prefix_back[None].astype(jnp.bfloat16),
        totals[0],
        totals[1],
        totals[2],
        totals[3],
        totals[4],
        totals[5],
        totals[6],
        totals[7],
        totals[8],
        totals[9],
    )


PAIR = 128


def head_lanes(array, which, width):
    lanes = lax.broadcasted_iota(jnp.int32, array.shape, 1)
    return jnp.where((lanes >= which * width) & (lanes < (which + 1) * width), array, 0)


def scores_t(keys, q_head):
    return lax.dot_general(
        keys, q_head, (((1,), (1,)), ((), ())), preferred_element_type=jnp.float32
    )


def masked_scores(kind, info_ref, ok_ref, keys, q_head):
    if kind == "cross":
        scores = scores_t(keys, q_head)
        return jnp.where(ok_ref[:, 0:1] > 0, scores, -1e9)
    half = keys.shape[0] // 2
    before = scores_t(keys[:half], q_head)
    own = scores_t(keys[half:], q_head)
    before = jnp.where(info_ref[0] > 0, before, -1e9)
    key_at = lax.broadcasted_iota(jnp.int32, own.shape, 0)
    query_at = lax.broadcasted_iota(jnp.int32, own.shape, 1)
    own = jnp.where((key_at <= query_at) & (key_at < info_ref[1]), own, -1e9)
    return jnp.concatenate([before, own], 0)


def attend_body(kind, width, info_ref, ok_ref, q_ref, k_ref, v_ref, o_ref, lse_ref):
    keys, values = k_ref[...], v_ref[...]
    outs = []
    for which in range(PAIR // width):
        q_head = head_lanes(q_ref[...], which, width)
        scores = masked_scores(kind, info_ref, ok_ref, keys, q_head)
        top = jnp.max(scores, 0, keepdims=True)
        weights = jnp.exp(scores - top)
        total = jnp.sum(weights, 0, keepdims=True)
        lse_ref[0, which : which + 1, :] = top + jnp.log(total)
        out_t = lax.dot_general(
            head_lanes(values, which, width),
            weights.astype(LOW),
            (((0,), (0,)), ((), ())),
            preferred_element_type=jnp.float32,
        )
        outs.append(out_t / total)
    o_ref[...] = (outs[0] + outs[1]).T.astype(o_ref.dtype)


def attend_back_body(
    kind, width, scale, info_ref, ok_ref, q_ref, k_ref, v_ref, do_ref, lse_ref, dq_ref, dk_ref, dv_ref
):
    keys, values = k_ref[...], v_ref[...]
    dq_t, dk, dv = None, None, None
    for which in range(PAIR // width):
        q_head = head_lanes(q_ref[...], which, width)
        do_head = head_lanes(do_ref[...], which, width)
        scores = masked_scores(kind, info_ref, ok_ref, keys, q_head)
        probs = jnp.exp(scores - lse_ref[0, which : which + 1, :])
        d_probs = scores_t(values, do_head)
        delta = jnp.sum(probs * d_probs, 0, keepdims=True)
        ds = (probs * (d_probs - delta)).astype(LOW)
        part_k = jnp.dot(ds, q_head, preferred_element_type=jnp.float32)
        part_v = jnp.dot(probs.astype(LOW), do_head, preferred_element_type=jnp.float32)
        part_q = lax.dot_general(
            head_lanes(keys, which, width),
            ds,
            (((0,), (0,)), ((), ())),
            preferred_element_type=jnp.float32,
        )
        dk = part_k if dk is None else dk + part_k
        dv = part_v if dv is None else dv + part_v
        dq_t = part_q if dq_t is None else dq_t + part_q
    dq_ref[...] = (dq_t * scale).T.astype(dq_ref.dtype)
    dk_ref[...] = dk.astype(dk_ref.dtype)
    dv_ref[...] = dv.astype(dv_ref.dtype)


def attention_specs(rows, keys, ok):
    return [
        pl.BlockSpec(memory_space=pltpu.SMEM),
        pl.BlockSpec(ok.shape, lambda i: (0, 0)),
        pl.BlockSpec((rows, PAIR), lambda i: (0, i)),
        pl.BlockSpec((keys, PAIR), lambda i: (0, i)),
        pl.BlockSpec((keys, PAIR), lambda i: (0, i)),
    ]


def attend(kind, info, ok, q, k, v):
    rows, features = q.shape
    keys = k.shape[0]
    width = features // HEADS
    pairs = features // PAIR
    return pl.pallas_call(
        functools.partial(attend_body, kind, width),
        name=kind + "_attend",
        grid=(pairs,),
        in_specs=attention_specs(rows, keys, ok),
        out_specs=(
            pl.BlockSpec((rows, PAIR), lambda i: (0, i)),
            pl.BlockSpec((1, 8, rows), lambda i: (i, 0, 0)),
        ),
        out_shape=(
            jax.ShapeDtypeStruct((rows, features), LOW),
            jax.ShapeDtypeStruct((pairs, 8, rows), jnp.float32),
        ),
        compiler_params=BIG,
        cost_estimate=pl.CostEstimate(
            flops=4 * rows * keys * features, bytes_accessed=2 * (2 * rows + 2 * keys) * features,
            transcendentals=rows * keys * HEADS,
        ),
    )(info, ok, q, k, v)


def attend_grads(kind, info, ok, q, k, v, d_out, lse, scale):
    rows, features = q.shape
    keys = k.shape[0]
    width = features // HEADS
    pairs = features // PAIR
    return pl.pallas_call(
        functools.partial(attend_back_body, kind, width, scale),
        name=kind + "_attend_back",
        grid=(pairs,),
        in_specs=attention_specs(rows, keys, ok)
        + [
            pl.BlockSpec((rows, PAIR), lambda i: (0, i)),
            pl.BlockSpec((1, 8, rows), lambda i: (i, 0, 0)),
        ],
        out_specs=(
            pl.BlockSpec((rows, PAIR), lambda i: (0, i)),
            pl.BlockSpec((keys, PAIR), lambda i: (0, i)),
            pl.BlockSpec((keys, PAIR), lambda i: (0, i)),
        ),
        out_shape=(
            jax.ShapeDtypeStruct((rows, features), LOW),
            jax.ShapeDtypeStruct((keys, features), LOW),
            jax.ShapeDtypeStruct((keys, features), LOW),
        ),
        compiler_params=BIG,
        cost_estimate=pl.CostEstimate(
            flops=10 * rows * keys * features, bytes_accessed=2 * (3 * rows + 6 * keys) * features,
            transcendentals=rows * keys * HEADS,
        ),
    )(info, ok, q, k, v, d_out, lse)


def weight_grads_body(jobs, targets, owners, *refs):
    count = len(refs) - 4
    ins, (o_ref, left_ref, right_ref, sum_ref) = refs[:count], refs[count:]
    step = pl.program_id(0)
    for at, (left, right, rows, row_at, left_col, right_col) in enumerate(jobs):

        @pl.when(step == at)
        def _():
            size = left_ref.shape[1]
            left_ref[:rows] = ins[left][row_at : row_at + rows, left_col : left_col + size]
            right_ref[:rows] = ins[right][row_at : row_at + rows, right_col : right_col + size]
            if rows < left_ref.shape[0]:
                left_ref[rows:] = jnp.zeros((left_ref.shape[0] - rows, size), left_ref.dtype)
                right_ref[rows:] = jnp.zeros((left_ref.shape[0] - rows, size), left_ref.dtype)

    product = lax.dot_general(
        left_ref[...], right_ref[...], (((0,), (0,)), ((), ())), preferred_element_type=jnp.float32
    )
    for at, target in enumerate(targets):
        if at and targets[at - 1] == target:

            @pl.when(step == at)
            def _():
                sum_ref[...] += product

        else:

            @pl.when(step == at)
            def _():
                sum_ref[...] = product

    put_grads(owners, targets, step, o_ref, sum_ref)


def put_grads(owners, targets, step, o_ref, sum_ref):
    total = sum_ref[...].astype(o_ref.dtype)
    if owners == "mlp":
        tall = total.shape[0] // 4

        @pl.when(step < 4)
        def _():
            for part in range(4):
                o_ref[2 * (4 * step + part)] = total[tall * part : tall * (part + 1)]

        @pl.when(step >= 4)
        def _():
            short = total.shape[0] // 16
            start = pl.multiple_of(short * (step - 4), short)
            for a in range(16):
                o_ref[2 * a + 1, pl.ds(start, short)] = total[short * a : short * (a + 1)]

    else:
        first_twice = len(targets) - 4
        target = jnp.where(step < first_twice, step, first_twice + (step - first_twice) // 2)
        short = total.shape[0] // 16
        start = pl.multiple_of(short * lax.rem(target, 4), short)
        for a in range(16):
            o_ref[2 * a + target // 4, pl.ds(start, short)] = total[short * a : short * (a + 1)]


def weight_grads(jobs, targets, owners, arrays, features, rows):
    return pl.pallas_call(
        functools.partial(weight_grads_body, tuple(jobs), tuple(targets), owners),
        name="weight_grads",
        grid=(len(jobs),),
        in_specs=[pl.BlockSpec(memory_space=pltpu.VMEM)] * len(arrays),
        out_specs=pl.BlockSpec(memory_space=pltpu.VMEM),
        out_shape=jax.ShapeDtypeStruct((32, features // 4, features), LOW),
        scratch_shapes=[
            pltpu.VMEM((rows, features), LOW),
            pltpu.VMEM((rows, features), LOW),
            pltpu.VMEM((features, features), jnp.float32),
        ],
        compiler_params=BIG,
        cost_estimate=pl.CostEstimate(
            flops=2 * len(jobs) * rows * features * features,
            bytes_accessed=2 * 8 * features * features,
            transcendentals=0,
        ),
    )(*arrays)


def low_dot(left, right):
    return dot_float(left, right).astype(LOW)


def dot_t(left, right):
    return lax.dot_general(left, right, (((1,), (1,)), ((), ())), preferred_element_type=jnp.float32)


def t_dot(left, right):
    return lax.dot_general(left, right, (((0,), (0,)), ((), ())), preferred_element_type=jnp.float32)


def stem_weight_blocks(w_conv, w_patch, norm_params, s):
    features = w_patch.shape[1]
    flat = jnp.concatenate([w_conv.reshape(-1, features), w_patch], 0).T
    blocks = slots_to_devices(flat.reshape(PORTIONS, 32, GROUP, flat.shape[1]))
    blocks = blocks.reshape(16, 2, PORTIONS * GROUP, flat.shape[1])
    blocks = lax.dynamic_index_in_dim(blocks, s, 1, keepdims=False)
    rows = PORTIONS * GROUP
    extra = jnp.pad(norm_params, ((0, rows - norm_params.shape[0]), (0, 0)))
    blocks = jnp.concatenate([blocks, jnp.broadcast_to(extra, (16,) + extra.shape)], 2)
    return blocks


def stem_weights(got, w_conv, w_patch, norm_params):
    depth, conv_rows, features = w_conv.shape
    rows = PORTIONS * GROUP
    convs = []
    for layer in range(depth):
        part = got[:, :, layer * conv_rows : (layer + 1) * conv_rows]
        part = part.transpose(1, 0, 2).reshape(rows, 9, features).transpose(1, 0, 2)
        convs.append(part.reshape(9 * rows, features))
    at = depth * conv_rows
    patch = got[:, :, at : at + w_patch.shape[0]].transpose(1, 0, 2).reshape(rows, -1)
    norms = got[:, : norm_params.shape[0], at + w_patch.shape[0] :]
    return convs, patch, norms.transpose(1, 0, 2).reshape(norm_params.shape[0], -1)


def own_columns(norms):
    bits = my_bits()
    cut = norms.reshape(norms.shape[0], PORTIONS, 32, GROUP)
    parts = [
        lax.dynamic_index_in_dim(cut[:, p], slot_of(bits, p), 1, keepdims=False)
        for p in range(PORTIONS)
    ]
    mine = jnp.concatenate(parts, 1).T
    return jnp.pad(mine, ((0, 0), (0, 128 - mine.shape[1])))


def fast_device(
    captions,
    patches,
    prefix,
    prefix_count,
    caption_len,
    cotangent,
    w_patch,
    w_conv,
    w_self_qkv,
    w_self_out,
    w_cross_q,
    w_cross_kv,
    w_cross_out,
    w_up,
    w_down,
    norm_params,
):
    a_index, s_index = lax.axis_index("dp"), lax.axis_index("seq")
    examples, halves = 16, 2
    features = w_self_out.shape[1]
    score_scale = (features // HEADS) ** (-0.5)

    def chunks(w):
        return [w[:, i * features : (i + 1) * features] for i in range(w.shape[1] // features)]

    shard_rows = w_patch.shape[0]
    pieces = [(0, 0, features * i) for i in range(3)] + [(1, 0, 0), (2, 0, 0)]
    pieces += [(3, 0, 0), (3, 0, features), (4, 0, 0)]
    pieces += [(5, 0, features * i) for i in range(4)] + [(6, shard_rows * i, 0) for i in range(4)]
    all_w = pack(
        pieces,
        [w_self_qkv, w_self_out, w_cross_q, w_cross_kv, w_cross_out, w_up, w_down],
        shard_rows,
        features,
    )
    all_w = lax.all_gather(all_w, "dp", axis=1, tiled=True)
    qkv_w = all_w[:3]
    sout_w, cq_w, ck_w, cv_w, cout_w = (all_w[3 + i] for i in range(5))
    up_ws = [all_w[8 + i] for i in range(4)]
    down_w = all_w[12:].reshape(4, examples, -1, features).transpose(1, 0, 2, 3)
    down_w = down_w.reshape(4 * features, features)
    pixels, got_blocks, earlier, prefix_other = gather_many(
        [],
        [patches[0]],
        [stem_weight_blocks(w_conv, w_patch, norm_params, s_index)],
        [captions[0], prefix[0]],
        0,
    )

    convs, patch_w, norms_low = stem_weights(got_blocks, w_conv, w_patch, norm_params)
    norms = norms_low.astype(jnp.float32)
    own_gb = own_columns(norms[:6])
    own_cells = patches.shape[1]
    number = own_cells * examples * halves
    cells = -(-number // CHUNK) * CHUNK
    rows_own = PORTIONS * GROUP
    grid = halves * own_cells
    masks = jnp.asarray(tap_masks(cells, examples))
    def to_channels(by_row, cid):
        blocks = slots_to_devices(by_row.T.reshape(PORTIONS, 32, GROUP, by_row.shape[0]))
        return exchange_all(blocks.reshape(32, rows_own, by_row.shape[0]), cid)

    def laid_out(blocks):
        flat = blocks.transpose(1, 0, 2).reshape(rows_own, number)
        return jnp.pad(flat, ((0, 0), (0, cells - number)))

    n1, r1, y1, x1 = first_block(pixels, patch_w, own_gb, masks, number)
    (x1_all,) = gather_many([x1], [], [], [], 2)
    x1_all = x1_all.reshape(features, cells)
    n2, r2, y2, x2 = conv_block(1, x1_all, convs[0], own_gb, masks, y1, number)
    inputs = captions[0].astype(jnp.float32)
    row_count = inputs.shape[0]
    earlier = earlier.astype(jnp.float32)
    low_one = layer_norm(inputs, norms[6], norms[7]).astype(LOW)
    low_all = jnp.concatenate(
        [layer_norm(earlier, norms[6], norms[7]).astype(LOW), low_one], 0
    )
    queries = (dot_float(low_one, qkv_w[0]).astype(LOW) * score_scale).astype(LOW)
    all_keys, all_values = low_dot(low_all, qkv_w[1]), low_dot(low_all, qkv_w[2])
    info = jnp.stack([s_index, caption_len[0] - s_index * row_count]).astype(jnp.int32)
    no_ok = jnp.zeros((8, 128), jnp.float32)
    self_low, self_lse, x2_all = attend_gather(info, no_ok, queries, all_keys, all_values, x2, 3)
    x2_all = x2_all.reshape(features, cells)
    n3, r3, y3, x3 = conv_block(2, x2_all, convs[1], own_gb, masks, y2, number)
    out_blocks = x3.reshape(rows_own, cells)[:, :number].reshape(rows_own, examples, grid)
    out_blocks = jnp.broadcast_to(
        out_blocks.transpose(1, 0, 2)[:, None], (examples, halves, rows_own, grid)
    )
    in_blocks = exchange_all(out_blocks.reshape(32, rows_own, grid), 4)
    patch_all = devices_to_slots(in_blocks.reshape(32, PORTIONS, GROUP, grid))
    patch_all = patch_all.reshape(features, grid).T

    prefix_own = prefix[0]
    prefix_half = prefix_own.shape[0]
    first_half = s_index == 0
    prefix_all = jnp.concatenate(
        [
            jnp.where(first_half, prefix_own, prefix_other),
            jnp.where(first_half, prefix_other, prefix_own),
        ],
        0,
    )
    memory = jnp.concatenate([prefix_all, patch_all], 0)
    mem_rows = memory.shape[0]
    prefix_total = prefix_all.shape[0]
    mem_padded = jnp.pad(memory, ((0, -mem_rows % 128), (0, 0)))
    mem_keys = low_dot(mem_padded, ck_w)
    mem_values = low_dot(mem_padded, cv_w)
    slot_ids = jnp.arange(mem_padded.shape[0], dtype=jnp.int32)
    mem_ok = (slot_ids < mem_rows) & ((slot_ids >= prefix_total) | (slot_ids < prefix_count[0]))
    mem_ok = jnp.broadcast_to(mem_ok.astype(jnp.float32)[:, None], (mem_padded.shape[0], 128))

    after_self = inputs + dot_float(self_low, sout_w)
    low_two = layer_norm(after_self, norms[8], norms[9]).astype(LOW)
    cross_q = (dot_float(low_two, cq_w).astype(LOW) * score_scale).astype(LOW)
    cross_low, cross_lse = attend("cross", info, mem_ok, cross_q, mem_keys, mem_values)
    after_cross = after_self + dot_float(cross_low, cout_w)
    low_three = layer_norm(after_cross, norms[10], norms[11]).astype(LOW)
    up_proj = jnp.concatenate([dot_float(low_three, w) for w in up_ws], 1)
    hidden = jax.nn.gelu(up_proj).astype(LOW)
    result = after_cross + dot_float(hidden, down_w)

    out_grad = cotangent[0].astype(jnp.float32)
    grad_low = cotangent[0]
    d_upper = (dot_t(grad_low, down_w) * gelu_slope(up_proj)).astype(LOW)
    jobs = [(0, 1, row_count, 0, features * q, 0) for q in range(4)]
    jobs += [(2, 3, row_count, 0, 0, features * j) for j in range(4)]
    mlp_parts = weight_grads(
        jobs, range(8), "mlp", [hidden, grad_low, low_three, d_upper], features, row_count
    )
    mlp_parts, d_upper = lax.optimization_barrier((mlp_parts, d_upper))
    d_normed = sum(dot_t(d, w) for d, w in zip(chunks(d_upper), up_ws))
    unused_three, norm_back_three = jax.vjp(layer_norm, after_cross, norms[10], norms[11])
    d_three, grad_gain_three, grad_bias_three = norm_back_three(d_normed)

    def scattered(parts):
        parts = parts.reshape(examples, -1, features)
        return lax.psum_scatter(parts, "dp", scatter_dimension=0, tiled=True)[0]

    mlp_own = scattered(mlp_parts)
    d_after_cross = out_grad + d_three
    cross_grad_low = d_after_cross.astype(LOW)
    d_cross = dot_t(cross_grad_low, cout_w).astype(LOW)
    d_cross_low, d_mem_keys, d_mem_values = attend_grads(
        "cross", info, mem_ok, cross_q, mem_keys, mem_values, d_cross, cross_lse, score_scale
    )
    unused_two, norm_back_two = jax.vjp(layer_norm, after_self, norms[8], norms[9])
    d_two, grad_gain_two, grad_bias_two = norm_back_two(dot_t(d_cross_low, cq_w))
    d_after_self = d_after_cross + d_two
    d_mem_rows = dot_t(d_mem_keys[:mem_rows], ck_w) + dot_t(d_mem_values[:mem_rows], cv_w)
    d_prefix = d_mem_rows[:prefix_total].reshape(halves, prefix_half, features)
    prefix_back = lax.dynamic_index_in_dim(d_prefix, s_index, 0, keepdims=False)
    away = lax.dynamic_index_in_dim(d_prefix, 1 - s_index, 0, keepdims=False).astype(LOW)
    d_third = d_mem_rows[prefix_total:].astype(LOW)

    self_grad_low = d_after_self.astype(LOW)
    d_self = dot_t(self_grad_low, sout_w).astype(LOW)
    d_query, d_all_keys, d_all_values = attend_grads(
        "self", info, no_ok, queries, all_keys, all_values, d_self, self_lse, score_scale
    )
    d_normed_all = dot_t(d_all_keys, qkv_w[1]) + dot_t(d_all_values, qkv_w[2])
    from_later = lax.ppermute(d_normed_all[:row_count].astype(LOW), "seq", [(1, 0)])
    arrays = [cross_low, cross_grad_low, low_two, d_cross_low, mem_padded, d_mem_keys, d_mem_values]
    arrays += [self_low, self_grad_low, low_all, d_query, d_all_keys, d_all_values, low_one]
    mem_count = mem_padded.shape[0]
    jobs = [
        (0, 1, row_count, 0, 0, 0),
        (2, 3, row_count, 0, 0, 0),
        (4, 5, mem_count, 0, 0, 0),
        (4, 6, mem_count, 0, 0, 0),
        (7, 8, row_count, 0, 0, 0),
        (13, 10, row_count, 0, 0, 0),
        (9, 11, row_count, 0, 0, 0),
        (9, 11, row_count, row_count, 0, 0),
        (9, 12, row_count, 0, 0, 0),
        (9, 12, row_count, row_count, 0, 0),
    ]
    rest_parts = weight_grads(
        jobs, (0, 1, 2, 3, 4, 5, 6, 6, 7, 7), "rest", arrays, features, row_count
    )
    rest_own = scattered(rest_parts)

    d_y3 = to_channels(d_third, 6).astype(jnp.float32)
    d_y3 = laid_out(jnp.sum(d_y3.reshape(examples, halves, rows_own, grid), 1))

    def back_through(layer, d_y, n, r, x_all, w, swaps, cid):
        dx, grad_w, sums = conv_block_back(layer, d_y, n, r, own_gb, masks, x_all, w.T, number)
        total, *got = reduce_all(dx.reshape(PORTIONS, 32, GROUP, cells), swaps, cid)
        grad_w = grad_w.reshape(9, rows_own, features).transpose(1, 0, 2)
        grad_w = grad_w.reshape(rows_own, examples, -1).transpose(1, 0, 2)
        return d_y + total.reshape(rows_own, cells), grad_w, sums, got

    d_y2, grad_conv_one, sums3, _ = back_through(2, d_y3, n3, r3, x2_all, convs[1], [], 7)
    d_y2, mlp_own = lax.optimization_barrier((d_y2, mlp_own))
    d_y1, grad_conv_zero, sums2, got = back_through(
        1, d_y2, n2, r2, x1_all, convs[0], [grad_conv_one, away], 8
    )
    got_one, prefix_part = got
    prefix_back = prefix_back + prefix_part.astype(jnp.float32)
    from_later, d_y1 = lax.optimization_barrier((from_later, d_y1))
    d_normed_one = dot_t(d_query, qkv_w[0]) + d_normed_all[row_count:]
    d_normed_one = d_normed_one + from_later.astype(jnp.float32)
    unused_one, norm_back_one = jax.vjp(layer_norm, inputs, norms[6], norms[7])
    d_one, grad_gain_one, grad_bias_one = norm_back_one(d_normed_one)
    d_inputs = d_after_self + d_one
    grad_patch, sums1 = first_block_back(d_y1, n1, r1, own_gb, pixels, number)
    grad_patch = grad_patch.reshape(rows_own, examples, -1).transpose(1, 0, 2)
    patch_rows = grad_patch.shape[2]
    bn_grads = jnp.concatenate([sums1[:, :2], sums2[:, :2], sums3[:, :2]], 1).astype(LOW)
    ln_grads = jnp.stack(
        [
            grad_gain_one,
            grad_bias_one,
            grad_gain_two,
            grad_bias_two,
            grad_gain_three,
            grad_bias_three,
        ]
    ).astype(LOW)
    ln_count = ln_grads.shape[0]
    ln_blocks = ln_grads.reshape(ln_count, examples, -1).transpose(1, 0, 2)
    ln_blocks = jnp.pad(ln_blocks, ((0, 0), (0, rows_own - ln_count), (0, 0)))
    send_blocks = jnp.concatenate(
        [
            grad_conv_zero,
            grad_patch,
            jnp.broadcast_to(bn_grads, (examples,) + bn_grads.shape),
            ln_blocks,
        ],
        2,
    )
    def by_sender(blocks):
        return blocks.transpose(1, 0, 2, 3).reshape(32, rows_own, -1)

    def channels_last(blocks):
        mixed = devices_to_slots(blocks.reshape(32, PORTIONS, GROUP, -1))
        return mixed.reshape(features, -1)

    mlp_other = lax.ppermute(mlp_own, "seq", [(0, 1), (1, 0)])
    got, rest_other = swap_both(send_blocks, rest_own, 9)
    got = by_sender(got)
    width = w_conv.shape[1] + patch_rows
    mixed = channels_last(got[:, :, : width + 6])
    conv_rows = w_conv.shape[1]
    stem_grads = jnp.concatenate(
        [mixed[:, :conv_rows], channels_last(by_sender(got_one)), mixed[:, conv_rows:width]], 1
    )
    stem_grads = stem_grads.T.astype(jnp.float32)
    bn_part = lax.dynamic_slice_in_dim(mixed[:, width:], a_index * patch_rows, patch_rows, 0)
    ln_part = jnp.sum(got[:, :ln_count, width + 6 :].astype(jnp.float32), 0)
    norm_grads = jnp.concatenate([bn_part.T.astype(jnp.float32), ln_part], 0)

    mlp_sum = mlp_own.astype(jnp.float32) + mlp_other.astype(jnp.float32)
    rest_sum = rest_own.astype(jnp.float32) + rest_other.astype(jnp.float32)
    down_sum = mlp_sum[: 4 * shard_rows]
    up_sum = [mlp_sum[(4 + i) * shard_rows : (5 + i) * shard_rows] for i in range(4)]
    rest = [rest_sum[i * shard_rows : (i + 1) * shard_rows] for i in range(8)]
    return (
        result[None].astype(LOW),
        d_inputs[None].astype(LOW),
        prefix_back[None].astype(LOW),
        stem_grads[2 * conv_rows :],
        stem_grads[: 2 * conv_rows].reshape(w_conv.shape),
        jnp.concatenate(rest[5:], 1),
        rest[4],
        rest[1],
        jnp.concatenate(rest[2:4], 1),
        rest[0],
        jnp.concatenate(up_sum, 1),
        down_sum,
        norm_grads,
    )


def suits(mesh):
    return mesh.shape["dp"] == 16 and mesh.shape["seq"] == 2


def solution(mesh):
    return jax.shard_map(
        fast_device if suits(mesh) else general_device,
        mesh=mesh,
        in_specs=(
            P("dp", "seq", None),
            P("dp", "seq", None),
            P("dp", "seq", None),
            P("dp"),
            P("dp"),
            P("dp", "seq", None),
            P("dp", None),
            P(None, "dp", None),
            P("dp", None),
            P("dp", None),
            P("dp", None),
            P("dp", None),
            P("dp", None),
            P("dp", None),
            P("dp", None),
            P(None, "dp"),
        ),
        out_specs=(
            P("dp", "seq", None),
            P("dp", "seq", None),
            P("dp", "seq", None),
            P("dp", None),
            P(None, "dp", None),
            P("dp", None),
            P("dp", None),
            P("dp", None),
            P("dp", None),
            P("dp", None),
            P("dp", None),
            P("dp", None),
            P(None, "dp"),
        ),
        check_vma=False,
    )
```
